32 devices in a mesh: req: 4 (over y, x), seq: 8 (over z, core).
Axes of the slice: x: 2, y: 2, z: 4, core: 2. Of those that a mesh axis runs over, the one named last changes fastest.
Arguments:
- query_rows: bfloat16 [4096, 2048], P(('req', 'seq')), parts along dimension 0, may hold values from -6 to 6
- key_rows: bfloat16 [4096, 2048], P(('req', 'seq')), parts along dimension 0, may hold values from -6 to 6
- value_rows: bfloat16 [4096, 2048], P(('req', 'seq')), parts along dimension 0, may hold values from -6 to 6
- query_taps: float32 [4, 2048], replicated, may hold values from -3 to 3
- key_taps: float32 [4, 2048], replicated, may hold values from -3 to 3
- value_taps: float32 [4, 2048], replicated, may hold values from -3 to 3
- log_alpha: float32 [16, 4096], P(None, ('req', 'seq')), parts along dimension 1, may hold values from -1 to 0
- write_strength: float32 [16, 4096], P(None, ('req', 'seq')), parts along dimension 1, may hold values from 0 to 1
- tier_mixture: float32 [11, 16, 4096], P(None, None, ('req', 'seq')), parts along dimension 2, may hold values from 0.25 to 4
- output_gate: bfloat16 [4096, 2048], P(('req', 'seq')), parts along dimension 0, may hold values from -6 to 6
- norm_gain: float32 [128], replicated, may hold values from 0.1 to 1.9
Outputs:
- layer_output: bfloat16 [4096, 2048], P(('req', 'seq')), parts along dimension 0
The draws below stay inside these ranges and needn't reach their ends.
There are 4 independent parts, one for each index of `req`. The reference program is written for one: setup_inputs(seed, part) draws one part's arguments, and reference() takes and returns one part's arrays. A program takes and returns all parts, laid end to end along the dimension named above; an argument that names none is the same for every part. Nothing has to cross between parts.
All inputs are finite; a program needn't handle non-finite values.
Results may differ from the reference program's by a relative error of at most 0.001.
Values may be sent and summed in bfloat16 or wider, within the bound.
No kernel may reach another device: no remote copies, remote signals or barrier semaphores. Data moves between devices by JAX's collectives and lax.ppermute only.
A program may use at most 128 MiB of HBM per device.

```python
import math
import jax
import jax.numpy as jnp
import numpy as np
from jax import lax

TOK_DEV = 128
HEADS = 16
HEAD_DIM = 128
SPAN = 64
TAPS = 4
PROMPT_LENGTH = 1024
LEVELS = 11


def slow_mask(key):
    ranking = jax.random.permutation(jax.random.fold_in(key, 7), HEADS)
    limit = max(1, HEADS // 2)
    return ranking < limit


def draw_log_alpha(key, part):
    chosen_variant = slow_mask(key)[:, None]
    streams = jax.random.split(jax.random.fold_in(key, 101), 6)
    token_factor = jnp.exp(jax.random.uniform(streams[0], (HEADS, PROMPT_LENGTH), jnp.float32, -0.6931, 0.6931))
    shard_draw = jnp.exp(jax.random.uniform(streams[1], (HEADS, PROMPT_LENGTH // TOK_DEV, 1), jnp.float32, -0.6931, 0.6931))
    shard_factor = jnp.broadcast_to(shard_draw, (HEADS, PROMPT_LENGTH // TOK_DEV, TOK_DEV)).reshape(HEADS, PROMPT_LENGTH)
    slow_rate = jnp.exp(jax.random.uniform(streams[2], (HEADS, 1), jnp.float32, -2.9957, -1.204)) / PROMPT_LENGTH
    fast_rate = jnp.exp(jax.random.uniform(streams[3], (HEADS, 1), jnp.float32, -3.912, -3.4012))
    forget_multiplier = jnp.where(chosen_variant, slow_rate, fast_rate) * token_factor * shard_factor
    sequence_indexes = jax.random.randint(streams[4], (3,), 0, PROMPT_LENGTH)
    writing_beta = jax.random.uniform(streams[5], (3,), jnp.float32, 0.22, 0.5)
    element_batch = jnp.sum(jnp.where(jnp.arange(PROMPT_LENGTH)[None, :] == sequence_indexes[:, None], writing_beta[:, None], 0.0), axis=0)
    return (-(forget_multiplier + jnp.where(chosen_variant, element_batch[None, :], 0.0))).astype(jnp.float32)


def draw_write_strength(key, part):
    chosen_variant = slow_mask(key)[:, None]
    streams = jax.random.split(jax.random.fold_in(key, 203), 2)
    fast_value = jax.random.uniform(streams[0], (HEADS, PROMPT_LENGTH), jnp.float32, 0.2, 0.9)
    slow_value = jnp.exp(jax.random.uniform(streams[1], (HEADS, PROMPT_LENGTH), jnp.float32, -2.9957, -0.9163)) * HEAD_DIM / PROMPT_LENGTH
    return jnp.where(chosen_variant, slow_value, fast_value).astype(jnp.float32)


def levels(rng, extent, shards, smallest, high):
    level = 1.0
    for dim, parts in shards:
        heights = jax.random.uniform(jax.random.fold_in(jax.random.fold_in(rng, 6), dim), (parts,), jnp.float32, smallest / len(shards), high / len(shards))
        level = level * jnp.repeat(jnp.exp(heights), extent[dim] // parts).reshape((-1,) + (1,) * (len(extent) - 1 - dim))
    return level


def centred(own_key, extent, width, most, cuts=(), held_as=jnp.bfloat16):
    entries = width * jax.random.normal(own_key, extent, jnp.float32)
    if cuts:
        entries = entries * levels(own_key, extent, cuts, -0.22, 0.18)
    return jnp.clip(entries, -most, most).astype(held_as)


def setup_inputs(seed: int = 0, part: int = 0) -> dict:
    arg_keys = jax.random.split(jax.random.key(seed), 12)
    own_keys = jax.random.split(jax.random.fold_in(arg_keys[11], part), 12)
    query_rows = centred(own_keys[0], (PROMPT_LENGTH, HEADS * HEAD_DIM), 1.0, 6.0, ((0, 8),))
    key_rows = centred(own_keys[1], (PROMPT_LENGTH, HEADS * HEAD_DIM), 1.0, 6.0, ((0, 8),))
    value_rows = centred(own_keys[2], (PROMPT_LENGTH, HEADS * HEAD_DIM), 1.0, 6.0, ((0, 8),))
    query_taps = centred(arg_keys[3], (TAPS, HEADS * HEAD_DIM), TAPS ** -0.5, 3.0, (), jnp.float32)
    key_taps = centred(arg_keys[4], (TAPS, HEADS * HEAD_DIM), TAPS ** -0.5, 3.0, (), jnp.float32)
    value_taps = centred(arg_keys[5], (TAPS, HEADS * HEAD_DIM), TAPS ** -0.5, 3.0, (), jnp.float32)
    log_alpha = draw_log_alpha(jax.random.fold_in(jax.random.fold_in(arg_keys[11], part), 71), part)
    write_strength = draw_write_strength(jax.random.fold_in(jax.random.fold_in(arg_keys[11], part), 71), part)
    tier_mixture = jnp.clip(jnp.exp(math.log(4.0) - 2.7725887 * jax.random.uniform(own_keys[8], (LEVELS, HEADS, PROMPT_LENGTH), jnp.float32) ** levels(own_keys[8], (LEVELS, HEADS, PROMPT_LENGTH), ((2, 8),), -0.2, 0.2)), 0.25, 4.0)
    output_gate = centred(own_keys[9], (PROMPT_LENGTH, HEADS * HEAD_DIM), 1.0, 6.0, ((0, 8),))
    norm_gain = jnp.clip(1.0 + 0.18 * jax.random.normal(arg_keys[10], (HEAD_DIM,), jnp.float32), 0.1, 1.9)
    return {"query_rows": query_rows, "key_rows": key_rows, "value_rows": value_rows, "query_taps": query_taps, "key_taps": key_taps, "value_taps": value_taps, "log_alpha": log_alpha, "write_strength": write_strength, "tier_mixture": tier_mixture, "output_gate": output_gate, "norm_gain": norm_gain}


precise = lax.Precision.HIGHEST

def unit_inverse(coupling, length):
    negated = -coupling
    inverse = jnp.eye(length, dtype=jnp.float32) + negated
    powered = negated
    for repeat in range((length - 1).bit_length() - 1):
        powered = jnp.einsum('nhij,nhjk->nhik', powered, powered, precision=precise)
        inverse = inverse + jnp.einsum('nhij,nhjk->nhik', inverse, powered, precision=precise)
    return inverse

def span_terms(query_unit, key_unit, value_block, log_decay, write_rate, level_near):
    length = log_decay.shape[-1]
    cumulative = jnp.cumsum(log_decay, axis=-1)
    lower_mask = jnp.asarray(np.tril(np.ones((length, length), dtype=bool)))
    strict_mask = jnp.asarray(np.tril(np.ones((length, length)), -1), dtype=jnp.float32)
    log_ratio = cumulative[..., :, None] - cumulative[..., None, :]
    decay_mat = jnp.where(lower_mask, jnp.exp(jnp.where(lower_mask, log_ratio, 0.0)), 0.0)
    key_heads = jnp.swapaxes(key_unit, 1, 2)
    query_heads = jnp.swapaxes(query_unit, 1, 2)
    value_heads = jnp.swapaxes(value_block, 1, 2)
    key_gram = jnp.einsum('nhtd,nhid->nhti', key_heads, key_heads, precision=precise)
    coupling = key_gram * decay_mat * strict_mask * write_rate[..., :, None]
    inverse = unit_inverse(coupling, length)
    gamma_run = jnp.exp(cumulative)
    scores = jnp.einsum('nhtd,nhid->nhti', query_heads, key_heads, precision=precise) * decay_mat
    mixing = jnp.einsum('nhti,nhij->nhtj', scores, inverse, precision=precise)
    level_count = length.bit_length()
    level_table = np.array([[(row ^ column).bit_length() for column in range(length)] for row in range(length)])
    one_hot = jnp.asarray(level_table[None] == np.arange(level_count)[:, None, None], dtype=jnp.float32)
    level_mat = jnp.einsum('ltj,nlht->nhtj', one_hot, level_near, precision=precise)
    weights = mixing * level_mat * write_rate[..., None, :]
    within = jnp.einsum('nhtj,nhjd->nhtd', weights, value_heads, precision=precise)
    key_mix = jnp.einsum('nhij,nhjd->nhid', inverse, key_heads * (write_rate * gamma_run)[..., None], precision=precise)
    value_mix = jnp.einsum('nhij,nhjd->nhid', inverse, value_heads * write_rate[..., None], precision=precise)
    effective = gamma_run[..., None] * query_heads - jnp.einsum('nhti,nhid->nhtd', scores, key_mix, precision=precise)
    to_end = jnp.exp(cumulative[..., -1:] - cumulative)
    key_tail = key_heads * to_end[..., None]
    identity = jnp.eye(key_heads.shape[-1], dtype=jnp.float32)
    transit = gamma_run[..., -1, None, None] * identity - jnp.einsum('nhid,nhie->nhde', key_tail, key_mix, precision=precise)
    states = jnp.einsum('nhid,nhie->nhde', key_tail, value_mix, precision=precise)
    return (within, effective, transit, states)

def short_conv(signal_rows, taps):
    taps_count = taps.shape[0]
    signal = signal_rows.astype(jnp.float32)
    padded = jnp.concatenate([jnp.zeros((taps_count - 1, signal.shape[1]), jnp.float32), signal], axis=0)
    summed = taps[0] * padded[0:signal.shape[0]]
    for offset in range(1, taps_count):
        summed = summed + taps[offset] * padded[offset:offset + signal.shape[0]]
    return jax.nn.silu(summed)

def unit_norm(vectors):
    return vectors / jnp.sqrt(lax.optimization_barrier(jnp.sum(vectors * vectors, axis=-1, keepdims=True)) + 1e-06)

def finish(attended, gate_rows, gain):
    scale = lax.rsqrt(lax.optimization_barrier(jnp.mean(attended * attended, axis=-1, keepdims=True)) + 1e-05)
    gated = jax.nn.silu(gate_rows.astype(jnp.float32).reshape(attended.shape))
    return (attended * scale * gain * gated).reshape(attended.shape[0], -1).astype(jnp.bfloat16)

def reference(query_rows, key_rows, value_rows, query_taps, key_taps, value_taps, log_alpha, write_strength, tier_mixture, output_gate, norm_gain):
    query_unit = unit_norm(short_conv(query_rows, query_taps).reshape(PROMPT_LENGTH, HEADS, HEAD_DIM))
    key_unit = unit_norm(short_conv(key_rows, key_taps).reshape(PROMPT_LENGTH, HEADS, HEAD_DIM))
    value_block = short_conv(value_rows, value_taps).reshape(PROMPT_LENGTH, HEADS, HEAD_DIM)
    window_count = PROMPT_LENGTH // SPAN
    near_count = SPAN.bit_length()
    far_count = LEVELS - near_count
    query_blocks = query_unit.reshape(window_count, SPAN, HEADS, HEAD_DIM)
    key_blocks = key_unit.reshape(window_count, SPAN, HEADS, HEAD_DIM)
    value_blocks = value_block.reshape(window_count, SPAN, HEADS, HEAD_DIM)
    decay_blocks = log_alpha.reshape(HEADS, window_count, SPAN).transpose(1, 0, 2)
    write_blocks = write_strength.reshape(HEADS, window_count, SPAN).transpose(1, 0, 2)
    level_blocks = tier_mixture.reshape(LEVELS, HEADS, window_count, SPAN).transpose(2, 0, 1, 3)
    carry_marks = jnp.asarray(np.array([(index ^ index + 1).bit_length() for index in range(window_count)]), dtype=jnp.int32)
    far_levels = jnp.arange(1, far_count + 1, dtype=jnp.int32)

    def advance(buckets, inputs):
        query_window, key_span, value_span, decay_span, write_span, level_span, marker = inputs
        within, effective, transit, states = span_terms(query_window[None], key_span[None], value_span[None], decay_span[None], write_span[None], level_span[None, :near_count])
        readout = jnp.einsum('htd,lhde->lhte', effective[0], buckets, precision=precise)
        output = within[0] + lax.optimization_barrier(jnp.sum(level_span[near_count:][..., None] * readout, axis=0))
        chosen_variant = jnp.where((far_levels > marker)[:, None, None, None], buckets, 0.0)
        merged = lax.optimization_barrier(jnp.sum(jnp.where((far_levels < marker)[:, None, None, None], buckets, 0.0), axis=0))
        at_mark = (far_levels == marker)[:, None, None, None]
        chosen_variant = jnp.where(at_mark, merged[None], chosen_variant)
        advanced = jnp.einsum('hde,lhef->lhdf', transit[0], chosen_variant, precision=precise) + jnp.where(at_mark, states, 0.0)
        return (advanced, output)
    initial = jnp.zeros((far_count, HEADS, HEAD_DIM, HEAD_DIM), jnp.float32)
    final_state, span_outputs = lax.scan(advance, initial, (query_blocks, key_blocks, value_blocks, decay_blocks, write_blocks, level_blocks, carry_marks))
    attended = span_outputs.transpose(0, 2, 1, 3).reshape(PROMPT_LENGTH, HEADS, HEAD_DIM)
    return finish(attended, output_gate, norm_gain)
```

```python
import functools

import jax
import jax.numpy as jnp
from jax import lax
from jax.experimental import pallas as pl
from jax.experimental.pallas import tpu as pltpu
from jax.sharding import PartitionSpec as P

HEAD_DIM = 128
CHUNK = 128
CODE = 125.0
F32 = jnp.float32
BF16 = jnp.bfloat16


def split(x):
    high = x.astype(BF16)
    return high, (x - high.astype(F32)).astype(BF16)


def dot(a, b):
    return jnp.dot(a, b, preferred_element_type=F32)


def wide(b):
    row = jnp.concatenate(b, axis=1)
    return jnp.concatenate([row, row], axis=0)


def mm(a, b):
    width = b[0].shape[1]
    if width > 128:
        both = jnp.concatenate([b[0], b[0]], axis=0)
        return dot(jnp.concatenate(a, axis=1), both) + dot(a[0], b[1])
    out = dot(jnp.concatenate(a, axis=1), wide(b))
    return out[:, :width] + out[:, width:]


def silu(u):
    return u / (1.0 + jnp.exp(-u))


def encode(state):
    top = jnp.max(jnp.abs(state), axis=0, keepdims=True)
    scale = (top * 1.02 + 1e-30).astype(BF16).astype(F32)
    grade = jnp.abs(state) / scale
    level = jnp.exp2(grade * (2.0 * CODE) - CODE)
    return jnp.where(state < 0, -level, level).astype(BF16), scale


def decode(code, scale):
    grade = jnp.log2(jnp.abs(code)) * (0.5 / CODE) + 0.5
    size = grade * scale
    return jnp.where(code < 0, -size, size)


def iotas(rows, columns):
    return (
        lax.broadcasted_iota(jnp.int32, (rows, columns), 0),
        lax.broadcasted_iota(jnp.int32, (rows, columns), 1),
    )


def place():
    index = lax.axis_index("seq")
    return index % 2, index // 2


def fill(scratch, own, other, halo, core, first):
    scratch[0:8, :] = jnp.zeros((8, scratch.shape[1]), F32)
    scratch[5:8, :] = halo[first : first + 3]
    start = pl.multiple_of(8 + CHUNK * core, 8)
    scratch[pl.ds(start, CHUNK), :] = own[...].astype(F32)
    start = pl.multiple_of(8 + CHUNK * (1 - core), 8)
    scratch[pl.ds(start, CHUNK), :] = other[...].astype(F32)


def conv(scratch, taps, chunk, columns):
    total = None
    for tap in range(4):
        part = taps[tap : tap + 1, columns] * scratch[
            5 + tap + CHUNK * chunk : 5 + tap + CHUNK * chunk + CHUNK, columns
        ]
        total = part if total is None else total + part
    return silu(total)


def unit(rows):
    return rows * lax.rsqrt(jnp.sum(rows * rows, axis=-1, keepdims=True) + 1e-6)


def token_row(own, other, row, core, chunk):
    return jnp.where(core == chunk, own[pl.ds(row, 1), :], other[pl.ds(row, 1), :])


def sums(own, other, heads, core, step):
    base = 8 * core + heads * step
    rows = [
        token_row(own, other, base + head, core, chunk)
        for head in range(heads)
        for chunk in range(2)
    ]
    pad = -len(rows) % 8
    if pad:
        rows.append(jnp.zeros((pad, CHUNK), F32))
    t, j = iotas(CHUNK, CHUNK)
    upper = (t <= j).astype(F32)
    return jnp.dot(
        jnp.concatenate(rows, axis=0),
        upper,
        preferred_element_type=F32,
        precision=lax.Precision.HIGHEST,
    )


def invert(coupling, t, j):
    apart = t ^ j
    count = len(coupling)
    near = [split(jnp.where(apart < 8, -a, 0.0)) for a in coupling]
    eye = (t == j).astype(F32)
    squared = [mm(n, n) for n in near]
    grown = []
    fourth = []
    for i in range(count):
        base = eye + near[i][0].astype(F32) + near[i][1].astype(F32)
        left = split(jnp.concatenate([squared[i], base], axis=0))
        both = mm(left, split(squared[i]))
        fourth.append(both[:CHUNK])
        grown.append(base + both[CHUNK:])
    inverse = [
        grown[i] + mm(split(grown[i]), split(fourth[i])) for i in range(count)
    ]
    inverse = [split(x) for x in inverse]
    size = 8
    while size < CHUNK:
        starts = range(size, CHUNK, 2 * size)

        def pick(x):
            return jnp.concatenate([x[s : s + size] for s in starts], axis=0)

        zero = jnp.zeros((size, CHUNK), BF16)

        def spread(x):
            pieces = []
            for k in range(len(starts)):
                pieces += [zero, x[k * size : (k + 1) * size]]
            return jnp.concatenate(pieces, axis=0)

        def merge(x, rows):
            pieces = []
            for k, s in enumerate(starts):
                pieces += [x[s - size : s], rows[k * size : (k + 1) * size]]
            return jnp.concatenate(pieces, axis=0)

        mask = pick((apart >= size) & (apart < 2 * size))
        middle = []
        for i in range(count):
            lower = split(jnp.where(mask, pick(coupling[i]), 0.0))
            middle.append(split(mm(lower, inverse[i])))
        for i in range(count):
            high, low = inverse[i]
            rows = (pick(high), pick(low))
            change = mm(rows, tuple(spread(m) for m in middle[i]))
            fresh = split(rows[0].astype(F32) + rows[1].astype(F32) - change)
            inverse[i] = (merge(high, fresh[0]), merge(low, fresh[1]))
        size *= 2
    return inverse


def decay(column, row, t, j):
    return jnp.exp(jnp.where(t >= j, column - row, -1e30))


def states_kernel(
    heads,
    key_own,
    key_other,
    value_own,
    value_other,
    key_taps,
    value_taps,
    halo_one,
    halo_two,
    small_own,
    small_other,
    key_cols_out,
    inverse_out,
    write_out,
    first_state_out,
    state_out,
    transit_one_out,
    transit_out,
    code_out,
    key_scratch,
    value_scratch,
    scale_scratch,
):
    core, _ = place()
    step = pl.program_id(0)
    halo = halo_one[...].astype(F32) + halo_two[...].astype(F32)
    fill(key_scratch, key_own, key_other, halo, core, 3)
    fill(value_scratch, value_own, value_other, halo, core, 6)
    t, j = iotas(CHUNK, CHUNK)
    run = sums(small_own, small_other, heads, core, step)
    strengths = [
        token_row(small_own, small_other, 16 + 8 * core + heads * step + head, core, chunk)
        for head in range(heads)
        for chunk in range(2)
    ]
    table = jnp.concatenate([run[: 2 * heads]] + strengths, axis=0)
    pad = -table.shape[0] % 8
    if pad:
        table = jnp.concatenate([table, jnp.zeros((pad, CHUNK), F32)], axis=0)
    columns = table.T
    parts = [(head, chunk) for head in range(heads) for chunk in range(2)]
    key_cols = []
    key_units = []
    coupling = []
    for i, (head, chunk) in enumerate(parts):
        lanes = slice(head * 128, head * 128 + 128)
        key = unit(conv(key_scratch, key_taps, chunk, lanes))
        key_t = key.T
        key_cols.append(key_t)
        key_units.append(key)
        pair = split(key_t)
        key_cols_out[head, chunk, 0] = pair[0]
        key_cols_out[head, chunk, 1] = pair[1]
        gram = mm(split(key), pair)
        ratio = decay(columns[:, i : i + 1], run[i : i + 1], t, j)
        beta = columns[:, 2 * heads + i : 2 * heads + i + 1]
        coupling.append(jnp.where(t > j, gram * ratio * beta, 0.0))
    inverse = invert(coupling, t, j)
    transits = []
    states = []
    for i, (head, chunk) in enumerate(parts):
        lanes = slice(head * 128, head * 128 + 128)
        inverse_out[head, chunk, 0] = inverse[i][0]
        inverse_out[head, chunk, 1] = inverse[i][1]
        value = conv(value_scratch, value_taps, chunk, lanes)
        beta = columns[:, 2 * heads + i : 2 * heads + i + 1]
        grow = jnp.exp(columns[:, i : i + 1])
        write = jnp.concatenate([key_units[i] * (beta * grow), value * beta], axis=1)
        write = split(write)
        write_out[head, chunk, 0] = write[0]
        write_out[head, chunk, 1] = write[1]
        last = run[i : i + 1, CHUNK - 1 : CHUNK]
        tail = key_cols[i] * jnp.exp(last - run[i : i + 1])
        mixed = mm(split(tail), inverse[i])
        both = mm(split(mixed), write)
        transits.append(jnp.where(t == j, jnp.exp(last), 0.0) - both[:, :128])
        states.append(both[:, 128:])
    for head in range(heads):
        low, high = 2 * head, 2 * head + 1
        first = split(states[low])
        low_transit = split(transits[low])
        pair = split(transits[high])
        state = mm(pair, first) + states[high]
        transit = mm(pair, low_transit)
        first_state_out[head] = states[low]
        transit_one_out[head] = transits[low]
        state_out[head] = state
        transit_out[head] = transit
        code, scale = encode(state)
        index = heads * step + head
        code_out[pl.ds(pl.multiple_of(index * 128, 128), 128), :] = code
        scale_scratch[index] = scale

    @pl.when(step == pl.num_programs(0) - 1)
    def _():
        rows = [scale_scratch[h] for h in range(8)]
        rows.append(jnp.zeros((8, 128), F32))
        code_out[1024:1040, :] = jnp.concatenate(rows, axis=0).astype(BF16)


def queries_kernel(
    heads,
    near,
    query_own,
    query_other,
    query_taps,
    halo_one,
    halo_two,
    small_own,
    small_other,
    key_cols,
    inverse,
    write,
    first_state,
    transit_one,
    out,
    moved,
    query_scratch,
):
    core, _ = place()
    step = pl.program_id(0)
    halo = halo_one[...].astype(F32) + halo_two[...].astype(F32)
    fill(query_scratch, query_own, query_other, halo, core, 0)
    t, j = iotas(CHUNK, CHUNK)
    apart = t ^ j
    run = sums(small_own, small_other, heads, core, step)
    parts = [(head, chunk) for head in range(heads) for chunk in range(2)]
    rows = [run[: 2 * heads]]
    for head, chunk in parts:
        for level in range(near + 1):
            row = 32 + 16 * level + 8 * core + heads * step + head
            rows.append(token_row(small_own, small_other, row, core, chunk))
    table = jnp.concatenate(rows, axis=0)
    pad = -table.shape[0] % 8
    if pad:
        table = jnp.concatenate([table, jnp.zeros((pad, CHUNK), F32)], axis=0)
    columns = table.T
    for i, (head, chunk) in enumerate(parts):
        lanes = slice(head * 128, head * 128 + 128)
        query = unit(conv(query_scratch, query_taps, chunk, lanes))
        ratio = decay(columns[:, i : i + 1], run[i : i + 1], t, j)
        scores = mm(split(query), (key_cols[head, chunk, 0], key_cols[head, chunk, 1])) * ratio
        mixing = mm(split(scores), (inverse[head, chunk, 0], inverse[head, chunk, 1]))
        at = 2 * heads + i * (near + 1)
        level_mat = columns[:, at : at + 1]
        for level in range(1, near):
            weight = columns[:, at + level : at + level + 1]
            level_mat = jnp.where(apart >= 1 << (level - 1), weight, level_mat)
        high, low = (write[head, chunk, 0], write[head, chunk, 1])
        within = mm(split(mixing * level_mat), (high[:, 128:], low[:, 128:]))
        grow = jnp.exp(columns[:, i : i + 1])
        effective = grow * query - mm(split(mixing), (high[:, :128], low[:, :128]))
        rows = pl.ds(chunk * CHUNK, CHUNK)
        if chunk:
            pair = split(effective)
            weight = columns[:, at + near : at + near + 1]
            within = within + weight * mm(pair, split(first_state[head]))
            effective = mm(pair, split(transit_one[head]))
        out[head, rows, :] = within
        moved[head, rows, :] = effective


def received(refs, head):
    code = None
    scale = None
    for ref in refs:
        part = ref[head * 128 : head * 128 + 128, :].astype(F32)
        row = ref[1024 + head : 1025 + head, :].astype(F32)
        code = part if code is None else code + part
        scale = row if scale is None else scale + row
    return decode(code, scale)


def pack_rows(scales):
    return jnp.concatenate(scales + [jnp.zeros((8, 128), F32)], axis=0).astype(BF16)


def join_kernel(level, arrivals, with_transit, *refs):
    state_in = refs[:arrivals]
    refs = refs[arrivals:]
    transit_in = ()
    if with_transit:
        transit_in = refs[:arrivals]
        refs = refs[arrivals:]
    state, transit, refs = refs[0], refs[1], refs[2:]
    code_out, refs = refs[0], refs[1:]
    _, node = place()
    upper = (node >> level) % 2 == 1

    @pl.when(upper)
    def _():
        scales = []
        for head in range(8):
            pair = split(transit[head])
            fresh = mm(pair, split(received(state_in, head))) + state[head]
            code, scale = encode(fresh)
            code_out[head * 128 : head * 128 + 128, :] = code
            scales.append(scale)
            if with_transit:
                refs[0][head] = fresh
                refs[1][head] = mm(pair, split(received(transit_in, head)))
        code_out[1024:1040, :] = pack_rows(scales)
        if with_transit:
            scales = []
            for head in range(8):
                code, scale = encode(refs[1][head])
                refs[2][head * 128 : head * 128 + 128, :] = code
                scales.append(scale)
            refs[2][1024:1040, :] = pack_rows(scales)

    @pl.when(jnp.logical_not(upper))
    def _():
        scales = []
        for head in range(8):
            code, scale = encode(state[head])
            code_out[head * 128 : head * 128 + 128, :] = code
            scales.append(scale)
            if with_transit:
                refs[0][head] = state[head]
                refs[1][head] = transit[head]
        code_out[1024:1040, :] = pack_rows(scales)
        if with_transit:
            scales = []
            for head in range(8):
                code, scale = encode(transit[head])
                refs[2][head * 128 : head * 128 + 128, :] = code
                scales.append(scale)
            refs[2][1024:1040, :] = pack_rows(scales)


def code_kernel(value, code_out):
    scales = []
    for head in range(8):
        code, scale = encode(value[head])
        code_out[head * 128 : head * 128 + 128, :] = code
        scales.append(scale)
    code_out[1024:1040, :] = pack_rows(scales)


def level_weight(own, other, row, core):
    rows = [token_row(own, other, row, core, chunk) for chunk in range(2)]
    rows.append(jnp.zeros((6, CHUNK), F32))
    columns = jnp.concatenate(rows, axis=0).T
    return jnp.concatenate([columns[:, 0:1], columns[:, 1:2]], axis=0)


def absorb_kernel(level, weight_row, arrivals, *refs):
    state_in = refs[:arrivals]
    transit_in = refs[arrivals : 2 * arrivals]
    small_own, small_other, out_in, moved_in, out, moved = refs[2 * arrivals :]
    core, node = place()
    upper = (node >> level) % 2 == 1
    later = (node >> (level + 1)) > 0

    @pl.when(upper)
    def _():
        for head in range(8):
            pair = split(moved_in[head])
            weight = level_weight(small_own, small_other, weight_row + 8 * core + head, core)
            gain = mm(pair, split(received(state_in, head)))
            out[head] = out_in[head] + weight * gain

    @pl.when(jnp.logical_not(upper))
    def _():
        out[...] = out_in[...]

    @pl.when(upper & later)
    def _():
        for head in range(8):
            moved[head] = mm(split(moved_in[head]), split(received(transit_in, head)))

    @pl.when(jnp.logical_not(upper & later))
    def _():
        moved[...] = moved_in[...]


def finish_kernel(level, weight_row, arrivals, *refs):
    state_in = refs[:arrivals]
    (small_own, small_other, out_in, moved_in, gate_own, gate_other, gain, out, total) = refs[
        arrivals:
    ]
    core, node = place()
    upper = (node >> level) % 2 == 1

    @pl.when(upper)
    def _():
        for head in range(8):
            weight = level_weight(small_own, small_other, weight_row + 8 * core + head, core)
            extra = mm(split(moved_in[head]), split(received(state_in, head)))
            total[head] = out_in[head] + weight * extra

    @pl.when(jnp.logical_not(upper))
    def _():
        total[...] = out_in[...]

    for head in range(8):
        lanes = slice(head * 128, head * 128 + 128)
        attended = total[head]
        scale = lax.rsqrt(jnp.mean(attended * attended, axis=-1, keepdims=True) + 1e-5)
        normed = attended * scale * gain[...]
        total[head] = normed
        for source, chunk in ((gate_own, core), (gate_other, 1 - core)):
            rows = pl.ds(pl.multiple_of(chunk * CHUNK, CHUNK), CHUNK)
            gated = total[head, rows, :] * silu(source[:, lanes].astype(F32))
            out[rows, lanes] = gated.astype(BF16)


def halo_kernel(query, key, value, out):
    rows = [x[13:16, :].astype(F32) for x in (query, key, value)]
    rows.append(jnp.zeros((7, query.shape[1]), F32))
    out[...] = jnp.concatenate(rows, axis=0).astype(BF16)


def swap_kernel(own, other, out):
    core, _ = place()
    width = own.shape[1]
    start = pl.multiple_of(core * width, width)
    out[:, pl.ds(start, width)] = own[pl.ds(pl.multiple_of(core * CHUNK, CHUNK), CHUNK), :]
    start = pl.multiple_of((1 - core) * width, width)
    out[:, pl.ds(start, width)] = other[...]


def struct(shape, dtype=F32):
    return jax.ShapeDtypeStruct(shape, dtype)


PARAMS = pltpu.CompilerParams(vmem_limit_bytes=48 << 20)


def per_device(
    query_rows,
    key_rows,
    value_rows,
    query_taps,
    key_taps,
    value_taps,
    log_alpha,
    write_strength,
    tier_mixture,
    output_gate,
    norm_gain,
):
    rows, width = query_rows.shape
    half = width // 2
    size = lax.axis_size("seq")
    nodes = size // 2
    level_total = tier_mixture.shape[0]
    near = CHUNK.bit_length()
    cores = [(i, i ^ 1) for i in range(size)]
    small = jnp.concatenate(
        [log_alpha, write_strength, tier_mixture.reshape(level_total * 16, rows)], axis=0
    )
    halo = pl.pallas_call(
        halo_kernel,
        grid=(1,),
        in_specs=[pl.BlockSpec((16, width), lambda i: (rows // 16 - 1, 0))] * 3,
        out_specs=pl.BlockSpec((16, width), lambda i: (0, 0)),
        out_shape=struct((16, width), BF16),
        name="halo",
    )(query_rows, key_rows, value_rows)
    halo_one = lax.ppermute(halo, "seq", [(i, i + 1) for i in range(1, size - 1, 2)])
    halo_two = lax.ppermute(halo, "seq", [(i, i + 2) for i in range(1, size - 1, 2)])
    key_other = lax.ppermute(key_rows, "seq", cores)
    value_other = lax.ppermute(value_rows, "seq", cores)
    small_other = lax.ppermute(small, "seq", cores)
    query_other = lax.ppermute(query_rows, "seq", cores)
    gate_other = lax.ppermute(output_gate, "seq", cores)

    heads = 2
    steps = 8 // heads
    lanes = heads * 128

    def feature(row_count):
        return pl.BlockSpec(
            (row_count, lanes), lambda g: (0, (lax.axis_index("seq") % 2) * steps + g)
        )

    def whole(shape):
        return pl.BlockSpec(shape, lambda g: (0,) * len(shape))

    def by_head(*tail):
        return pl.BlockSpec((heads,) + tail, lambda g: (g,) + (0,) * len(tail))

    small_spec = whole(small.shape)
    pair = (2, 2, 128, 128)
    pair_wide = (2, 2, 128, 256)
    square = (128, 128)
    (key_cols, inverse, write, first_state, state, transit_one, transit, code) = pl.pallas_call(
        functools.partial(states_kernel, heads),
        grid=(steps,),
        in_specs=[feature(rows)] * 4
        + [feature(4)] * 2
        + [feature(16)] * 2
        + [small_spec, small_spec],
        out_specs=[
            by_head(*pair),
            by_head(*pair),
            by_head(*pair_wide),
            by_head(*square),
            by_head(*square),
            by_head(*square),
            by_head(*square),
            whole((1040, 128)),
        ],
        out_shape=[
            struct((8,) + pair, BF16),
            struct((8,) + pair, BF16),
            struct((8,) + pair_wide, BF16),
            struct((8,) + square),
            struct((8,) + square),
            struct((8,) + square),
            struct((8,) + square),
            struct((1040, 128), BF16),
        ],
        scratch_shapes=[
            pltpu.VMEM((8 + 2 * CHUNK, lanes), F32),
            pltpu.VMEM((8 + 2 * CHUNK, lanes), F32),
            pltpu.VMEM((8, 1, 128), F32),
        ],
        compiler_params=PARAMS,
        cost_estimate=pl.CostEstimate(
            flops=8_000_000_000, bytes_accessed=12_000_000, transcendentals=0
        ),
        name="states",
    )(
        key_rows,
        key_other,
        value_rows,
        value_other,
        key_taps,
        value_taps,
        halo_one,
        halo_two,
        small,
        small_other,
    )

    shard_bits = nodes.bit_length() - 1

    def fan(value, level, keep):
        span = 1 << level
        results = []
        for offset in range(span):
            route = []
            for low in range(0, nodes, 2 * span):
                source, target = low + span - 1, low + span + offset
                if keep(target):
                    route += [(2 * source + c, 2 * target + c) for c in range(2)]
            results.append(lax.ppermute(value, "seq", route))
        return results

    arrived = fan(code, 0, lambda target: True) if shard_bits else []

    moved_shape = struct((8, 2 * CHUNK, 128))
    out, moved = pl.pallas_call(
        functools.partial(queries_kernel, heads, near),
        grid=(steps,),
        in_specs=[feature(rows)] * 2
        + [feature(4)]
        + [feature(16)] * 2
        + [small_spec, small_spec]
        + [
            by_head(*pair),
            by_head(*pair),
            by_head(*pair_wide),
            by_head(*square),
            by_head(*square),
        ],
        out_specs=[by_head(2 * CHUNK, 128)] * 2,
        out_shape=[moved_shape, moved_shape],
        scratch_shapes=[pltpu.VMEM((8 + 2 * CHUNK, lanes), F32)],
        compiler_params=PARAMS,
        cost_estimate=pl.CostEstimate(
            flops=6_000_000_000, bytes_accessed=10_000_000, transcendentals=0
        ),
        name="queries",
    )(
        query_rows,
        query_other,
        query_taps,
        halo_one,
        halo_two,
        small,
        small_other,
        key_cols,
        inverse,
        write,
        first_state,
        transit_one,
    )

    transit_code = None
    if shard_bits > 1:
        transit_code = pl.pallas_call(
            code_kernel,
            out_shape=struct((1040, 128), BF16),
            compiler_params=PARAMS,
            name="code",
        )(transit)
    for level in range(shard_bits - 1):
        keeps = level < shard_bits - 2
        transit_arrived = fan(
            transit_code, level, lambda target: keeps or target >> (level + 1) > 0
        )
        shapes = [struct((1040, 128), BF16)]
        operands = list(arrived)
        if keeps:
            shapes += [struct((8, 128, 128)), struct((8, 128, 128)), struct((1040, 128), BF16)]
            operands += transit_arrived
        joined = pl.pallas_call(
            functools.partial(join_kernel, level, len(arrived), keeps),
            out_shape=shapes,
            compiler_params=PARAMS,
            cost_estimate=pl.CostEstimate(
                flops=300_000_000, bytes_accessed=2_000_000, transcendentals=0
            ),
            name="join",
        )(*operands, state, transit)
        code = joined[0]
        following = fan(code, level + 1, lambda target: True)
        if keeps:
            state, transit, transit_code = joined[1:]
        out, moved = pl.pallas_call(
            functools.partial(
                absorb_kernel, level, 32 + 16 * (near + 1 + level), len(arrived)
            ),
            out_shape=[moved_shape, moved_shape],
            compiler_params=PARAMS,
            cost_estimate=pl.CostEstimate(
                flops=1_500_000_000, bytes_accessed=6_000_000, transcendentals=0
            ),
            name="absorb",
        )(*arrived, *transit_arrived, small, small_other, out, moved)
        arrived = following

    level = max(shard_bits - 1, 0)
    core_half = pl.BlockSpec((rows, half), lambda i: (0, lax.axis_index("seq") % 2))
    full = lambda x: pl.BlockSpec(x.shape, lambda i: (0,) * x.ndim)
    gain = norm_gain.reshape(1, 128)
    operands = list(arrived) + [small, small_other, out, moved]
    result = pl.pallas_call(
        functools.partial(finish_kernel, level, 32 + 16 * (near + 1 + level), len(arrived)),
        grid=(1,),
        in_specs=[full(x) for x in operands] + [core_half, core_half, full(gain)],
        out_specs=pl.BlockSpec((2 * rows, half), lambda i: (0, 0)),
        out_shape=struct((2 * rows, half), BF16),
        scratch_shapes=[pltpu.VMEM((8, 2 * CHUNK, 128), F32)],
        compiler_params=PARAMS,
        name="finish",
    )(*operands, output_gate, gate_other, gain)
    core = lax.axis_index("seq") % 2
    leaving = lax.dynamic_slice(result, ((1 - core) * rows, 0), (rows, half))
    coming = lax.ppermute(leaving, "seq", cores)
    return pl.pallas_call(
        swap_kernel,
        out_shape=struct((rows, width), BF16),
        compiler_params=PARAMS,
        name="swap",
    )(result, coming)


def solution(mesh):
    placed = (
        P(("req", "seq"), None),
        P(("req", "seq"), None),
        P(("req", "seq"), None),
        P(),
        P(),
        P(),
        P(None, ("req", "seq")),
        P(None, ("req", "seq")),
        P(None, None, ("req", "seq")),
        P(("req", "seq"), None),
        P(),
    )
    return jax.shard_map(
        per_device, mesh=mesh, in_specs=placed, out_specs=P(("req", "seq"), None), check_vma=False
    )
```

```python
import functools

import jax
import jax.numpy as jnp
from jax import lax
from jax.experimental import pallas as pl
from jax.experimental.pallas import tpu as pltpu
from jax.sharding import PartitionSpec as P

HEAD_DIM = 128
CHUNK = 128
CODE = 125.0
F32 = jnp.float32
BF16 = jnp.bfloat16


def split(x):
    high = x.astype(BF16)
    return high, (x - high.astype(F32)).astype(BF16)


def dot(a, b):
    return jnp.dot(a, b, preferred_element_type=F32)


def wide(b):
    row = jnp.concatenate(b, axis=1)
    return jnp.concatenate([row, row], axis=0)


def mm(a, b):
    width = b[0].shape[1]
    if width > 128:
        both = jnp.concatenate([b[0], b[0]], axis=0)
        return dot(jnp.concatenate(a, axis=1), both) + dot(a[0], b[1])
    out = dot(jnp.concatenate(a, axis=1), wide(b))
    return out[:, :width] + out[:, width:]


def silu(u):
    return u / (1.0 + jnp.exp(-u))


def encode(state):
    top = jnp.max(jnp.abs(state), axis=0, keepdims=True)
    scale = (top * 1.02 + 1e-30).astype(BF16).astype(F32)
    grade = jnp.abs(state) / scale
    level = jnp.exp2(grade * (2.0 * CODE) - CODE)
    return jnp.where(state < 0, -level, level).astype(BF16), scale


def decode(code, scale):
    grade = jnp.log2(jnp.abs(code)) * (0.5 / CODE) + 0.5
    size = grade * scale
    return jnp.where(code < 0, -size, size)


def iotas(rows, columns):
    return (
        lax.broadcasted_iota(jnp.int32, (rows, columns), 0),
        lax.broadcasted_iota(jnp.int32, (rows, columns), 1),
    )


def place():
    index = lax.axis_index("seq")
    return index % 2, index // 2


def fill(scratch, own, other, halo, core, group, first):
    lanes = scratch.shape[1]
    start = pl.multiple_of(core * 8 * HEAD_DIM + group * lanes, lanes)
    rows = halo[0][:, pl.ds(start, lanes)].astype(F32) + halo[1][:, pl.ds(start, lanes)].astype(F32)
    scratch[5:8, :] = rows[first : first + 3]
    place_own = pl.multiple_of(8 + CHUNK * core, 8)
    scratch[pl.ds(place_own, CHUNK), :] = own[:, group * lanes : (group + 1) * lanes].astype(F32)
    place_other = pl.multiple_of(8 + CHUNK * (1 - core), 8)
    scratch[pl.ds(place_other, CHUNK), :] = other[:, pl.ds(start, lanes)].astype(F32)


def conv(scratch, taps, chunk, columns, taps_columns):
    total = None
    for tap in range(4):
        part = taps[tap : tap + 1, taps_columns] * scratch[
            5 + tap + CHUNK * chunk : 5 + tap + CHUNK * chunk + CHUNK, columns
        ]
        total = part if total is None else total + part
    return silu(total)


def unit(rows):
    return rows * lax.rsqrt(jnp.sum(rows * rows, axis=-1, keepdims=True) + 1e-6)


def token_row(own, other, row, core, chunk):
    return jnp.where(core == chunk, own[pl.ds(row, 1), :], other[pl.ds(row, 1), :])


def rows_table(rows):
    pad = -len(rows) % 8
    if pad:
        rows = rows + [jnp.zeros((pad, CHUNK), F32)]
    return jnp.concatenate(rows, axis=0)


def sums(own, other, base, parts, core):
    rows = [token_row(own, other, base + head, core, chunk) for head, chunk in parts]
    t, j = iotas(CHUNK, CHUNK)
    upper = (t <= j).astype(F32)
    run = jnp.dot(
        rows_table(rows), upper, preferred_element_type=F32, precision=lax.Precision.HIGHEST
    )
    return [run[i : i + 1] for i in range(len(parts))]


def invert(coupling, t, j):
    apart = t ^ j
    count = len(coupling)
    near = [split(jnp.where(apart < 8, -a, 0.0)) for a in coupling]
    eye = (t == j).astype(F32)
    squared = [mm(n, n) for n in near]
    grown = []
    fourth = []
    for i in range(count):
        base = eye + near[i][0].astype(F32) + near[i][1].astype(F32)
        left = split(jnp.concatenate([squared[i], base], axis=0))
        both = mm(left, split(squared[i]))
        fourth.append(both[:CHUNK])
        grown.append(base + both[CHUNK:])
    inverse = [
        grown[i] + mm(split(grown[i]), split(fourth[i])) for i in range(count)
    ]
    inverse = [split(x) for x in inverse]
    size = 8
    while size < CHUNK:
        starts = range(size, CHUNK, 2 * size)

        def pick(x):
            return jnp.concatenate([x[s : s + size] for s in starts], axis=0)

        zero = jnp.zeros((size, CHUNK), BF16)

        def spread(x):
            pieces = []
            for k in range(len(starts)):
                pieces += [zero, x[k * size : (k + 1) * size]]
            return jnp.concatenate(pieces, axis=0)

        def merge(x, rows):
            pieces = []
            for k, s in enumerate(starts):
                pieces += [x[s - size : s], rows[k * size : (k + 1) * size]]
            return jnp.concatenate(pieces, axis=0)

        mask = pick((apart >= size) & (apart < 2 * size))
        middle = []
        for i in range(count):
            lower = split(jnp.where(mask, pick(coupling[i]), 0.0))
            middle.append(split(mm(lower, inverse[i])))
        for i in range(count):
            high, low = inverse[i]
            rows = (pick(high), pick(low))
            change = mm(rows, tuple(spread(m) for m in middle[i]))
            fresh = split(rows[0].astype(F32) + rows[1].astype(F32) - change)
            inverse[i] = (merge(high, fresh[0]), merge(low, fresh[1]))
        size *= 2
    return inverse


def decay(column, row, t, j):
    return jnp.exp(jnp.where(t >= j, column - row, -1e30))


def prepare_kernel(query, key, value, gate, log_alpha, strength, mixture, query_taps, key_taps,
                   value_taps, query_half, key_half, value_half, gate_half, query_taps_half,
                   key_taps_half, value_taps_half, halo, small, tails, sems):
    core, _ = place()
    rows, half = query_half.shape
    lanes = pl.ds(pl.multiple_of(core * half, half), half)
    copies = []

    def copy(source, target):
        made = pltpu.make_async_copy(source, target, sems.at[len(copies)])
        made.start()
        copies.append(made)

    for i, x in enumerate((query, key, value)):
        copy(x.at[rows - 16 : rows, :], tails.at[i])
    copy(log_alpha, small.at[0:16])
    copy(strength, small.at[16:32])
    copy(mixture, small.at[32 : small.shape[0]])
    for x, y in (
        (key, key_half),
        (value, value_half),
        (key_taps, key_taps_half),
        (value_taps, value_taps_half),
        (query_taps, query_taps_half),
        (query, query_half),
        (gate, gate_half),
    ):
        copy(x.at[:, lanes], y)
    for made in copies:
        made.wait()
    message = [tails[i][13:16, :].astype(F32) for i in range(3)]
    message.append(jnp.zeros((7, 2 * half), F32))
    halo[...] = jnp.concatenate(message, axis=0).astype(BF16)


def states_kernel(
    group,
    heads,
    key_own,
    key_other,
    value_own,
    value_other,
    key_taps,
    value_taps,
    halo_one,
    halo_two,
    small_own,
    small_other,
    key_cols_out,
    inverse_out,
    write_out,
    first_state_out,
    state_out,
    transit_one_out,
    transit_out,
    code_out,
    key_scratch,
    value_scratch,
):
    core, _ = place()
    fill(key_scratch, key_own, key_other, (halo_one, halo_two), core, group, 3)
    fill(value_scratch, value_own, value_other, (halo_one, halo_two), core, group, 6)
    t, j = iotas(CHUNK, CHUNK)
    parts = [(head, chunk) for head in range(heads) for chunk in range(2)]
    count = len(parts)
    base = 8 * core + heads * group
    run = sums(small_own, small_other, base, parts, core)
    strengths = [
        token_row(small_own, small_other, 16 + base + head, core, chunk) for head, chunk in parts
    ]
    columns = rows_table(run + strengths).T

    def lanes(head):
        return slice(head * 128, head * 128 + 128)

    def taps_lanes(head):
        return lanes(group * heads + head)

    def beta(i):
        return columns[:, count + i : count + i + 1]

    keys = [
        unit(conv(key_scratch, key_taps, chunk, lanes(head), taps_lanes(head)))
        for head, chunk in parts
    ]
    keys_t = [key.T for key in keys]
    coupling = []
    for i, (head, chunk) in enumerate(parts):
        pair = split(keys_t[i])
        key_cols_out[head, chunk, 0] = pair[0]
        key_cols_out[head, chunk, 1] = pair[1]
        gram = mm(split(keys[i]), pair)
        ratio = decay(columns[:, i : i + 1], run[i], t, j)
        coupling.append(jnp.where(t > j, gram * ratio * beta(i), 0.0))
    inverse = invert(coupling, t, j)
    mixed = []
    for i, (head, chunk) in enumerate(parts):
        inverse_out[head, chunk, 0] = inverse[i][0]
        inverse_out[head, chunk, 1] = inverse[i][1]
        last = run[i][:, CHUNK - 1 : CHUNK]
        tail = keys_t[i] * jnp.exp(last - run[i])
        mixed.append(mm(split(tail), inverse[i]))
    transits = []
    states = []
    for i, (head, chunk) in enumerate(parts):
        value = conv(value_scratch, value_taps, chunk, lanes(head), taps_lanes(head))
        grow = jnp.exp(columns[:, i : i + 1])
        write = jnp.concatenate([keys[i] * (beta(i) * grow), value * beta(i)], axis=1)
        write = split(write)
        write_out[head, chunk, 0] = write[0]
        write_out[head, chunk, 1] = write[1]
        last = run[i][:, CHUNK - 1 : CHUNK]
        both = mm(split(mixed[i]), write)
        transits.append(jnp.where(t == j, jnp.exp(last), 0.0) - both[:, :128])
        states.append(both[:, 128:])
    scales = []
    for head in range(heads):
        low, high = 2 * head, 2 * head + 1
        pair = split(transits[high])
        state = mm(pair, split(states[low])) + states[high]
        first_state_out[head] = states[low]
        transit_one_out[head] = transits[low]
        state_out[head] = state
        transit_out[head] = mm(pair, split(transits[low]))
        code, scale = encode(state)
        code_out[head * 128 : head * 128 + 128, :] = code
        scales.append(scale)
    code_out[heads * 128 : heads * 128 + 16, :] = pack_rows(scales)


def queries_kernel(
    group,
    heads,
    first,
    count,
    near,
    query_own,
    query_other,
    query_taps,
    halo_one,
    halo_two,
    small_own,
    small_other,
    key_cols,
    inverse,
    write,
    first_state,
    transit_one,
    out,
    moved,
    query_scratch,
):
    core, _ = place()
    piece = (group * heads + first) // count
    fill(query_scratch, query_own, query_other, (halo_one, halo_two), core, piece, 0)
    t, j = iotas(CHUNK, CHUNK)
    apart = t ^ j
    parts = [(head, chunk) for head in range(count) for chunk in range(2)]
    base = 8 * core + heads * group + first
    run = sums(small_own, small_other, base, parts, core)
    rows = list(run)
    for head, chunk in parts:
        for level in range(near + 1):
            row = 32 + 16 * level + base + head
            rows.append(token_row(small_own, small_other, row, core, chunk))
    columns = rows_table(rows).T
    mixings = []
    queries = []
    for i, (head, chunk) in enumerate(parts):
        lanes = slice(head * 128, head * 128 + 128)
        full = group * heads + first + head
        taps_lanes = slice(full * 128, full * 128 + 128)
        query = unit(conv(query_scratch, query_taps, chunk, lanes, taps_lanes))
        queries.append(query)
        at = first + head
        ratio = decay(columns[:, i : i + 1], run[i], t, j)
        scores = mm(split(query), (key_cols[at, chunk, 0], key_cols[at, chunk, 1])) * ratio
        mixings.append(mm(split(scores), (inverse[at, chunk, 0], inverse[at, chunk, 1])))
    for i, (head, chunk) in enumerate(parts):
        at = len(parts) + i * (near + 1)
        level_mat = columns[:, at : at + 1]
        for level in range(1, near):
            weight = columns[:, at + level : at + level + 1]
            level_mat = jnp.where(apart >= 1 << (level - 1), weight, level_mat)
        high, low = (write[first + head, chunk, 0], write[first + head, chunk, 1])
        within = mm(split(mixings[i] * level_mat), (high[:, 128:], low[:, 128:]))
        grow = jnp.exp(columns[:, i : i + 1])
        effective = grow * queries[i] - mm(split(mixings[i]), (high[:, :128], low[:, :128]))
        rows = slice(chunk * CHUNK, chunk * CHUNK + CHUNK)
        if chunk:
            pair = split(effective)
            weight = columns[:, at + near : at + near + 1]
            within = within + weight * mm(pair, split(first_state[first + head]))
            effective = mm(pair, split(transit_one[first + head]))
        out[head, rows, :] = within
        moved[head, rows, :] = effective


def received(refs, head):
    code = None
    scale = None
    for ref in refs:
        tail = ref.shape[0] - 16 + head
        part = ref[head * 128 : head * 128 + 128, :].astype(F32)
        row = ref[tail : tail + 1, :].astype(F32)
        code = part if code is None else code + part
        scale = row if scale is None else scale + row
    return decode(code, scale)


def pack_rows(scales):
    zeros = jnp.zeros((16 - len(scales), 128), F32)
    return jnp.concatenate(scales + [zeros], axis=0).astype(BF16)


def encode_all(values, code_out):
    scales = []
    for head, value in enumerate(values):
        code, scale = encode(value)
        code_out[head * 128 : head * 128 + 128, :] = code
        scales.append(scale)
    head = len(values)
    code_out[head * 128 : head * 128 + 16, :] = pack_rows(scales)


def join_kernel(level, arrivals, with_transit, *refs):
    state_in = refs[:arrivals]
    refs = refs[arrivals:]
    transit_in = ()
    if with_transit:
        transit_in = refs[:arrivals]
        refs = refs[arrivals:]
    state, transit, code_out = refs[:3]
    refs = refs[3:]
    heads = state.shape[0]
    _, node = place()
    upper = (node >> level) % 2 == 1

    @pl.when(upper)
    def _():
        fresh = []
        for head in range(heads):
            pair = split(transit[head])
            fresh.append(mm(pair, split(received(state_in, head))) + state[head])
            if with_transit:
                refs[0][head] = fresh[head]
                refs[1][head] = mm(pair, split(received(transit_in, head)))
        encode_all(fresh, code_out)
        if with_transit:
            encode_all([refs[1][head] for head in range(heads)], refs[2])

    @pl.when(jnp.logical_not(upper))
    def _():
        encode_all([state[head] for head in range(heads)], code_out)
        if with_transit:
            for head in range(heads):
                refs[0][head] = state[head]
                refs[1][head] = transit[head]
            encode_all([transit[head] for head in range(heads)], refs[2])


def code_kernel(value, code_out):
    encode_all([value[head] for head in range(value.shape[0])], code_out)


def level_weight(own, other, row, core):
    rows = [token_row(own, other, row, core, chunk) for chunk in range(2)]
    columns = rows_table(rows).T
    return jnp.concatenate([columns[:, 0:1], columns[:, 1:2]], axis=0)


def absorb_kernel(level, weight_row, group, heads, arrivals, pieces, *refs):
    state_in = refs[:arrivals]
    transit_in = refs[arrivals : 2 * arrivals]
    refs = refs[2 * arrivals :]
    small_own, small_other = refs[:2]
    outs_in = refs[2 : 2 + pieces]
    moved_in = refs[2 + pieces : 2 + 2 * pieces]
    out, moved = refs[2 + 2 * pieces :]
    core, node = place()
    upper = (node >> level) % 2 == 1
    later = (node >> (level + 1)) > 0
    each = heads // pieces

    @pl.when(upper)
    def _():
        for head in range(heads):
            pair = split(moved_in[head // each][head % each])
            row = weight_row + 8 * core + heads * group + head
            weight = level_weight(small_own, small_other, row, core)
            gain = mm(pair, split(received(state_in, head)))
            out[head] = outs_in[head // each][head % each] + weight * gain

    @pl.when(jnp.logical_not(upper))
    def _():
        for head in range(heads):
            out[head] = outs_in[head // each][head % each]

    @pl.when(upper & later)
    def _():
        for head in range(heads):
            pair = split(moved_in[head // each][head % each])
            moved[head] = mm(pair, split(received(transit_in, head)))

    @pl.when(jnp.logical_not(upper & later))
    def _():
        for head in range(heads):
            moved[head] = moved_in[head // each][head % each]


def finish_kernel(level, weight_row, group, heads, arrivals, pieces, *refs):
    state_in = refs[:arrivals]
    refs = refs[arrivals:]
    small_own, small_other, gate_own, gate_other, gain = refs[:5]
    outs_in = refs[5 : 5 + pieces]
    moved_in = refs[5 + pieces : 5 + 2 * pieces]
    stay, leave, total = refs[5 + 2 * pieces :]
    core, node = place()
    upper = (node >> level) % 2 == 1
    each = heads // pieces

    @pl.when(upper)
    def _():
        for head in range(heads):
            row = weight_row + 8 * core + heads * group + head
            weight = level_weight(small_own, small_other, row, core)
            extra = mm(split(moved_in[head // each][head % each]), split(received(state_in, head)))
            total[head] = outs_in[head // each][head % each] + weight * extra

    @pl.when(jnp.logical_not(upper))
    def _():
        for head in range(heads):
            total[head] = outs_in[head // each][head % each]

    lanes_all = heads * 128
    start = pl.multiple_of(core * 8 * HEAD_DIM + group * lanes_all, lanes_all)
    gates = (
        gate_own[:, group * lanes_all : (group + 1) * lanes_all],
        gate_other[:, pl.ds(start, lanes_all)],
    )
    for head in range(heads):
        lanes = slice(head * 128, head * 128 + 128)
        for gate, chunk, target in ((gates[0], core, stay), (gates[1], 1 - core, leave)):
            rows = pl.ds(pl.multiple_of(chunk * CHUNK, CHUNK), CHUNK)
            attended = total[head, rows, :]
            scale = lax.rsqrt(jnp.mean(attended * attended, axis=-1, keepdims=True) + 1e-5)
            gated = attended * scale * gain[...] * silu(gate[:, lanes].astype(F32))
            target[:, lanes] = gated.astype(BF16)


def swap_kernel(*refs):
    out = refs[-1]
    count = (len(refs) - 1) // 2
    core, _ = place()
    half = out.shape[1] // 2
    width = half // count
    for i in range(count):
        start = pl.multiple_of(core * half + i * width, width)
        out[:, pl.ds(start, width)] = refs[i][...]
        start = pl.multiple_of((1 - core) * half + i * width, width)
        out[:, pl.ds(start, width)] = refs[count + i][...]


def struct(shape, dtype=F32):
    return jax.ShapeDtypeStruct(shape, dtype)


def params(mib):
    return pltpu.CompilerParams(vmem_limit_bytes=mib << 20)


def cost(flops):
    return pl.CostEstimate(flops=flops, bytes_accessed=1_000_000, transcendentals=0)


GROUPS = 2
PIECES = 2


def per_device(
    query_rows,
    key_rows,
    value_rows,
    query_taps,
    key_taps,
    value_taps,
    log_alpha,
    write_strength,
    tier_mixture,
    output_gate,
    norm_gain,
):
    rows, width = query_rows.shape
    half = width // 2
    size = lax.axis_size("seq")
    nodes = size // 2
    level_total = tier_mixture.shape[0]
    near = CHUNK.bit_length()
    heads = 8 // GROUPS
    lanes = heads * 128
    shard_bits = nodes.bit_length() - 1
    cores = [(i, i ^ 1) for i in range(size)]
    small_rows = 16 * (2 + level_total)
    key_other = lax.ppermute(key_rows, "seq", cores)
    value_other = lax.ppermute(value_rows, "seq", cores)
    half_shape = struct((rows, half), BF16)
    taps_shape = struct((4, half))
    (
        query_half,
        key_half,
        value_half,
        gate_half,
        query_taps_half,
        key_taps_half,
        value_taps_half,
        halo,
        small,
    ) = pl.pallas_call(
        prepare_kernel,
        in_specs=[pl.BlockSpec(memory_space=pltpu.HBM)] * 10,
        out_shape=[half_shape] * 4
        + [taps_shape] * 3
        + [struct((16, width), BF16), struct((small_rows, 128))],
        scratch_shapes=[pltpu.VMEM((3, 16, width), BF16), pltpu.SemaphoreType.DMA((13,))],
        compiler_params=params(8),
        name="prepare",
    )(
        *[
            pltpu.with_memory_space_constraint(x, pltpu.HBM)
            for x in (
                query_rows,
                key_rows,
                value_rows,
                output_gate,
                log_alpha,
                write_strength,
                tier_mixture.reshape(level_total * 16, rows),
                query_taps,
                key_taps,
                value_taps,
            )
        ]
    )
    halo_one = lax.ppermute(halo, "seq", [(i, i + 1) for i in range(1, size - 1, 2)])
    halo_two = lax.ppermute(halo, "seq", [(i, i + 2) for i in range(1, size - 1, 2)])
    small_other = lax.ppermute(small, "seq", cores)
    query_other = lax.ppermute(query_rows, "seq", cores)
    gate_other = lax.ppermute(output_gate, "seq", cores)

    def fan(value, level, keep):
        span = 1 << level
        results = []
        for offset in reversed(range(span)):
            route = []
            for low in range(0, nodes, 2 * span):
                source, target = low + span - 1, low + span + offset
                if keep(target):
                    route += [(2 * source + c, 2 * target + c) for c in range(2)]
            results.append(lax.ppermute(value, "seq", route))
        return results

    square = (heads, 128, 128)
    pair = struct((heads, 2, 2, 128, 128), BF16)
    code_shape = struct((heads * 128 + 16, 128), BF16)
    local = []
    arrived = []
    for group in range(GROUPS):
        local.append(
            pl.pallas_call(
                functools.partial(states_kernel, group, heads),
                out_shape=[
                    pair,
                    pair,
                    struct((heads, 2, 2, 128, 256), BF16),
                    struct(square),
                    struct(square),
                    struct(square),
                    struct(square),
                    code_shape,
                ],
                scratch_shapes=[pltpu.VMEM((8 + 2 * CHUNK, lanes), F32)] * 2,
                compiler_params=params(24),
                cost_estimate=cost(4_000_000_000),
                name="states",
            )(
                key_half,
                key_other,
                value_half,
                value_other,
                key_taps_half,
                value_taps_half,
                halo_one,
                halo_two,
                small,
                small_other,
            )
        )
        arrived.append(fan(local[group][7], 0, lambda target: True) if shard_bits else [])
    state = [x[4] for x in local]
    transit = [x[6] for x in local]
    transit_code = [None] * GROUPS
    outs = [None] * GROUPS
    moved = [None] * GROUPS

    def ask(group):
        key_cols, inverse, write, first_state, _, transit_one, _, _ = local[group]
        outs[group] = []
        moved[group] = []
        count = heads // PIECES
        shape = struct((count, 2 * CHUNK, 128))
        for piece in range(PIECES):
            first = piece * count
            out, move = pl.pallas_call(
                functools.partial(queries_kernel, group, heads, first, count, near),
                out_shape=[shape, shape],
                scratch_shapes=[pltpu.VMEM((8 + 2 * CHUNK, count * 128), F32)],
                compiler_params=params(16),
                cost_estimate=cost(1_500_000_000),
                name="queries",
            )(
                query_half,
                query_other,
                query_taps_half,
                halo_one,
                halo_two,
                small,
                small_other,
                key_cols,
                inverse,
                write,
                first_state,
                transit_one,
            )
            outs[group].append(out)
            moved[group].append(move)

    def encoded(value):
        return pl.pallas_call(
            code_kernel,
            out_shape=code_shape,
            compiler_params=params(8),
            name="code",
        )(value)

    moved_shape = struct((heads, 2 * CHUNK, 128))
    if shard_bits > 1:
        transit_code = [encoded(x) for x in transit]
    if shard_bits < 2:
        for group in range(GROUPS):
            ask(group)
    for level in range(shard_bits - 1):
        keeps = level < shard_bits - 2
        following = []
        for group in range(GROUPS):
            transit_arrived = fan(
                transit_code[group], level, lambda target: keeps or target >> (level + 1) > 0
            )
            shapes = [code_shape]
            operands = list(arrived[group])
            if keeps:
                shapes += [struct(square), struct(square), code_shape]
                operands += transit_arrived
            joined = pl.pallas_call(
                functools.partial(join_kernel, level, len(arrived[group]), keeps),
                out_shape=shapes,
                compiler_params=params(12),
                cost_estimate=cost(300_000_000),
                name="join",
            )(*operands, state[group], transit[group])
            following.append(fan(joined[0], level + 1, lambda target: True))
            if keeps:
                state[group], transit[group], transit_code[group] = joined[1:]
            if level == 0:
                ask(group)
            arrivals = len(arrived[group])
            out, move = pl.pallas_call(
                functools.partial(
                    absorb_kernel,
                    level,
                    32 + 16 * (near + 1 + level),
                    group,
                    heads,
                    arrivals,
                    len(outs[group]),
                ),
                out_shape=[moved_shape, moved_shape],
                compiler_params=params(12),
                cost_estimate=cost(800_000_000),
                name="absorb",
            )(
                *arrived[group],
                *transit_arrived,
                small,
                small_other,
                *outs[group],
                *moved[group],
            )
            outs[group], moved[group] = [out], [move]
        arrived = following

    level = max(shard_bits - 1, 0)
    gain = norm_gain.reshape(1, 128)
    stays = []
    comes = []
    for group in range(GROUPS):
        stay, leave = pl.pallas_call(
            functools.partial(
                finish_kernel,
                level,
                32 + 16 * (near + 1 + level),
                group,
                heads,
                len(arrived[group]),
                len(outs[group]),
            ),
            out_shape=[struct((rows, lanes), BF16)] * 2,
            scratch_shapes=[pltpu.VMEM((heads, 2 * CHUNK, 128), F32)],
            compiler_params=params(12),
            cost_estimate=cost(600_000_000),
            name="finish",
        )(
            *arrived[group],
            small,
            small_other,
            gate_half,
            gate_other,
            gain,
            *outs[group],
            *moved[group],
        )
        stays.append(stay)
        comes.append(lax.ppermute(leave, "seq", cores))
    return pl.pallas_call(
        swap_kernel,
        out_shape=struct((rows, width), BF16),
        compiler_params=params(4),
        name="swap",
    )(*stays, *comes)


def solution(mesh):
    placed = (
        P(("req", "seq"), None),
        P(("req", "seq"), None),
        P(("req", "seq"), None),
        P(),
        P(),
        P(),
        P(None, ("req", "seq")),
        P(None, ("req", "seq")),
        P(None, None, ("req", "seq")),
        P(("req", "seq"), None),
        P(),
    )
    return jax.shard_map(
        per_device, mesh=mesh, in_specs=placed, out_specs=P(("req", "seq"), None), check_vma=False
    )
```

```python
import functools

import jax
import jax.numpy as jnp
from jax import lax
from jax.experimental import pallas as pl
from jax.experimental.pallas import tpu as pltpu
from jax.sharding import PartitionSpec as P

HEAD_DIM = 128
CHUNK = 128
CODE = 125.0
F32 = jnp.float32
BF16 = jnp.bfloat16


def split(x):
    high = x.astype(BF16)
    return high, (x - high.astype(F32)).astype(BF16)


def dot(a, b):
    return jnp.dot(a, b, preferred_element_type=F32)


def wide(b):
    row = jnp.concatenate(b, axis=1)
    return jnp.concatenate([row, row], axis=0)


def mm(a, b):
    width = b[0].shape[1]
    if width > 128:
        both = jnp.concatenate([b[0], b[0]], axis=0)
        return dot(jnp.concatenate(a, axis=1), both) + dot(a[0], b[1])
    out = dot(jnp.concatenate(a, axis=1), wide(b))
    return out[:, :width] + out[:, width:]


def silu(u):
    return u / (1.0 + jnp.exp(-u))


def encode(state):
    top = jnp.max(jnp.abs(state), axis=0, keepdims=True)
    scale = (top * 1.02 + 1e-30).astype(BF16).astype(F32)
    grade = jnp.abs(state) / scale
    level = jnp.exp2(grade * (2.0 * CODE) - CODE)
    return jnp.where(state < 0, -level, level).astype(BF16), scale


def decode(code, scale):
    grade = jnp.log2(jnp.abs(code)) * (0.5 / CODE) + 0.5
    size = grade * scale
    return jnp.where(code < 0, -size, size)


def iotas(rows, columns):
    return (
        lax.broadcasted_iota(jnp.int32, (rows, columns), 0),
        lax.broadcasted_iota(jnp.int32, (rows, columns), 1),
    )


def place():
    index = lax.axis_index("seq")
    return index % 2, index // 2


def fill(scratch, own, other, before, core, chunk, first_lane):
    lanes = scratch.shape[1]
    start = pl.multiple_of(core * 8 * HEAD_DIM + first_lane, 128)
    mine = own[:, first_lane : first_lane + lanes]
    theirs = other[:, pl.ds(start, lanes)]
    if before is None:
        last = jnp.where(core == 1, theirs[CHUNK - 16 :], mine[CHUNK - 16 :]).astype(F32)[13:16]
    else:
        one, two, first = before
        rows = one[:, pl.ds(start, lanes)].astype(F32) + two[:, pl.ds(start, lanes)].astype(F32)
        last = rows[first : first + 3]
    scratch[5:8, :] = last
    scratch[8 : 8 + CHUNK, :] = jnp.where(core == chunk, mine, theirs).astype(F32)


def conv(scratch, taps, columns, taps_columns):
    total = None
    for tap in range(4):
        part = taps[tap : tap + 1, taps_columns] * scratch[5 + tap : 5 + tap + CHUNK, columns]
        total = part if total is None else total + part
    return silu(total)


def unit(rows):
    return rows * lax.rsqrt(jnp.sum(rows * rows, axis=-1, keepdims=True) + 1e-6)


def token_row(own, other, row, core, chunk):
    return jnp.where(core == chunk, own[pl.ds(row, 1), :], other[pl.ds(row, 1), :])


def rows_table(rows):
    pad = -len(rows) % 8
    if pad:
        rows = rows + [jnp.zeros((pad, CHUNK), F32)]
    return jnp.concatenate(rows, axis=0)


def sums(own, other, base, parts, core):
    rows = [token_row(own, other, base + head, core, chunk) for head, chunk in parts]
    t, j = iotas(CHUNK, CHUNK)
    upper = (t <= j).astype(F32)
    run = jnp.dot(
        rows_table(rows), upper, preferred_element_type=F32, precision=lax.Precision.HIGHEST
    )
    return [run[i : i + 1] for i in range(len(parts))]


def invert(coupling, t, j):
    apart = t ^ j
    count = len(coupling)
    near = [split(jnp.where(apart < 8, -a, 0.0)) for a in coupling]
    eye = (t == j).astype(F32)
    squared = [mm(n, n) for n in near]
    grown = []
    fourth = []
    for i in range(count):
        base = eye + near[i][0].astype(F32) + near[i][1].astype(F32)
        left = split(jnp.concatenate([squared[i], base], axis=0))
        both = mm(left, split(squared[i]))
        fourth.append(both[:CHUNK])
        grown.append(base + both[CHUNK:])
    inverse = [
        grown[i] + mm(split(grown[i]), split(fourth[i])) for i in range(count)
    ]
    inverse = [split(x) for x in inverse]
    size = 8
    while size < CHUNK:
        starts = range(size, CHUNK, 2 * size)

        def pick(x):
            return jnp.concatenate([x[s : s + size] for s in starts], axis=0)

        zero = jnp.zeros((size, CHUNK), BF16)

        def spread(x):
            pieces = []
            for k in range(len(starts)):
                pieces += [zero, x[k * size : (k + 1) * size]]
            return jnp.concatenate(pieces, axis=0)

        def merge(x, rows):
            pieces = []
            for k, s in enumerate(starts):
                pieces += [x[s - size : s], rows[k * size : (k + 1) * size]]
            return jnp.concatenate(pieces, axis=0)

        mask = pick((apart >= size) & (apart < 2 * size))
        middle = []
        for i in range(count):
            lower = split(jnp.where(mask, pick(coupling[i]), 0.0))
            middle.append(split(mm(lower, inverse[i])))
        for i in range(count):
            high, low = inverse[i]
            rows = (pick(high), pick(low))
            change = mm(rows, tuple(spread(m) for m in middle[i]))
            fresh = split(rows[0].astype(F32) + rows[1].astype(F32) - change)
            inverse[i] = (merge(high, fresh[0]), merge(low, fresh[1]))
        size *= 2
    return inverse


def decay(column, row, t, j):
    return jnp.exp(jnp.where(t >= j, column - row, -1e30))


def prepare_kernel(query, key, value, gate, log_alpha, strength, mixture, query_taps, key_taps,
                   value_taps, gain, query_half, key_half, value_half, gate_half, query_taps_half,
                   key_taps_half, value_taps_half, halo, small, gain_out, tails, sems):
    core, _ = place()
    rows, half = query_half.shape
    lanes = pl.ds(pl.multiple_of(core * half, half), half)
    copies = []

    def copy(source, target):
        made = pltpu.make_async_copy(source, target, sems.at[len(copies)])
        made.start()
        copies.append(made)

    for i, x in enumerate((query, key, value)):
        copy(x.at[rows - 16 : rows, :], tails.at[i])
    copy(log_alpha, small.at[0:16])
    copy(strength, small.at[16:32])
    copy(mixture, small.at[32 : small.shape[0]])
    for x, y in (
        (key, key_half),
        (value, value_half),
        (key_taps, key_taps_half),
        (value_taps, value_taps_half),
        (query_taps, query_taps_half),
        (query, query_half),
        (gate, gate_half),
    ):
        copy(x.at[:, lanes], y)
    copy(gain, gain_out)
    for made in copies:
        made.wait()
    message = [tails[i][13:16, :].astype(F32) for i in range(3)]
    message.append(jnp.zeros((7, 2 * half), F32))
    halo[...] = jnp.concatenate(message, axis=0).astype(BF16)


def chunk_states(
    chunk,
    first,
    heads,
    key_taps,
    value_taps,
    small_own,
    small_other,
    key_cols_out,
    inverse_out,
    write_out,
    key_scratch,
    value_scratch,
):
    core, _ = place()
    t, j = iotas(CHUNK, CHUNK)
    base = 8 * core + first
    parts = [(head, chunk) for head in range(heads)]
    run = sums(small_own, small_other, base, parts, core)
    strengths = [
        token_row(small_own, small_other, 16 + base + head, core, chunk) for head in range(heads)
    ]
    columns = rows_table(run + strengths).T

    def lanes(head):
        return slice(head * 128, head * 128 + 128)

    def beta(head):
        return columns[:, heads + head : heads + head + 1]

    keys = [
        unit(conv(key_scratch, key_taps, lanes(head), lanes(first + head)))
        for head in range(heads)
    ]
    keys_t = [key.T for key in keys]
    coupling = []
    for head in range(heads):
        pair = split(keys_t[head])
        key_cols_out[head, 0] = pair[0]
        key_cols_out[head, 1] = pair[1]
        gram = mm(split(keys[head]), pair)
        ratio = decay(columns[:, head : head + 1], run[head], t, j)
        coupling.append(jnp.where(t > j, gram * ratio * beta(head), 0.0))
    inverse = invert(coupling, t, j)
    mixed = []
    for head in range(heads):
        inverse_out[head, 0] = inverse[head][0]
        inverse_out[head, 1] = inverse[head][1]
        last = run[head][:, CHUNK - 1 : CHUNK]
        tail = keys_t[head] * jnp.exp(last - run[head])
        mixed.append(mm(split(tail), inverse[head]))
    transits = []
    states = []
    for head in range(heads):
        value = conv(value_scratch, value_taps, lanes(head), lanes(first + head))
        grow = jnp.exp(columns[:, head : head + 1])
        write = jnp.concatenate([keys[head] * (beta(head) * grow), value * beta(head)], axis=1)
        write = split(write)
        write_out[head, 0] = write[0]
        write_out[head, 1] = write[1]
        last = run[head][:, CHUNK - 1 : CHUNK]
        both = mm(split(mixed[head]), write)
        transits.append(jnp.where(t == j, jnp.exp(last), 0.0) - both[:, :128])
        states.append(both[:, 128:])
    return transits, states


def upper_kernel(
    key_own,
    key_other,
    value_own,
    value_other,
    key_taps,
    value_taps,
    small_own,
    small_other,
    key_cols_out,
    inverse_out,
    write_out,
    transit_out,
    state_out,
    key_scratch,
    value_scratch,
):
    core, _ = place()
    fill(key_scratch, key_own, key_other, None, core, 1, 0)
    fill(value_scratch, value_own, value_other, None, core, 1, 0)
    transits, states = chunk_states(
        1,
        0,
        8,
        key_taps,
        value_taps,
        small_own,
        small_other,
        key_cols_out,
        inverse_out,
        write_out,
        key_scratch,
        value_scratch,
    )
    for head in range(8):
        transit_out[head] = transits[head]
        state_out[head] = states[head]


def lower_kernel(
    group,
    heads,
    key_own,
    key_other,
    value_own,
    value_other,
    key_taps,
    value_taps,
    halo_one,
    halo_two,
    small_own,
    small_other,
    upper_transit,
    upper_state,
    key_cols_out,
    inverse_out,
    write_out,
    first_state_out,
    state_out,
    transit_one_out,
    transit_out,
    code_out,
    key_scratch,
    value_scratch,
):
    core, _ = place()
    first = group * heads
    fill(key_scratch, key_own, key_other, (halo_one, halo_two, 3), core, 0, first * 128)
    fill(value_scratch, value_own, value_other, (halo_one, halo_two, 6), core, 0, first * 128)
    transits, states = chunk_states(
        0,
        first,
        heads,
        key_taps,
        value_taps,
        small_own,
        small_other,
        key_cols_out,
        inverse_out,
        write_out,
        key_scratch,
        value_scratch,
    )
    joined = []
    pairs = [split(upper_transit[first + head]) for head in range(heads)]
    for head in range(heads):
        joined.append(mm(pairs[head], split(states[head])) + upper_state[first + head])
    encode_all(joined, code_out)
    for head in range(heads):
        first_state_out[head] = states[head]
        transit_one_out[head] = transits[head]
        state_out[head] = joined[head]
        transit_out[head] = mm(pairs[head], split(transits[head]))


def queries_kernel(
    group,
    heads,
    first,
    count,
    near,
    query_own,
    query_other,
    query_taps,
    halo_one,
    halo_two,
    small_own,
    small_other,
    key_cols_one,
    inverse_one,
    write_one,
    key_cols_two,
    inverse_two,
    write_two,
    first_state,
    transit_one,
    out,
    moved,
    scratch_one,
    scratch_two,
):
    core, _ = place()
    start = group * heads + first
    fill(scratch_one, query_own, query_other, (halo_one, halo_two, 0), core, 0, start * 128)
    fill(scratch_two, query_own, query_other, None, core, 1, start * 128)
    t, j = iotas(CHUNK, CHUNK)
    apart = t ^ j
    parts = [(head, chunk) for head in range(count) for chunk in range(2)]
    base = 8 * core + start
    run = sums(small_own, small_other, base, parts, core)
    rows = list(run)
    for head, chunk in parts:
        for level in range(near + 1):
            row = 32 + 16 * level + base + head
            rows.append(token_row(small_own, small_other, row, core, chunk))
    columns = rows_table(rows).T

    def held(one, two, head, chunk):
        if chunk:
            return two[start + head, 0], two[start + head, 1]
        return one[first + head, 0], one[first + head, 1]

    mixings = []
    queries = []
    for i, (head, chunk) in enumerate(parts):
        lanes = slice(head * 128, head * 128 + 128)
        taps_lanes = slice((start + head) * 128, (start + head) * 128 + 128)
        scratch = scratch_two if chunk else scratch_one
        query = unit(conv(scratch, query_taps, lanes, taps_lanes))
        queries.append(query)
        ratio = decay(columns[:, i : i + 1], run[i], t, j)
        scores = mm(split(query), held(key_cols_one, key_cols_two, head, chunk)) * ratio
        mixings.append(mm(split(scores), held(inverse_one, inverse_two, head, chunk)))
    for i, (head, chunk) in enumerate(parts):
        at = len(parts) + i * (near + 1)
        level_mat = columns[:, at : at + 1]
        for level in range(1, near):
            weight = columns[:, at + level : at + level + 1]
            level_mat = jnp.where(apart >= 1 << (level - 1), weight, level_mat)
        high, low = held(write_one, write_two, head, chunk)
        within = mm(split(mixings[i] * level_mat), (high[:, 128:], low[:, 128:]))
        grow = jnp.exp(columns[:, i : i + 1])
        effective = grow * queries[i] - mm(split(mixings[i]), (high[:, :128], low[:, :128]))
        rows = slice(chunk * CHUNK, chunk * CHUNK + CHUNK)
        if chunk:
            pair = split(effective)
            weight = columns[:, at + near : at + near + 1]
            within = within + weight * mm(pair, split(first_state[first + head]))
            effective = mm(pair, split(transit_one[first + head]))
        out[head, rows, :] = within
        moved[head, rows, :] = effective


def received(refs, head):
    code = None
    scale = None
    for ref in refs:
        tail = ref.shape[0] - 16 + head
        part = ref[head * 128 : head * 128 + 128, :].astype(F32)
        row = ref[tail : tail + 1, :].astype(F32)
        code = part if code is None else code + part
        scale = row if scale is None else scale + row
    return decode(code, scale)


def pack_rows(scales):
    zeros = jnp.zeros((16 - len(scales), 128), F32)
    return jnp.concatenate(scales + [zeros], axis=0).astype(BF16)


def encode_all(values, code_out):
    scales = []
    for head, value in enumerate(values):
        code, scale = encode(value)
        code_out[head * 128 : head * 128 + 128, :] = code
        scales.append(scale)
    head = len(values)
    code_out[head * 128 : head * 128 + 16, :] = pack_rows(scales)


def join_kernel(level, arrivals, with_transit, shift, *refs):
    state_in = refs[:arrivals]
    refs = refs[arrivals:]
    transit_in = ()
    if with_transit:
        transit_in = refs[:arrivals]
        refs = refs[arrivals:]
    state, transit, code_out = refs[:3]
    refs = refs[3:]
    heads = state.shape[0]
    _, node = place()
    upper = (node >> level) % 2 == 1
    if not with_transit:
        upper = upper & ((node >> (level + 1)) % 2 == 0)

    @pl.when(upper)
    def _():
        fresh = []
        for head in range(heads):
            pair = split(transit[head])
            fresh.append(mm(pair, split(received(state_in, head))) + state[head])
            if with_transit:
                refs[0][head] = fresh[head]
                refs[1][head] = mm(pair, split(received(transit_in, shift + head)))
        encode_all(fresh, code_out)
        if with_transit:
            encode_all([refs[1][head] for head in range(heads)], refs[2])

    if with_transit:

        @pl.when(jnp.logical_not(upper))
        def _():
            encode_all([state[head] for head in range(heads)], code_out)
            for head in range(heads):
                refs[0][head] = state[head]
                refs[1][head] = transit[head]
            encode_all([transit[head] for head in range(heads)], refs[2])


def code_kernel(*refs):
    values = [ref[head] for ref in refs[:-1] for head in range(ref.shape[0])]
    encode_all(values, refs[-1])


def level_weight(own, other, row, core):
    rows = [token_row(own, other, row, core, chunk) for chunk in range(2)]
    columns = rows_table(rows).T
    return jnp.concatenate([columns[:, 0:1], columns[:, 1:2]], axis=0)


def absorb_kernel(level, weight_row, group, heads, arrivals, passed, pieces, *refs):
    state_in = refs[:arrivals]
    transit_in = refs[arrivals : arrivals + passed]
    refs = refs[arrivals + passed :]
    small_own, small_other = refs[:2]
    outs_in = refs[2 : 2 + pieces]
    moved_in = refs[2 + pieces : 2 + 2 * pieces]
    out, moved = refs[2 + 2 * pieces :]
    core, node = place()
    upper = (node >> level) % 2 == 1
    each = heads // pieces
    behind = jnp.bool_(False)
    if passed:
        behind = ((node >> (level - 1)) % 2 == 1) & ((node >> level) > 0)

        @pl.when(behind)
        def _():
            shift = group * heads if level == 1 else 0
            for head in range(heads):
                pair = split(moved_in[head // each][head % each])
                moved[head] = mm(pair, split(received(transit_in, shift + head)))

    @pl.when(jnp.logical_not(behind))
    def _():
        for head in range(heads):
            moved[head] = moved_in[head // each][head % each]

    @pl.when(upper)
    def _():
        for head in range(heads):
            pair = split(moved[head])
            row = weight_row + 8 * core + heads * group + head
            weight = level_weight(small_own, small_other, row, core)
            gain = mm(pair, split(received(state_in, head)))
            out[head] = outs_in[head // each][head % each] + weight * gain

    @pl.when(jnp.logical_not(upper))
    def _():
        for head in range(heads):
            out[head] = outs_in[head // each][head % each]


def tail_kernel(level, weight_row, groups, heads, count, pending, near, arrivals, *refs):
    state_in = [refs[g * arrivals : (g + 1) * arrivals] for g in range(groups)]
    refs = refs[groups * arrivals :]
    query_refs, refs = refs[:7], refs[7:]
    uppers, refs = refs[:3], refs[3:]
    lowers = {}
    for group in sorted({group for group, _ in pending}):
        lowers[group], refs = refs[:5], refs[5:]
    pieces = heads // count
    outs_in = {}
    for group in range(groups):
        for piece in range(pieces):
            if (group, piece) not in pending:
                outs_in[group, piece], refs = refs[:2], refs[2:]
    outs, refs = refs[: 2 * groups], refs[2 * groups :]
    scratch, refs = refs[:2], refs[2:]
    for group, piece in pending:
        temporary, refs = refs[:2], refs[2:]
        made = lowers[group]
        queries_kernel(
            group,
            heads,
            piece * count,
            count,
            near,
            *query_refs,
            *made[:3],
            *uppers,
            *made[3:],
            *temporary,
            *scratch,
        )
        outs_in[group, piece] = temporary
    for group in range(groups):
        absorb_kernel(
            level,
            weight_row,
            group,
            heads,
            arrivals,
            0,
            pieces,
            *state_in[group],
            *query_refs[5:7],
            *[outs_in[group, piece][0] for piece in range(pieces)],
            *[outs_in[group, piece][1] for piece in range(pieces)],
            outs[2 * group],
            outs[2 * group + 1],
        )


def finish_kernel(level, weight_row, group, heads, arrivals, passed, pieces, *refs):
    state_in = refs[:arrivals]
    transit_in = refs[arrivals : arrivals + passed]
    refs = refs[arrivals + passed :]
    small_own, small_other, gate_own, gate_other, gain = refs[:5]
    outs_in = refs[5 : 5 + pieces]
    moved_in = refs[5 + pieces : 5 + 2 * pieces]
    stay, leave, total = refs[5 + 2 * pieces :]
    core, node = place()
    upper = (node >> level) % 2 == 1
    each = heads // pieces

    def add(through):
        states = [received(state_in, head) for head in range(heads)]
        if through:
            shift = group * heads if level == 1 else 0
            states = [
                mm(split(received(transit_in, shift + head)), split(states[head]))
                for head in range(heads)
            ]
        for head in range(heads):
            row = weight_row + 8 * core + heads * group + head
            weight = level_weight(small_own, small_other, row, core)
            extra = mm(split(moved_in[head // each][head % each]), split(states[head]))
            total[head] = outs_in[head // each][head % each] + weight * extra

    through = jnp.bool_(False)
    if passed:
        through = (node >> (level - 1)) % 2 == 1

    @pl.when(upper & jnp.logical_not(through))
    def _():
        add(False)

    if passed:

        @pl.when(upper & through)
        def _():
            add(True)

    @pl.when(jnp.logical_not(upper))
    def _():
        for head in range(heads):
            total[head] = outs_in[head // each][head % each]

    lanes_all = heads * 128
    start = pl.multiple_of(core * 8 * HEAD_DIM + group * lanes_all, lanes_all)
    gates = (
        gate_own[:, group * lanes_all : (group + 1) * lanes_all],
        gate_other[:, pl.ds(start, lanes_all)],
    )
    for head in range(heads):
        lanes = slice(head * 128, head * 128 + 128)
        for gate, chunk, target in ((gates[0], core, stay), (gates[1], 1 - core, leave)):
            rows = pl.ds(pl.multiple_of(chunk * CHUNK, CHUNK), CHUNK)
            attended = total[head, rows, :]
            scale = lax.rsqrt(jnp.mean(attended * attended, axis=-1, keepdims=True) + 1e-5)
            gated = attended * scale * gain[...] * silu(gate[:, lanes].astype(F32))
            target[:, lanes] = gated.astype(BF16)


def swap_kernel(*refs):
    out = refs[-1]
    count = (len(refs) - 1) // 2
    core, _ = place()
    half = out.shape[1] // 2
    width = half // count
    for i in range(count):
        start = pl.multiple_of(core * half + i * width, width)
        out[:, pl.ds(start, width)] = refs[i][...]
        start = pl.multiple_of((1 - core) * half + i * width, width)
        out[:, pl.ds(start, width)] = refs[count + i][...]


def struct(shape, dtype=F32):
    return jax.ShapeDtypeStruct(shape, dtype)


def params(mib):
    return pltpu.CompilerParams(vmem_limit_bytes=mib << 20)


def cost(flops):
    return pl.CostEstimate(flops=flops, bytes_accessed=1_000_000, transcendentals=0)


GROUPS = 2
PIECES = 1


def per_device(
    query_rows,
    key_rows,
    value_rows,
    query_taps,
    key_taps,
    value_taps,
    log_alpha,
    write_strength,
    tier_mixture,
    output_gate,
    norm_gain,
):
    rows, width = query_rows.shape
    half = width // 2
    size = lax.axis_size("seq")
    nodes = size // 2
    level_total = tier_mixture.shape[0]
    near = CHUNK.bit_length()
    heads = 8 // GROUPS
    lanes = heads * 128
    shard_bits = nodes.bit_length() - 1
    cores = [(i, i ^ 1) for i in range(size)]
    small_rows = 16 * (2 + level_total)
    key_other = lax.ppermute(key_rows, "seq", cores)
    value_other = lax.ppermute(value_rows, "seq", cores)
    half_shape = struct((rows, half), BF16)
    taps_shape = struct((4, half))
    (
        query_half,
        key_half,
        value_half,
        gate_half,
        query_taps_half,
        key_taps_half,
        value_taps_half,
        halo,
        small,
        gain,
    ) = pl.pallas_call(
        prepare_kernel,
        in_specs=[pl.BlockSpec(memory_space=pltpu.HBM)] * 11,
        out_shape=[half_shape] * 4
        + [taps_shape] * 3
        + [struct((16, width), BF16), struct((small_rows, 128)), struct((1, 128))],
        scratch_shapes=[pltpu.VMEM((3, 16, width), BF16), pltpu.SemaphoreType.DMA((14,))],
        compiler_params=params(8),
        name="prepare",
    )(
        *[
            pltpu.with_memory_space_constraint(x, pltpu.HBM)
            for x in (
                query_rows,
                key_rows,
                value_rows,
                output_gate,
                log_alpha,
                write_strength,
                tier_mixture.reshape(level_total * 16, rows),
                query_taps,
                key_taps,
                value_taps,
                norm_gain.reshape(1, 128),
            )
        ]
    )
    small_other = lax.ppermute(small, "seq", cores)
    halo_one = lax.ppermute(halo, "seq", [(i, i + 1) for i in range(1, size - 1, 2)])
    halo_two = lax.ppermute(halo, "seq", [(i, i + 2) for i in range(1, size - 1, 2)])

    def fan(value, level, keep):
        span = 1 << level
        results = []
        for offset in reversed(range(span)):
            route = []
            for low in range(0, nodes, 2 * span):
                source, target = low + span - 1, low + span + offset
                if keep(target):
                    route += [(2 * source + c, 2 * target + c) for c in range(2)]
            results.append(lax.ppermute(value, "seq", route))
        return results

    def held(count):
        return [
            struct((count, 2, 128, 128), BF16),
            struct((count, 2, 128, 128), BF16),
            struct((count, 2, 128, 256), BF16),
        ]

    square = (heads, 128, 128)
    code_shape = struct((heads * 128 + 16, 128), BF16)
    upper = pl.pallas_call(
        upper_kernel,
        out_shape=held(8) + [struct((8, 128, 128))] * 2,
        scratch_shapes=[pltpu.VMEM((8 + CHUNK, half), F32)] * 2,
        compiler_params=params(24),
        cost_estimate=cost(4_000_000_000),
        name="upper",
    )(
        key_half,
        key_other,
        value_half,
        value_other,
        key_taps_half,
        value_taps_half,
        small,
        small_other,
    )
    local = []
    arrived = []
    after = upper[4]
    for group in range(GROUPS):
        after, halo_first = lax.optimization_barrier((after, halo_one))
        made = pl.pallas_call(
            functools.partial(lower_kernel, group, heads),
            out_shape=held(heads)
            + [struct(square), struct(square), struct(square), struct(square), code_shape],
            scratch_shapes=[pltpu.VMEM((8 + CHUNK, lanes), F32)] * 2,
            compiler_params=params(24),
            cost_estimate=cost(2_500_000_000),
            name="lower",
        )(
            key_half,
            key_other,
            value_half,
            value_other,
            key_taps_half,
            value_taps_half,
            halo_first,
            halo_two,
            small,
            small_other,
            upper[3],
            upper[4],
        )
        local.append(made)
        after = made[7]
        arrived.append(fan(made[7], 0, lambda target: True) if shard_bits else [])
    after, query_late, gate_late = lax.optimization_barrier((after, query_rows, output_gate))
    query_other = lax.ppermute(query_late, "seq", cores)
    gate_other = lax.ppermute(gate_late, "seq", cores)
    after, query_other, gate_other = lax.optimization_barrier((after, query_other, gate_other))
    state = [x[4] for x in local]
    transit = [x[6] for x in local]
    count = heads // PIECES
    outs = [[] for _ in range(GROUPS)]
    moved = [[] for _ in range(GROUPS)]
    pending = [(group, piece) for group in range(GROUPS) for piece in range(PIECES)]

    def ask(after):
        group, piece = pending.pop(0)
        made = local[group]
        shape = struct((count, 2 * CHUNK, 128))
        after, small_here = lax.optimization_barrier((after, small))
        out, move = pl.pallas_call(
            functools.partial(queries_kernel, group, heads, piece * count, count, near),
            out_shape=[shape, shape],
            scratch_shapes=[pltpu.VMEM((8 + CHUNK, count * 128), F32)] * 2,
            compiler_params=params(16),
            cost_estimate=cost(4_000_000_000),
            name="queries",
        )(
            query_half,
            query_other,
            query_taps_half,
            halo_one,
            halo_two,
            small_here,
            small_other,
            *made[:3],
            *upper[:3],
            made[3],
            made[5],
        )
        outs[group].append(out)
        moved[group].append(move)
        return out

    moved_shape = struct((heads, 2 * CHUNK, 128))
    transit_codes = [None] * GROUPS

    def send_transit(after):
        after, first_transit = lax.optimization_barrier((after, transit[0]))
        return pl.pallas_call(
            code_kernel,
            out_shape=struct((8 * 128 + 16, 128), BF16),
            compiler_params=params(8),
            cost_estimate=cost(300_000_000),
            name="code",
        )(first_transit, *transit[1:])

    shifts = [heads * group for group in range(GROUPS)]
    passing = [[]] * GROUPS
    for level in range(shard_bits - 1):
        keeps = level < shard_bits - 2

        def wanted(target):
            return keeps or target >> (level + 1) > 0

        if level:
            fanned = [fan(x, level, wanted) for x in transit_codes]
        elif keeps:
            fanned = [fan(send_transit(after), level, wanted)] * GROUPS
        following = []
        for group in range(GROUPS):
            shapes = [code_shape]
            operands = list(arrived[group])
            if keeps:
                shapes += [struct(square), struct(square), code_shape]
                operands += fanned[group]
            after, state_here = lax.optimization_barrier((after, state[group]))
            joined = pl.pallas_call(
                functools.partial(
                    join_kernel, level, len(arrived[group]), keeps, shifts[group]
                ),
                out_shape=shapes,
                compiler_params=params(12),
                cost_estimate=cost(4_000_000_000),
                name="join",
            )(*operands, state_here, transit[group])
            after = joined[0]
            if level == 0 and group == 0:
                if not keeps:
                    fanned = [fan(send_transit(after), level, wanted)] * GROUPS
            following.append(fan(joined[0], level + 1, lambda target: True))
            if keeps:
                state[group], transit[group], transit_codes[group] = joined[1:]
        arrivals = len(arrived[0])
        if level == 0:
            after, small_here = lax.optimization_barrier((after, small))
            operands = [x for group in range(GROUPS) for x in arrived[group]]
            operands += [query_half, query_other, query_taps_half, halo_one, halo_two]
            operands += [small_here, small_other, *upper[:3]]
            for group in sorted({group for group, _ in pending}):
                made = local[group]
                operands += [*made[:3], made[3], made[5]]
            for group in range(GROUPS):
                for out, move in zip(outs[group], moved[group]):
                    operands += [out, move]
            results = pl.pallas_call(
                functools.partial(
                    tail_kernel,
                    level,
                    32 + 16 * (near + 1 + level),
                    GROUPS,
                    heads,
                    count,
                    tuple(pending),
                    near,
                    arrivals,
                ),
                out_shape=[moved_shape] * (2 * GROUPS),
                scratch_shapes=[pltpu.VMEM((8 + CHUNK, count * 128), F32)] * 2
                + [pltpu.VMEM((count, 2 * CHUNK, 128), F32)] * (2 * len(pending)),
                compiler_params=params(24),
                cost_estimate=cost(1_000_000),
                name="tail",
            )(*operands)
            pending.clear()
            for group in range(GROUPS):
                outs[group], moved[group] = [results[2 * group]], [results[2 * group + 1]]
        else:
            for group in range(GROUPS):
                out, move = pl.pallas_call(
                    functools.partial(
                        absorb_kernel,
                        level,
                        32 + 16 * (near + 1 + level),
                        group,
                        heads,
                        arrivals,
                        len(passing[group]),
                        len(outs[group]),
                    ),
                    out_shape=[moved_shape, moved_shape],
                    compiler_params=params(12),
                    cost_estimate=cost(800_000_000),
                    name="absorb",
                )(
                    *arrived[group],
                    *passing[group],
                    small,
                    small_other,
                    *outs[group],
                    *moved[group],
                )
                outs[group], moved[group] = [out], [move]
        arrived = following
        passing = fanned
        shifts = [0] * GROUPS
    while pending:
        after = ask(after)

    level = max(shard_bits - 1, 0)
    stays = []
    comes = []
    for group in range(GROUPS):
        stay, leave = pl.pallas_call(
            functools.partial(
                finish_kernel,
                level,
                32 + 16 * (near + 1 + level),
                group,
                heads,
                len(arrived[group]),
                len(passing[group]),
                len(outs[group]),
            ),
            out_shape=[struct((rows, lanes), BF16)] * 2,
            scratch_shapes=[pltpu.VMEM((heads, 2 * CHUNK, 128), F32)],
            compiler_params=params(12),
            cost_estimate=cost(600_000_000),
            name="finish",
        )(
            *arrived[group],
            *passing[group],
            small,
            small_other,
            gate_half,
            gate_other,
            gain,
            *outs[group],
            *moved[group],
        )
        stays.append(stay)
        comes.append(lax.ppermute(leave, "seq", cores))
    return pl.pallas_call(
        swap_kernel,
        out_shape=struct((rows, width), BF16),
        compiler_params=params(4),
        name="swap",
    )(*stays, *comes)


def solution(mesh):
    placed = (
        P(("req", "seq"), None),
        P(("req", "seq"), None),
        P(("req", "seq"), None),
        P(),
        P(),
        P(),
        P(None, ("req", "seq")),
        P(None, ("req", "seq")),
        P(None, None, ("req", "seq")),
        P(("req", "seq"), None),
        P(),
    )
    return jax.shard_map(
        per_device, mesh=mesh, in_specs=placed, out_specs=P(("req", "seq"), None), check_vma=False
    )
```

```python
import functools

import jax
import jax.numpy as jnp
from jax import lax
from jax.experimental import pallas as pl
from jax.experimental.pallas import tpu as pltpu
from jax.sharding import PartitionSpec as P

HEAD_DIM = 128
CHUNK = 128
CODE = 125.0
F32 = jnp.float32
BF16 = jnp.bfloat16


def split(x):
    high = x.astype(BF16)
    return high, (x - high.astype(F32)).astype(BF16)


def dot(a, b):
    return jnp.dot(a, b, preferred_element_type=F32)


def wide(b):
    row = jnp.concatenate(b, axis=1)
    return jnp.concatenate([row, row], axis=0)


def mm(a, b):
    width = b[0].shape[1]
    if b[0].shape[0] <= 128 and (width > 128 or a[0].shape[0] <= 128):
        both = jnp.concatenate([b[0], b[0]], axis=0)
        return dot(jnp.concatenate(a, axis=1), both) + dot(a[0], b[1])
    out = dot(jnp.concatenate(a, axis=1), wide(b))
    return out[:, :width] + out[:, width:]


def silu(u):
    return u / (1.0 + jnp.exp(-u))


def encode(state):
    top = jnp.max(jnp.abs(state), axis=0, keepdims=True)
    scale = (top * 1.02 + 1e-30).astype(BF16).astype(F32)
    grade = jnp.abs(state) / scale
    level = jnp.exp2(grade * (2.0 * CODE) - CODE)
    return jnp.where(state < 0, -level, level).astype(BF16), scale


def decode(code, scale):
    grade = jnp.log2(jnp.abs(code)) * (0.5 / CODE) + 0.5
    size = grade * scale
    return jnp.where(code < 0, -size, size)


def iotas(rows, columns):
    return (
        lax.broadcasted_iota(jnp.int32, (rows, columns), 0),
        lax.broadcasted_iota(jnp.int32, (rows, columns), 1),
    )


def place():
    index = lax.axis_index("seq")
    return index % 2, index // 2


def fill(scratch, own, other, before, core, chunk, first_lane):
    lanes = scratch.shape[1]
    start = pl.multiple_of(core * 8 * HEAD_DIM + first_lane, 128)
    mine = own[:, first_lane : first_lane + lanes]
    theirs = other[:, pl.ds(start, lanes)]
    if before is None:
        last = jnp.where(core == 1, theirs[CHUNK - 16 :], mine[CHUNK - 16 :]).astype(F32)[13:16]
    else:
        one, two, first = before
        rows = one[:, pl.ds(start, lanes)].astype(F32) + two[:, pl.ds(start, lanes)].astype(F32)
        last = rows[first : first + 3]
    scratch[5:8, :] = last
    scratch[8 : 8 + CHUNK, :] = jnp.where(core == chunk, mine, theirs).astype(F32)


def conv(scratch, taps, columns, taps_columns):
    total = None
    for tap in range(4):
        part = taps[tap : tap + 1, taps_columns] * scratch[5 + tap : 5 + tap + CHUNK, columns]
        total = part if total is None else total + part
    return silu(total)


def unit(rows):
    return rows * lax.rsqrt(jnp.sum(rows * rows, axis=-1, keepdims=True) + 1e-6)


def token_row(own, other, row, core, chunk):
    return jnp.where(core == chunk, own[pl.ds(row, 1), :], other[pl.ds(row, 1), :])


def rows_table(rows):
    pad = -len(rows) % 8
    if pad:
        rows = rows + [jnp.zeros((pad, CHUNK), F32)]
    return jnp.concatenate(rows, axis=0)


def sums(own, other, base, parts, core):
    rows = [token_row(own, other, base + head, core, chunk) for head, chunk in parts]
    t, j = iotas(CHUNK, CHUNK)
    upper = (t <= j).astype(F32)
    run = jnp.dot(
        rows_table(rows), upper, preferred_element_type=F32, precision=lax.Precision.HIGHEST
    )
    return [run[i : i + 1] for i in range(len(parts))]


def invert(coupling, t, j):
    apart = t ^ j
    count = len(coupling)
    near = [split(jnp.where(apart < 8, -a, 0.0)) for a in coupling]
    eye = (t == j).astype(F32)
    squared = [mm(n, n) for n in near]
    grown = []
    fourth = []
    for i in range(count):
        base = eye + near[i][0].astype(F32) + near[i][1].astype(F32)
        left = split(jnp.concatenate([squared[i], base], axis=0))
        both = mm(left, split(squared[i]))
        fourth.append(both[:CHUNK])
        grown.append(base + both[CHUNK:])
    inverse = [
        grown[i] + mm(split(grown[i]), split(fourth[i])) for i in range(count)
    ]
    inverse = [split(x) for x in inverse]
    size = 8
    while size < CHUNK:
        starts = range(size, CHUNK, 2 * size)

        def pick(x):
            return jnp.concatenate([x[s : s + size] for s in starts], axis=0)

        zero = jnp.zeros((size, CHUNK), BF16)

        def spread(x):
            pieces = []
            for k in range(len(starts)):
                pieces += [zero, x[k * size : (k + 1) * size]]
            return jnp.concatenate(pieces, axis=0)

        def merge(x, rows):
            pieces = []
            for k, s in enumerate(starts):
                pieces += [x[s - size : s], rows[k * size : (k + 1) * size]]
            return jnp.concatenate(pieces, axis=0)

        mask = pick((apart >= size) & (apart < 2 * size))
        middle = []
        for i in range(count):
            lower = split(jnp.where(mask, pick(coupling[i]), 0.0))
            middle.append(split(mm(lower, inverse[i])))
        for i in range(count):
            high, low = inverse[i]
            rows = (pick(high), pick(low))
            change = mm(rows, tuple(spread(m) for m in middle[i]))
            fresh = split(rows[0].astype(F32) + rows[1].astype(F32) - change)
            inverse[i] = (merge(high, fresh[0]), merge(low, fresh[1]))
        size *= 2
    return inverse


def decay(column, row, t, j):
    return jnp.exp(jnp.where(t >= j, column - row, -1e30))


def prepare_kernel(query, key, value, gate, log_alpha, strength, mixture, query_taps, key_taps,
                   value_taps, gain, query_half, key_half, value_half, gate_half, query_taps_half,
                   key_taps_half, value_taps_half, halo, small, gain_out, tails, sems):
    core, _ = place()
    rows, half = query_half.shape
    lanes = pl.ds(pl.multiple_of(core * half, half), half)
    copies = []

    def copy(source, target):
        made = pltpu.make_async_copy(source, target, sems.at[len(copies)])
        made.start()
        copies.append(made)

    for i, x in enumerate((query, key, value)):
        copy(x.at[rows - 16 : rows, :], tails.at[i])
    copy(log_alpha, small.at[0:16])
    copy(strength, small.at[16:32])
    copy(mixture, small.at[32 : small.shape[0]])
    for x, y in (
        (key, key_half),
        (value, value_half),
        (key_taps, key_taps_half),
        (value_taps, value_taps_half),
        (query_taps, query_taps_half),
        (query, query_half),
        (gate, gate_half),
    ):
        copy(x.at[:, lanes], y)
    copy(gain, gain_out)
    for made in copies:
        made.wait()
    message = [tails[i][13:16, :].astype(F32) for i in range(3)]
    message.append(jnp.zeros((7, 2 * half), F32))
    halo[...] = jnp.concatenate(message, axis=0).astype(BF16)


def chunk_states(
    chunk,
    first,
    heads,
    key_taps,
    value_taps,
    small_own,
    small_other,
    key_cols_out,
    inverse_out,
    write_out,
    key_scratch,
    value_scratch,
):
    core, _ = place()
    t, j = iotas(CHUNK, CHUNK)
    base = 8 * core + first
    parts = [(head, chunk) for head in range(heads)]
    run = sums(small_own, small_other, base, parts, core)
    strengths = [
        token_row(small_own, small_other, 16 + base + head, core, chunk) for head in range(heads)
    ]
    columns = rows_table(run + strengths).T

    def lanes(head):
        return slice(head * 128, head * 128 + 128)

    def beta(head):
        return columns[:, heads + head : heads + head + 1]

    keys = [
        unit(conv(key_scratch, key_taps, lanes(head), lanes(first + head)))
        for head in range(heads)
    ]
    keys_t = [key.T for key in keys]
    coupling = []
    for head in range(heads):
        pair = split(keys_t[head])
        key_cols_out[head, 0] = pair[0]
        key_cols_out[head, 1] = pair[1]
        gram = mm(split(keys[head]), pair)
        ratio = decay(columns[:, head : head + 1], run[head], t, j)
        coupling.append(jnp.where(t > j, gram * ratio * beta(head), 0.0))
    inverse = invert(coupling, t, j)
    mixed = []
    for head in range(heads):
        inverse_out[head, 0] = inverse[head][0]
        inverse_out[head, 1] = inverse[head][1]
        last = run[head][:, CHUNK - 1 : CHUNK]
        tail = keys_t[head] * jnp.exp(last - run[head])
        mixed.append(mm(split(tail), inverse[head]))
    transits = []
    states = []
    for head in range(heads):
        value = conv(value_scratch, value_taps, lanes(head), lanes(first + head))
        grow = jnp.exp(columns[:, head : head + 1])
        write = jnp.concatenate([keys[head] * (beta(head) * grow), value * beta(head)], axis=1)
        write = split(write)
        write_out[head, 0] = write[0]
        write_out[head, 1] = write[1]
        last = run[head][:, CHUNK - 1 : CHUNK]
        both = mm(split(mixed[head]), write)
        transits.append(jnp.where(t == j, jnp.exp(last), 0.0) - both[:, :128])
        states.append(both[:, 128:])
    return transits, states


def upper_kernel(
    key_own,
    key_other,
    value_own,
    value_other,
    key_taps,
    value_taps,
    small_own,
    small_other,
    key_cols_out,
    inverse_out,
    write_out,
    transit_out,
    state_out,
    key_scratch,
    value_scratch,
):
    core, _ = place()
    fill(key_scratch, key_own, key_other, None, core, 1, 0)
    fill(value_scratch, value_own, value_other, None, core, 1, 0)
    transits, states = chunk_states(
        1,
        0,
        8,
        key_taps,
        value_taps,
        small_own,
        small_other,
        key_cols_out,
        inverse_out,
        write_out,
        key_scratch,
        value_scratch,
    )
    for head in range(8):
        transit_out[head] = transits[head]
        state_out[head] = states[head]


def lower_kernel(
    group,
    heads,
    key_own,
    key_other,
    value_own,
    value_other,
    key_taps,
    value_taps,
    halo_one,
    halo_two,
    small_own,
    small_other,
    upper_transit,
    upper_state,
    key_cols_out,
    inverse_out,
    write_out,
    first_state_out,
    state_out,
    transit_one_out,
    transit_out,
    code_out,
    key_scratch,
    value_scratch,
):
    core, _ = place()
    first = group * heads
    fill(key_scratch, key_own, key_other, (halo_one, halo_two, 3), core, 0, first * 128)
    fill(value_scratch, value_own, value_other, (halo_one, halo_two, 6), core, 0, first * 128)
    transits, states = chunk_states(
        0,
        first,
        heads,
        key_taps,
        value_taps,
        small_own,
        small_other,
        key_cols_out,
        inverse_out,
        write_out,
        key_scratch,
        value_scratch,
    )
    joined = []
    pairs = [split(upper_transit[first + head]) for head in range(heads)]
    for head in range(heads):
        joined.append(mm(pairs[head], split(states[head])) + upper_state[first + head])
    encode_all(joined, code_out)
    for head in range(heads):
        first_state_out[head] = states[head]
        transit_one_out[head] = transits[head]
        state_out[head] = joined[head]
        transit_out[head] = mm(pairs[head], split(transits[head]))


def queries_kernel(
    group,
    heads,
    first,
    count,
    near,
    query_own,
    query_other,
    query_taps,
    halo_one,
    halo_two,
    small_own,
    small_other,
    key_cols_one,
    inverse_one,
    write_one,
    key_cols_two,
    inverse_two,
    write_two,
    first_state,
    transit_one,
    out,
    moved,
    scratch_one,
    scratch_two,
):
    core, _ = place()
    start = group * heads + first
    fill(scratch_one, query_own, query_other, (halo_one, halo_two, 0), core, 0, start * 128)
    fill(scratch_two, query_own, query_other, None, core, 1, start * 128)
    t, j = iotas(CHUNK, CHUNK)
    apart = t ^ j
    parts = [(head, chunk) for head in range(count) for chunk in range(2)]
    base = 8 * core + start
    run = sums(small_own, small_other, base, parts, core)
    rows = list(run)
    for head, chunk in parts:
        for level in range(near + 1):
            row = 32 + 16 * level + base + head
            rows.append(token_row(small_own, small_other, row, core, chunk))
    columns = rows_table(rows).T

    def held(one, two, head, chunk):
        if chunk:
            return two[start + head, 0], two[start + head, 1]
        return one[first + head, 0], one[first + head, 1]

    mixings = []
    queries = []
    for i, (head, chunk) in enumerate(parts):
        lanes = slice(head * 128, head * 128 + 128)
        taps_lanes = slice((start + head) * 128, (start + head) * 128 + 128)
        scratch = scratch_two if chunk else scratch_one
        query = unit(conv(scratch, query_taps, lanes, taps_lanes))
        queries.append(query)
        ratio = decay(columns[:, i : i + 1], run[i], t, j)
        scores = mm(split(query), held(key_cols_one, key_cols_two, head, chunk)) * ratio
        mixings.append(mm(split(scores), held(inverse_one, inverse_two, head, chunk)))
    for i, (head, chunk) in enumerate(parts):
        at = len(parts) + i * (near + 1)
        level_mat = columns[:, at : at + 1]
        for level in range(1, near):
            weight = columns[:, at + level : at + level + 1]
            level_mat = jnp.where(apart >= 1 << (level - 1), weight, level_mat)
        high, low = held(write_one, write_two, head, chunk)
        within = mm(split(mixings[i] * level_mat), (high[:, 128:], low[:, 128:]))
        grow = jnp.exp(columns[:, i : i + 1])
        effective = grow * queries[i] - mm(split(mixings[i]), (high[:, :128], low[:, :128]))
        rows = slice(chunk * CHUNK, chunk * CHUNK + CHUNK)
        if chunk:
            pair = split(effective)
            weight = columns[:, at + near : at + near + 1]
            within = within + weight * mm(pair, split(first_state[first + head]))
            effective = mm(pair, split(transit_one[first + head]))
        out[head, rows, :] = within
        moved[head, rows, :] = effective


def received(refs, head):
    code = None
    scale = None
    for ref in refs:
        tail = ref.shape[0] - 16 + head
        part = ref[head * 128 : head * 128 + 128, :].astype(F32)
        row = ref[tail : tail + 1, :].astype(F32)
        code = part if code is None else code + part
        scale = row if scale is None else scale + row
    return decode(code, scale)


def pack_rows(scales):
    zeros = jnp.zeros((16 - len(scales), 128), F32)
    return jnp.concatenate(scales + [zeros], axis=0).astype(BF16)


def encode_all(values, code_out):
    scales = []
    for head, value in enumerate(values):
        code, scale = encode(value)
        code_out[head * 128 : head * 128 + 128, :] = code
        scales.append(scale)
    head = len(values)
    code_out[head * 128 : head * 128 + 16, :] = pack_rows(scales)


def join_kernel(level, arrivals, with_transit, shift, waits, *refs):
    refs = refs[waits:]
    state_in = refs[:arrivals]
    refs = refs[arrivals:]
    transit_in = ()
    if with_transit:
        transit_in = refs[:arrivals]
        refs = refs[arrivals:]
    state, transit, code_out = refs[:3]
    refs = refs[3:]
    heads = state.shape[0]
    _, node = place()
    upper = (node >> level) % 2 == 1
    if not with_transit:
        late = (node >> (level + 1)) % 2 == 1
        riding = late & jnp.logical_not(upper)
        upper = upper & jnp.logical_not(late)

        @pl.when(riding)
        def _():
            encode_all([transit[head] for head in range(heads)], code_out)

    @pl.when(upper)
    def _():
        fresh = []
        for head in range(heads):
            pair = split(transit[head])
            fresh.append(mm(pair, split(received(state_in, head))) + state[head])
            if with_transit:
                refs[0][head] = fresh[head]
                refs[1][head] = mm(pair, split(received(transit_in, shift + head)))
        encode_all(fresh, code_out)
        if with_transit:
            encode_all([refs[1][head] for head in range(heads)], refs[2])

    if with_transit:

        @pl.when(jnp.logical_not(upper))
        def _():
            encode_all([state[head] for head in range(heads)], code_out)
            for head in range(heads):
                refs[0][head] = state[head]
                refs[1][head] = transit[head]
            encode_all([transit[head] for head in range(heads)], refs[2])


def code_kernel(*refs):
    values = [ref[head] for ref in refs[:-1] for head in range(ref.shape[0])]
    encode_all(values, refs[-1])


def level_weight(own, other, row, core):
    rows = [token_row(own, other, row, core, chunk) for chunk in range(2)]
    columns = rows_table(rows).T
    return jnp.concatenate([columns[:, 0:1], columns[:, 1:2]], axis=0)


def absorb_kernel(level, weight_row, group, heads, arrivals, passed, pieces, *refs):
    state_in = refs[:arrivals]
    transit_in = refs[arrivals : arrivals + passed]
    refs = refs[arrivals + passed :]
    small_own, small_other = refs[:2]
    outs_in = refs[2 : 2 + pieces]
    moved_in = refs[2 + pieces : 2 + 2 * pieces]
    out, moved = refs[2 + 2 * pieces :]
    core, node = place()
    upper = (node >> level) % 2 == 1
    each = heads // pieces
    behind = jnp.bool_(False)
    if passed:
        behind = ((node >> (level - 1)) % 2 == 1) & ((node >> level) > 0)

        @pl.when(behind)
        def _():
            shift = group * heads if level == 1 else 0
            for head in range(heads):
                pair = split(moved_in[head // each][head % each])
                moved[head] = mm(pair, split(received(transit_in, shift + head)))

    @pl.when(jnp.logical_not(behind))
    def _():
        for head in range(heads):
            moved[head] = moved_in[head // each][head % each]

    @pl.when(upper)
    def _():
        for head in range(heads):
            pair = split(moved[head])
            row = weight_row + 8 * core + heads * group + head
            weight = level_weight(small_own, small_other, row, core)
            gain = mm(pair, split(received(state_in, head)))
            out[head] = outs_in[head // each][head % each] + weight * gain

    @pl.when(jnp.logical_not(upper))
    def _():
        for head in range(heads):
            out[head] = outs_in[head // each][head % each]


def tail_kernel(level, weight_row, groups, heads, count, pending, near, arrivals, *refs):
    state_in = [refs[g * arrivals : (g + 1) * arrivals] for g in range(groups)]
    refs = refs[groups * arrivals :]
    query_refs, refs = refs[:7], refs[7:]
    uppers, refs = refs[:3], refs[3:]
    lowers = {}
    for group in sorted({group for group, _ in pending}):
        lowers[group], refs = refs[:5], refs[5:]
    pieces = heads // count
    outs_in = {}
    for group in range(groups):
        for piece in range(pieces):
            if (group, piece) not in pending:
                outs_in[group, piece], refs = refs[:2], refs[2:]
    outs, refs = refs[: 2 * groups], refs[2 * groups :]
    scratch, refs = refs[:2], refs[2:]
    for group, piece in pending:
        temporary, refs = refs[:2], refs[2:]
        made = lowers[group]
        queries_kernel(
            group,
            heads,
            piece * count,
            count,
            near,
            *query_refs,
            *made[:3],
            *uppers,
            *made[3:],
            *temporary,
            *scratch,
        )
        outs_in[group, piece] = temporary
    for group in range(groups):
        absorb_kernel(
            level,
            weight_row,
            group,
            heads,
            arrivals,
            0,
            pieces,
            *state_in[group],
            *query_refs[5:7],
            *[outs_in[group, piece][0] for piece in range(pieces)],
            *[outs_in[group, piece][1] for piece in range(pieces)],
            outs[2 * group],
            outs[2 * group + 1],
        )


def finish_kernel(level, weight_row, group, heads, arrivals, pieces, *refs):
    refs = refs[min(group, 1) :]
    state_in = refs[:arrivals]
    refs = refs[arrivals:]
    small_own, small_other, gate_own, gate_other, gain = refs[:5]
    outs_in = refs[5 : 5 + pieces]
    moved_in = refs[5 + pieces : 5 + 2 * pieces]
    stay, leave, total = refs[5 + 2 * pieces :]
    core, node = place()
    upper = (node >> level) % 2 == 1
    each = heads // pieces

    def add(states, transits):
        for head in range(heads):
            found = split(received(states, head))
            if transits is not None:
                found = split(mm(split(received(transits, head)), found))
            row = weight_row + 8 * core + heads * group + head
            weight = level_weight(small_own, small_other, row, core)
            extra = mm(split(moved_in[head // each][head % each]), found)
            total[head] = outs_in[head // each][head % each] + weight * extra

    if level:
        through = (node >> (level - 1)) % 2 == 1
        far, close = state_in[: arrivals // 2], state_in[arrivals // 2 :]

        @pl.when(upper & through)
        def _():
            add(far, close)

        @pl.when(upper & jnp.logical_not(through))
        def _():
            add(close, None)

    else:

        @pl.when(upper)
        def _():
            add(state_in, None)

    @pl.when(jnp.logical_not(upper))
    def _():
        for head in range(heads):
            total[head] = outs_in[head // each][head % each]

    lanes_all = heads * 128
    start = pl.multiple_of(core * 8 * HEAD_DIM + group * lanes_all, lanes_all)
    gates = (
        gate_own[:, group * lanes_all : (group + 1) * lanes_all],
        gate_other[:, pl.ds(start, lanes_all)],
    )
    for head in range(heads):
        lanes = slice(head * 128, head * 128 + 128)
        for gate, chunk, target in ((gates[0], core, stay), (gates[1], 1 - core, leave)):
            rows = pl.ds(pl.multiple_of(chunk * CHUNK, CHUNK), CHUNK)
            attended = total[head, rows, :]
            scale = lax.rsqrt(jnp.mean(attended * attended, axis=-1, keepdims=True) + 1e-5)
            gated = attended * scale * gain[...] * silu(gate[:, lanes].astype(F32))
            target[:, lanes] = gated.astype(BF16)


def swap_kernel(*refs):
    out = refs[-1]
    count = (len(refs) - 1) // 2
    core, _ = place()
    half = out.shape[1] // 2
    width = half // count
    for i in range(count):
        start = pl.multiple_of(core * half + i * width, width)
        out[:, pl.ds(start, width)] = refs[i][...]
        start = pl.multiple_of((1 - core) * half + i * width, width)
        out[:, pl.ds(start, width)] = refs[count + i][...]


def struct(shape, dtype=F32):
    return jax.ShapeDtypeStruct(shape, dtype)


def params(mib):
    return pltpu.CompilerParams(vmem_limit_bytes=mib << 20)


def cost(flops):
    return pl.CostEstimate(flops=flops, bytes_accessed=1_000_000, transcendentals=0)


GROUPS = 2
PIECES = 1


def per_device(
    query_rows,
    key_rows,
    value_rows,
    query_taps,
    key_taps,
    value_taps,
    log_alpha,
    write_strength,
    tier_mixture,
    output_gate,
    norm_gain,
):
    rows, width = query_rows.shape
    half = width // 2
    size = lax.axis_size("seq")
    nodes = size // 2
    level_total = tier_mixture.shape[0]
    near = CHUNK.bit_length()
    heads = 8 // GROUPS
    lanes = heads * 128
    shard_bits = nodes.bit_length() - 1
    cores = [(i, i ^ 1) for i in range(size)]
    small_rows = 16 * (2 + level_total)
    key_other = lax.ppermute(key_rows, "seq", cores)
    value_other = lax.ppermute(value_rows, "seq", cores)
    half_shape = struct((rows, half), BF16)
    taps_shape = struct((4, half))
    (
        query_half,
        key_half,
        value_half,
        gate_half,
        query_taps_half,
        key_taps_half,
        value_taps_half,
        halo,
        small,
        gain,
    ) = pl.pallas_call(
        prepare_kernel,
        in_specs=[pl.BlockSpec(memory_space=pltpu.HBM)] * 11,
        out_shape=[half_shape] * 4
        + [taps_shape] * 3
        + [struct((16, width), BF16), struct((small_rows, 128)), struct((1, 128))],
        scratch_shapes=[pltpu.VMEM((3, 16, width), BF16), pltpu.SemaphoreType.DMA((14,))],
        compiler_params=params(8),
        name="prepare",
    )(
        *[
            pltpu.with_memory_space_constraint(x, pltpu.HBM)
            for x in (
                query_rows,
                key_rows,
                value_rows,
                output_gate,
                log_alpha,
                write_strength,
                tier_mixture.reshape(level_total * 16, rows),
                query_taps,
                key_taps,
                value_taps,
                norm_gain.reshape(1, 128),
            )
        ]
    )
    small_other = lax.ppermute(small, "seq", cores)
    halo_one = lax.ppermute(halo, "seq", [(i, i + 1) for i in range(1, size - 1, 2)])
    halo_two = lax.ppermute(halo, "seq", [(i, i + 2) for i in range(1, size - 1, 2)])

    def fan(value, level, riders=False):
        span = 1 << level
        results = []
        for offset in reversed(range(span)):
            route = []
            for low in range(0, nodes, 2 * span):
                hops = [(low + span - 1, low + span + offset)]
                if riders and 2 * offset < span:
                    middle = low + span + span // 2
                    hops.append((middle - 1, middle + offset))
                for source, target in hops:
                    route += [(2 * source + c, 2 * target + c) for c in range(2)]
            results.append(lax.ppermute(value, "seq", route))
        return results

    def held(count):
        return [
            struct((count, 2, 128, 128), BF16),
            struct((count, 2, 128, 128), BF16),
            struct((count, 2, 128, 256), BF16),
        ]

    square = (heads, 128, 128)
    code_shape = struct((heads * 128 + 16, 128), BF16)
    upper = pl.pallas_call(
        upper_kernel,
        out_shape=held(8) + [struct((8, 128, 128))] * 2,
        scratch_shapes=[pltpu.VMEM((8 + CHUNK, half), F32)] * 2,
        compiler_params=params(24),
        cost_estimate=cost(4_000_000_000),
        name="upper",
    )(
        key_half,
        key_other,
        value_half,
        value_other,
        key_taps_half,
        value_taps_half,
        small,
        small_other,
    )
    local = []
    arrived = []
    after = upper[4]
    for group in range(GROUPS):
        after, halo_first = lax.optimization_barrier((after, halo_one))
        made = pl.pallas_call(
            functools.partial(lower_kernel, group, heads),
            out_shape=held(heads)
            + [struct(square), struct(square), struct(square), struct(square), code_shape],
            scratch_shapes=[pltpu.VMEM((8 + CHUNK, lanes), F32)] * 2,
            compiler_params=params(24),
            cost_estimate=cost(2_500_000_000),
            name="lower",
        )(
            key_half,
            key_other,
            value_half,
            value_other,
            key_taps_half,
            value_taps_half,
            halo_first,
            halo_two,
            small,
            small_other,
            upper[3],
            upper[4],
        )
        local.append(made)
        after = made[7]
        arrived.append(fan(made[7], 0) if shard_bits else [])

    def swap_rows(after):
        _, query_late, gate_late = lax.optimization_barrier((after, query_rows, output_gate))
        return lax.ppermute(query_late, "seq", cores), lax.ppermute(gate_late, "seq", cores)

    query_other, gate_other = swap_rows(local[0][7])
    state = [x[4] for x in local]
    transit = [x[6] for x in local]
    count = heads // PIECES
    outs = [[] for _ in range(GROUPS)]
    moved = [[] for _ in range(GROUPS)]
    pending = [(group, piece) for group in range(GROUPS) for piece in range(PIECES)]

    def ask(after):
        group, piece = pending.pop(0)
        made = local[group]
        shape = struct((count, 2 * CHUNK, 128))
        after, small_here = lax.optimization_barrier((after, small))
        out, move = pl.pallas_call(
            functools.partial(queries_kernel, group, heads, piece * count, count, near),
            out_shape=[shape, shape],
            scratch_shapes=[pltpu.VMEM((8 + CHUNK, count * 128), F32)] * 2,
            compiler_params=params(16),
            cost_estimate=cost(4_000_000_000),
            name="queries",
        )(
            query_half,
            query_other,
            query_taps_half,
            halo_one,
            halo_two,
            small_here,
            small_other,
            *made[:3],
            *upper[:3],
            made[3],
            made[5],
        )
        outs[group].append(out)
        moved[group].append(move)
        return out

    moved_shape = struct((heads, 2 * CHUNK, 128))
    transit_codes = [None] * GROUPS

    def send_transit():
        return pl.pallas_call(
            code_kernel,
            out_shape=struct((8 * 128 + 16, 128), BF16),
            compiler_params=params(8),
            cost_estimate=cost(1_000_000),
            name="code",
        )(*transit)

    shifts = [heads * group for group in range(GROUPS)]
    passing = [[]] * GROUPS
    for level in range(shard_bits - 1):
        keeps = level < shard_bits - 2

        fanned = [[]] * GROUPS
        if keeps and level == 0:
            fanned = [fan(send_transit(), level)] * GROUPS
        elif keeps:
            fanned = [fan(x, level) for x in transit_codes]
        following = []
        for group in range(GROUPS):
            shapes = [code_shape]
            operands = list(arrived[group])
            if keeps:
                shapes += [struct(square), struct(square), code_shape]
                operands += fanned[group]
            waits = [after]
            if level == 0 and group == GROUPS - 1:
                waits += [query_other, gate_other]
            joined = pl.pallas_call(
                functools.partial(
                    join_kernel, level, len(arrived[group]), keeps, shifts[group], len(waits)
                ),
                in_specs=[pl.BlockSpec(memory_space=pl.ANY)] * len(waits)
                + [pl.BlockSpec(memory_space=pltpu.VMEM)] * (len(operands) + 2),
                out_shape=shapes,
                compiler_params=params(12),
                cost_estimate=cost(4_000_000_000),
                name="join",
            )(*waits, *operands, state[group], transit[group])
            after = joined[0]
            following.append(fan(joined[0], level + 1, not keeps))
            if keeps:
                state[group], transit[group], transit_codes[group] = joined[1:]
        arrivals = len(arrived[0])
        if level == 0:
            after, small_here = lax.optimization_barrier((after, small))
            operands = [x for group in range(GROUPS) for x in arrived[group]]
            operands += [query_half, query_other, query_taps_half, halo_one, halo_two]
            operands += [small_here, small_other, *upper[:3]]
            for group in sorted({group for group, _ in pending}):
                made = local[group]
                operands += [*made[:3], made[3], made[5]]
            for group in range(GROUPS):
                for out, move in zip(outs[group], moved[group]):
                    operands += [out, move]
            results = pl.pallas_call(
                functools.partial(
                    tail_kernel,
                    level,
                    32 + 16 * (near + 1 + level),
                    GROUPS,
                    heads,
                    count,
                    tuple(pending),
                    near,
                    arrivals,
                ),
                out_shape=[moved_shape] * (2 * GROUPS),
                scratch_shapes=[pltpu.VMEM((8 + CHUNK, count * 128), F32)] * 2
                + [pltpu.VMEM((count, 2 * CHUNK, 128), F32)] * (2 * len(pending)),
                compiler_params=params(24),
                cost_estimate=cost(1_000_000),
                name="tail",
            )(*operands)
            pending.clear()
            for group in range(GROUPS):
                outs[group], moved[group] = [results[2 * group]], [results[2 * group + 1]]
        else:
            for group in range(GROUPS):
                out, move = pl.pallas_call(
                    functools.partial(
                        absorb_kernel,
                        level,
                        32 + 16 * (near + 1 + level),
                        group,
                        heads,
                        arrivals,
                        len(passing[group]),
                        len(outs[group]),
                    ),
                    out_shape=[moved_shape, moved_shape],
                    compiler_params=params(12),
                    cost_estimate=cost(800_000_000),
                    name="absorb",
                )(
                    *arrived[group],
                    *passing[group],
                    small,
                    small_other,
                    *outs[group],
                    *moved[group],
                )
                outs[group], moved[group] = [out], [move]
        arrived = following
        passing = fanned
        shifts = [0] * GROUPS
    while pending:
        after = ask(after)

    level = max(shard_bits - 1, 0)
    stays = []
    comes = []
    for group in range(GROUPS):
        operands = [
            *arrived[group],
            small,
            small_other,
            gate_half,
            gate_other,
            gain,
            *outs[group],
            *moved[group],
        ]
        specs = [pl.BlockSpec(memory_space=pltpu.VMEM)] * len(operands)
        if group:
            operands = [stays[-1]] + operands
            specs = [pl.BlockSpec(memory_space=pl.ANY)] + specs
        stay, leave = pl.pallas_call(
            functools.partial(
                finish_kernel,
                level,
                32 + 16 * (near + 1 + level),
                group,
                heads,
                len(arrived[group]),
                len(outs[group]),
            ),
            in_specs=specs,
            out_shape=[struct((rows, lanes), BF16)] * 2,
            scratch_shapes=[pltpu.VMEM((heads, 2 * CHUNK, 128), F32)],
            compiler_params=params(12),
            cost_estimate=cost(1_000_000),
            name="finish",
        )(*operands)
        stays.append(stay)
        comes.append(lax.ppermute(leave, "seq", cores))
    return pl.pallas_call(
        swap_kernel,
        out_shape=struct((rows, width), BF16),
        compiler_params=params(4),
        name="swap",
    )(*stays, *comes)


def solution(mesh):
    placed = (
        P(("req", "seq"), None),
        P(("req", "seq"), None),
        P(("req", "seq"), None),
        P(),
        P(),
        P(),
        P(None, ("req", "seq")),
        P(None, ("req", "seq")),
        P(None, None, ("req", "seq")),
        P(("req", "seq"), None),
        P(),
    )
    return jax.shard_map(
        per_device, mesh=mesh, in_specs=placed, out_specs=P(("req", "seq"), None), check_vma=False
    )
```

```python
import functools

import jax
import jax.numpy as jnp
from jax import lax
from jax.experimental import pallas as pl
from jax.experimental.pallas import tpu as pltpu
from jax.sharding import PartitionSpec as P

HEAD_DIM = 128
CHUNK = 128
CODE = 125.0
F32 = jnp.float32
BF16 = jnp.bfloat16


def split(x):
    high = x.astype(BF16)
    return high, (x - high.astype(F32)).astype(BF16)


def dot(a, b):
    return jnp.dot(a, b, preferred_element_type=F32)


def wide(b):
    row = jnp.concatenate(b, axis=1)
    return jnp.concatenate([row, row], axis=0)


def mm(a, b):
    width = b[0].shape[1]
    if b[0].shape[0] <= 128 and (width > 128 or a[0].shape[0] <= 128):
        both = jnp.concatenate([b[0], b[0]], axis=0)
        return dot(jnp.concatenate(a, axis=1), both) + dot(a[0], b[1])
    out = dot(jnp.concatenate(a, axis=1), wide(b))
    return out[:, :width] + out[:, width:]


def mm_three(a, b):
    return (dot(a[1], b[0]) + dot(a[0], b[1])) + dot(a[0], b[0])


def silu(u):
    half = 0.5 * u
    return half + half * jnp.tanh(half)


def encode(state):
    top = jnp.max(jnp.abs(state), axis=0, keepdims=True)
    scale = (top * 1.02 + 1e-30).astype(BF16).astype(F32)
    grade = jnp.abs(state) / scale
    level = jnp.exp2(grade * (2.0 * CODE) - CODE)
    return jnp.where(state < 0, -level, level).astype(BF16), scale


def decode(code, scale):
    grade = jnp.log2(jnp.abs(code)) * (0.5 / CODE) + 0.5
    size = grade * scale
    return jnp.where(code < 0, -size, size)


def iotas(rows, columns):
    return (
        lax.broadcasted_iota(jnp.int32, (rows, columns), 0),
        lax.broadcasted_iota(jnp.int32, (rows, columns), 1),
    )


def place():
    index = lax.axis_index("seq")
    return index % 2, index // 2


def fill(scratch, own, other, before, core, chunk, first_lane, packed=False):
    lanes = scratch.shape[1]
    start = pl.multiple_of(core * 8 * HEAD_DIM + first_lane, 128)
    mine = own[:, first_lane : first_lane + lanes]
    theirs = other[:, first_lane : first_lane + lanes] if packed else other[:, pl.ds(start, lanes)]
    if before is None:
        last = jnp.where(core == 1, theirs[CHUNK - 16 :], mine[CHUNK - 16 :]).astype(F32)[13:16]
    else:
        one, two, first = before
        rows = one[:, pl.ds(start, lanes)].astype(F32) + two[:, pl.ds(start, lanes)].astype(F32)
        last = rows[first : first + 3]
    scratch[5:8, :] = last
    scratch[8 : 8 + CHUNK, :] = jnp.where(core == chunk, mine, theirs).astype(F32)


def conv(scratch, taps, columns, taps_columns):
    total = None
    for tap in range(4):
        part = taps[tap : tap + 1, taps_columns] * scratch[5 + tap : 5 + tap + CHUNK, columns]
        total = part if total is None else total + part
    return silu(total)


def unit(rows):
    return rows * lax.rsqrt(jnp.sum(rows * rows, axis=-1, keepdims=True) + 1e-6)


def token_row(own, other, row, core, chunk):
    return jnp.where(core == chunk, own[pl.ds(row, 1), :], other[pl.ds(row, 1), :])


def rows_table(rows):
    pad = -len(rows) % 8
    if pad:
        rows = rows + [jnp.zeros((pad, CHUNK), F32)]
    return jnp.concatenate(rows, axis=0)


def sums(own, other, base, parts, core):
    rows = [token_row(own, other, base + head, core, chunk) for head, chunk in parts]
    t, j = iotas(CHUNK, CHUNK)
    upper = (t <= j).astype(F32)
    run = jnp.dot(
        rows_table(rows), upper, preferred_element_type=F32, precision=lax.Precision.HIGHEST
    )
    return [run[i : i + 1] for i in range(len(parts))]


def invert(coupling, t, j):
    apart = t ^ j
    count = len(coupling)
    near = [split(jnp.where(apart < 8, -a, 0.0)) for a in coupling]
    eye = (t == j).astype(F32)
    squared = [mm(n, n) for n in near]
    grown = []
    fourth = []
    for i in range(count):
        base = eye + near[i][0].astype(F32) + near[i][1].astype(F32)
        left = split(jnp.concatenate([squared[i], base], axis=0))
        both = mm(left, split(squared[i]))
        fourth.append(both[:CHUNK])
        grown.append(base + both[CHUNK:])
    inverse = [
        grown[i] + mm(split(grown[i]), split(fourth[i])) for i in range(count)
    ]
    inverse = [split(x) for x in inverse]
    size = 8
    while size < CHUNK:
        starts = range(size, CHUNK, 2 * size)

        def pick(x):
            return jnp.concatenate([x[s : s + size] for s in starts], axis=0)

        zero = jnp.zeros((size, CHUNK), BF16)

        def spread(x):
            pieces = []
            for k in range(len(starts)):
                pieces += [zero, x[k * size : (k + 1) * size]]
            return jnp.concatenate(pieces, axis=0)

        def merge(x, rows):
            pieces = []
            for k, s in enumerate(starts):
                pieces += [x[s - size : s], rows[k * size : (k + 1) * size]]
            return jnp.concatenate(pieces, axis=0)

        mask = pick((apart >= size) & (apart < 2 * size))
        middle = []
        for i in range(count):
            lower = split(jnp.where(mask, pick(coupling[i]), 0.0))
            middle.append(split(mm(lower, inverse[i])))
        for i in range(count):
            high, low = inverse[i]
            rows = (pick(high), pick(low))
            change = mm(rows, tuple(spread(m) for m in middle[i]))
            fresh = split(rows[0].astype(F32) + rows[1].astype(F32) - change)
            inverse[i] = (merge(high, fresh[0]), merge(low, fresh[1]))
        size *= 2
    return inverse


def decay(column, row, t, j):
    return jnp.exp(jnp.where(t >= j, column - row, -1e30))


def prepare_kernel(query, key, value, gate, log_alpha, strength, mixture, query_taps, key_taps,
                   value_taps, gain, query_half, key_half, value_half, gate_half, query_taps_half,
                   key_taps_half, value_taps_half, halo, small, gain_out, message_out,
                   tails, sems):
    core, _ = place()
    rows, half = query_half.shape
    lanes = pl.ds(pl.multiple_of(core * half, half), half)
    copies = []

    def copy(source, target):
        made = pltpu.make_async_copy(source, target, sems.at[len(copies)])
        made.start()
        copies.append(made)

    for i, x in enumerate((query, key, value)):
        copy(x.at[rows - 16 : rows, :], tails.at[i])
    copy(log_alpha, small.at[0:16])
    copy(strength, small.at[16:32])
    copy(mixture, small.at[32 : small.shape[0]])
    for x, y in (
        (key, key_half),
        (value, value_half),
        (key_taps, key_taps_half),
        (value_taps, value_taps_half),
        (query_taps, query_taps_half),
        (query, query_half),
        (gate, gate_half),
    ):
        copy(x.at[:, lanes], y)
    copy(gain, gain_out)
    away = pl.ds(pl.multiple_of((1 - core) * half, half), half)
    copy(query.at[:, away], message_out.at[:, 0:half])
    copy(gate.at[:, away], message_out.at[:, half : 2 * half])
    for made in copies:
        made.wait()
    message = [tails[i][13:16, :].astype(F32) for i in range(3)]
    message.append(jnp.zeros((7, 2 * half), F32))
    halo[...] = jnp.concatenate(message, axis=0).astype(BF16)


def chunk_states(
    chunk,
    first,
    heads,
    key_taps,
    value_taps,
    small_own,
    small_other,
    key_cols_out,
    inverse_out,
    write_out,
    key_scratch,
    value_scratch,
):
    core, _ = place()
    t, j = iotas(CHUNK, CHUNK)
    base = 8 * core + first
    parts = [(head, chunk) for head in range(heads)]
    run = sums(small_own, small_other, base, parts, core)
    strengths = [
        token_row(small_own, small_other, 16 + base + head, core, chunk) for head in range(heads)
    ]
    columns = rows_table(run + strengths).T

    def lanes(head):
        return slice(head * 128, head * 128 + 128)

    def beta(head):
        return columns[:, heads + head : heads + head + 1]

    keys = [
        unit(conv(key_scratch, key_taps, lanes(head), lanes(first + head)))
        for head in range(heads)
    ]
    keys_t = [key.T for key in keys]
    coupling = []
    for head in range(heads):
        pair = split(keys_t[head])
        key_cols_out[head, 0] = pair[0]
        key_cols_out[head, 1] = pair[1]
        gram = mm(split(keys[head]), pair)
        ratio = decay(columns[:, head : head + 1], run[head], t, j)
        coupling.append(jnp.where(t > j, gram * ratio * beta(head), 0.0))
    inverse = invert(coupling, t, j)
    mixed = []
    for head in range(heads):
        inverse_out[head, 0] = inverse[head][0]
        inverse_out[head, 1] = inverse[head][1]
        last = run[head][:, CHUNK - 1 : CHUNK]
        tail = keys_t[head] * jnp.exp(last - run[head])
        mixed.append(mm(split(tail), inverse[head]))
    transits = []
    states = []
    for head in range(heads):
        value = conv(value_scratch, value_taps, lanes(head), lanes(first + head))
        grow = jnp.exp(columns[:, head : head + 1])
        write = jnp.concatenate([keys[head] * (beta(head) * grow), value * beta(head)], axis=1)
        write = split(write)
        write_out[head, 0] = write[0]
        write_out[head, 1] = write[1]
        last = run[head][:, CHUNK - 1 : CHUNK]
        both = mm(split(mixed[head]), write)
        transits.append(jnp.where(t == j, jnp.exp(last), 0.0) - both[:, :128])
        states.append(both[:, 128:])
    return transits, states


def upper_kernel(
    key_own,
    key_other,
    value_own,
    value_other,
    key_taps,
    value_taps,
    small_own,
    small_other,
    key_cols_out,
    inverse_out,
    write_out,
    transit_out,
    state_out,
    key_scratch,
    value_scratch,
):
    core, _ = place()
    fill(key_scratch, key_own, key_other, None, core, 1, 0)
    fill(value_scratch, value_own, value_other, None, core, 1, 0)
    transits, states = chunk_states(
        1,
        0,
        8,
        key_taps,
        value_taps,
        small_own,
        small_other,
        key_cols_out,
        inverse_out,
        write_out,
        key_scratch,
        value_scratch,
    )
    for head in range(8):
        transit_out[head] = transits[head]
        state_out[head] = states[head]


def lower_kernel(
    group,
    heads,
    key_own,
    key_other,
    value_own,
    value_other,
    key_taps,
    value_taps,
    halo_one,
    halo_two,
    small_own,
    small_other,
    upper_transit,
    upper_state,
    key_cols_out,
    inverse_out,
    write_out,
    first_state_out,
    state_out,
    transit_one_out,
    transit_out,
    code_out,
    key_scratch,
    value_scratch,
):
    core, _ = place()
    first = group * heads
    fill(key_scratch, key_own, key_other, (halo_one, halo_two, 3), core, 0, first * 128)
    fill(value_scratch, value_own, value_other, (halo_one, halo_two, 6), core, 0, first * 128)
    transits, states = chunk_states(
        0,
        first,
        heads,
        key_taps,
        value_taps,
        small_own,
        small_other,
        key_cols_out,
        inverse_out,
        write_out,
        key_scratch,
        value_scratch,
    )
    joined = []
    pairs = [split(upper_transit[first + head]) for head in range(heads)]
    for head in range(heads):
        joined.append(mm(pairs[head], split(states[head])) + upper_state[first + head])
    encode_all(joined, code_out)
    for head in range(heads):
        first_state_out[head] = states[head]
        transit_one_out[head] = transits[head]
        state_out[head] = joined[head]
        transit_out[head] = mm(pairs[head], split(transits[head]))


def queries_kernel(
    group,
    heads,
    first,
    count,
    near,
    query_own,
    query_other,
    query_taps,
    halo_one,
    halo_two,
    small_own,
    small_other,
    key_cols_one,
    inverse_one,
    write_one,
    key_cols_two,
    inverse_two,
    write_two,
    first_state,
    transit_one,
    out,
    moved,
    scratch_one,
    scratch_two,
):
    core, _ = place()
    start = group * heads + first
    fill(scratch_one, query_own, query_other, (halo_one, halo_two, 0), core, 0, start * 128, True)
    fill(scratch_two, query_own, query_other, None, core, 1, start * 128, True)
    t, j = iotas(CHUNK, CHUNK)
    apart = t ^ j
    parts = [(head, chunk) for head in range(count) for chunk in range(2)]
    base = 8 * core + start
    run = sums(small_own, small_other, base, parts, core)
    rows = list(run)
    for head, chunk in parts:
        for level in range(near + 1):
            row = 32 + 16 * level + base + head
            rows.append(token_row(small_own, small_other, row, core, chunk))
    columns = rows_table(rows).T

    def held(one, two, head, chunk):
        if chunk:
            return two[start + head, 0], two[start + head, 1]
        return one[first + head, 0], one[first + head, 1]

    mixings = []
    queries = []
    for i, (head, chunk) in enumerate(parts):
        lanes = slice(head * 128, head * 128 + 128)
        taps_lanes = slice((start + head) * 128, (start + head) * 128 + 128)
        scratch = scratch_two if chunk else scratch_one
        query = unit(conv(scratch, query_taps, lanes, taps_lanes))
        queries.append(query)
        ratio = decay(columns[:, i : i + 1], run[i], t, j)
        scores = mm(split(query), held(key_cols_one, key_cols_two, head, chunk)) * ratio
        mixings.append(mm(split(scores), held(inverse_one, inverse_two, head, chunk)))
    for i, (head, chunk) in enumerate(parts):
        at = len(parts) + i * (near + 1)
        level_mat = columns[:, at : at + 1]
        for level in range(1, near):
            weight = columns[:, at + level : at + level + 1]
            level_mat = jnp.where(apart >= 1 << (level - 1), weight, level_mat)
        high, low = held(write_one, write_two, head, chunk)
        within = mm(split(mixings[i] * level_mat), (high[:, 128:], low[:, 128:]))
        grow = jnp.exp(columns[:, i : i + 1])
        effective = grow * queries[i] - mm(split(mixings[i]), (high[:, :128], low[:, :128]))
        rows = slice(chunk * CHUNK, chunk * CHUNK + CHUNK)
        if chunk:
            pair = split(effective)
            weight = columns[:, at + near : at + near + 1]
            within = within + weight * mm(pair, split(first_state[first + head]))
            effective = mm(pair, split(transit_one[first + head]))
        out[head, rows, :] = within
        moved[head, rows, :] = effective


def asked_kernel(group, heads, first, count, near, after, *refs):
    queries_kernel(group, heads, first, count, near, *refs)


def received(refs, head):
    code = None
    scale = None
    for ref in refs:
        tail = ref.shape[0] - 16 + head
        part = ref[head * 128 : head * 128 + 128, :].astype(F32)
        row = ref[tail : tail + 1, :].astype(F32)
        code = part if code is None else code + part
        scale = row if scale is None else scale + row
    return decode(code, scale)


def pack_rows(scales):
    zeros = jnp.zeros((16 - len(scales), 128), F32)
    return jnp.concatenate(scales + [zeros], axis=0).astype(BF16)


def encode_all(values, code_out):
    scales = []
    for head, value in enumerate(values):
        code, scale = encode(value)
        code_out[head * 128 : head * 128 + 128, :] = code
        scales.append(scale)
    head = len(values)
    code_out[head * 128 : head * 128 + 16, :] = pack_rows(scales)


def join_kernel(level, arrivals, with_transit, shift, waits, *refs):
    refs = refs[waits:]
    state_in = refs[:arrivals]
    refs = refs[arrivals:]
    transit_in = ()
    if with_transit:
        transit_in = refs[:arrivals]
        refs = refs[arrivals:]
    state, transit, code_out = refs[:3]
    refs = refs[3:]
    heads = state.shape[0]
    _, node = place()
    upper = (node >> level) % 2 == 1
    if not with_transit:
        late = (node >> (level + 1)) % 2 == 1
        riding = late & jnp.logical_not(upper)
        upper = upper & jnp.logical_not(late)

        @pl.when(riding)
        def _():
            encode_all([transit[head] for head in range(heads)], code_out)

    @pl.when(upper)
    def _():
        fresh = []
        for head in range(heads):
            pair = split(transit[head])
            fresh.append(mm(pair, split(received(state_in, head))) + state[head])
            if with_transit:
                refs[0][head] = fresh[head]
                refs[1][head] = mm(pair, split(received(transit_in, shift + head)))
        encode_all(fresh, code_out)
        if with_transit:
            encode_all([refs[1][head] for head in range(heads)], refs[2])

    if with_transit:

        @pl.when(jnp.logical_not(upper))
        def _():
            encode_all([state[head] for head in range(heads)], code_out)
            for head in range(heads):
                refs[0][head] = state[head]
                refs[1][head] = transit[head]
            encode_all([transit[head] for head in range(heads)], refs[2])


def code_kernel(*refs):
    values = [ref[head] for ref in refs[:-1] for head in range(ref.shape[0])]
    encode_all(values, refs[-1])


def level_weight(own, other, row, core):
    rows = [token_row(own, other, row, core, chunk) for chunk in range(2)]
    columns = rows_table(rows).T
    return jnp.concatenate([columns[:, 0:1], columns[:, 1:2]], axis=0)


def absorb_kernel(level, weight_row, group, heads, arrivals, passed, pieces, *refs):
    state_in = refs[:arrivals]
    transit_in = refs[arrivals : arrivals + passed]
    refs = refs[arrivals + passed :]
    small_own, small_other = refs[:2]
    outs_in = refs[2 : 2 + pieces]
    moved_in = refs[2 + pieces : 2 + 2 * pieces]
    out, moved = refs[2 + 2 * pieces :]
    core, node = place()
    upper = (node >> level) % 2 == 1
    each = heads // pieces
    behind = jnp.bool_(False)
    if passed:
        behind = ((node >> (level - 1)) % 2 == 1) & ((node >> level) > 0)

        @pl.when(behind)
        def _():
            shift = group * heads if level == 1 else 0
            for head in range(heads):
                pair = split(moved_in[head // each][head % each])
                moved[head] = mm(pair, split(received(transit_in, shift + head)))

    @pl.when(jnp.logical_not(behind))
    def _():
        for head in range(heads):
            moved[head] = moved_in[head // each][head % each]

    @pl.when(upper)
    def _():
        for head in range(heads):
            pair = split(moved[head])
            row = weight_row + 8 * core + heads * group + head
            weight = level_weight(small_own, small_other, row, core)
            gain = mm(pair, split(received(state_in, head)))
            out[head] = outs_in[head // each][head % each] + weight * gain

    @pl.when(jnp.logical_not(upper))
    def _():
        for head in range(heads):
            out[head] = outs_in[head // each][head % each]


def tail_kernel(level, weight_row, groups, heads, count, pending, near, arrivals, *refs):
    state_in = [refs[g * arrivals : (g + 1) * arrivals] for g in range(groups)]
    refs = refs[groups * arrivals :]
    query_refs, refs = refs[:7], refs[7:]
    uppers, refs = refs[:3], refs[3:]
    lowers = {}
    for group in sorted({group for group, _ in pending}):
        lowers[group], refs = refs[:5], refs[5:]
    pieces = heads // count
    outs_in = {}
    for group in range(groups):
        for piece in range(pieces):
            if (group, piece) not in pending:
                outs_in[group, piece], refs = refs[:2], refs[2:]
    outs, refs = refs[: 2 * groups], refs[2 * groups :]
    scratch, refs = refs[:2], refs[2:]
    for group, piece in pending:
        temporary, refs = refs[:2], refs[2:]
        made = lowers[group]
        queries_kernel(
            group,
            heads,
            piece * count,
            count,
            near,
            *query_refs,
            *made[:3],
            *uppers,
            *made[3:],
            *temporary,
            *scratch,
        )
        outs_in[group, piece] = temporary
    for group in range(groups):
        absorb_kernel(
            level,
            weight_row,
            group,
            heads,
            arrivals,
            0,
            pieces,
            *state_in[group],
            *query_refs[5:7],
            *[outs_in[group, piece][0] for piece in range(pieces)],
            *[outs_in[group, piece][1] for piece in range(pieces)],
            outs[2 * group],
            outs[2 * group + 1],
        )


def finish_kernel(level, weight_row, group, heads, arrivals, pieces, *refs):
    refs = refs[min(group, 1) :]
    state_in = refs[:arrivals]
    refs = refs[arrivals:]
    small_own, small_other, gate_own, gate_other, gain = refs[:5]
    outs_in = refs[5 : 5 + pieces]
    moved_in = refs[5 + pieces : 5 + 2 * pieces]
    stay, leave, total = refs[5 + 2 * pieces :]
    core, node = place()
    upper = (node >> level) % 2 == 1
    each = heads // pieces

    def add(states, transits):
        for head in range(heads):
            found = split(received(states, head))
            if transits is not None:
                found = split(mm(split(received(transits, head)), found))
            row = weight_row + 8 * core + heads * group + head
            weight = level_weight(small_own, small_other, row, core)
            extra = mm_three(split(moved_in[head // each][head % each]), found)
            total[head] = outs_in[head // each][head % each] + weight * extra

    if level:
        through = (node >> (level - 1)) % 2 == 1
        far, close = state_in[: arrivals // 2], state_in[arrivals // 2 :]

        @pl.when(upper & through)
        def _():
            add(far, close)

        @pl.when(upper & jnp.logical_not(through))
        def _():
            add(close, None)

    else:

        @pl.when(upper)
        def _():
            add(state_in, None)

    @pl.when(jnp.logical_not(upper))
    def _():
        for head in range(heads):
            total[head] = outs_in[head // each][head % each]

    lanes_all = heads * 128
    at = gate_other.shape[1] // 2 + group * lanes_all
    gates = (
        gate_own[:, group * lanes_all : (group + 1) * lanes_all],
        gate_other[:, at : at + lanes_all],
    )
    for head in range(heads):
        lanes = slice(head * 128, head * 128 + 128)
        for gate, chunk, target in ((gates[0], core, stay), (gates[1], 1 - core, leave)):
            rows = pl.ds(pl.multiple_of(chunk * CHUNK, CHUNK), CHUNK)
            attended = total[head, rows, :]
            scale = lax.rsqrt(jnp.mean(attended * attended, axis=-1, keepdims=True) + 1e-5)
            gated = attended * scale * gain[...] * silu(gate[:, lanes].astype(F32))
            target[:, lanes] = gated.astype(BF16)


def swap_kernel(*refs):
    out, sems = refs[-2:]
    count = (len(refs) - 2) // 2
    core, _ = place()
    half = out.shape[1] // 2
    width = half // count
    copies = []
    for i in range(count):
        for j, side in ((i, core), (count + i, 1 - core)):
            start = pl.multiple_of(side * half + i * width, width)
            made = pltpu.make_async_copy(refs[j], out.at[:, pl.ds(start, width)], sems.at[j])
            made.start()
            copies.append(made)
    for made in copies:
        made.wait()


def struct(shape, dtype=F32):
    return jax.ShapeDtypeStruct(shape, dtype)


def params(mib):
    return pltpu.CompilerParams(vmem_limit_bytes=mib << 20)


def cost(flops):
    return pl.CostEstimate(flops=flops, bytes_accessed=1_000_000, transcendentals=0)


GROUPS = 2
PIECES = 1


def per_device(
    query_rows,
    key_rows,
    value_rows,
    query_taps,
    key_taps,
    value_taps,
    log_alpha,
    write_strength,
    tier_mixture,
    output_gate,
    norm_gain,
):
    rows, width = query_rows.shape
    half = width // 2
    size = lax.axis_size("seq")
    nodes = size // 2
    level_total = tier_mixture.shape[0]
    near = CHUNK.bit_length()
    heads = 8 // GROUPS
    lanes = heads * 128
    shard_bits = nodes.bit_length() - 1
    cores = [(i, i ^ 1) for i in range(size)]
    small_rows = 16 * (2 + level_total)
    key_other = lax.ppermute(key_rows, "seq", cores)
    value_other = lax.ppermute(value_rows, "seq", cores)
    half_shape = struct((rows, half), BF16)
    taps_shape = struct((4, half))
    (
        query_half,
        key_half,
        value_half,
        gate_half,
        query_taps_half,
        key_taps_half,
        value_taps_half,
        halo,
        small,
        gain,
        message,
    ) = pl.pallas_call(
        prepare_kernel,
        in_specs=[pl.BlockSpec(memory_space=pltpu.HBM)] * 11,
        out_shape=[half_shape] * 4
        + [taps_shape] * 3
        + [struct((16, width), BF16), struct((small_rows, 128)), struct((1, 128))]
        + [struct((rows, width), BF16)],
        scratch_shapes=[pltpu.VMEM((3, 16, width), BF16), pltpu.SemaphoreType.DMA((16,))],
        compiler_params=params(8),
        name="prepare",
    )(
        *[
            pltpu.with_memory_space_constraint(x, pltpu.HBM)
            for x in (
                query_rows,
                key_rows,
                value_rows,
                output_gate,
                log_alpha,
                write_strength,
                tier_mixture.reshape(level_total * 16, rows),
                query_taps,
                key_taps,
                value_taps,
                norm_gain.reshape(1, 128),
            )
        ]
    )
    small_other = lax.ppermute(small, "seq", cores)
    halo_one = lax.ppermute(halo, "seq", [(i, i + 1) for i in range(1, size - 1, 2)])
    halo_two = lax.ppermute(halo, "seq", [(i, i + 2) for i in range(1, size - 1, 2)])

    def fan(value, level, riders=False):
        span = 1 << level
        results = []
        for offset in reversed(range(span)):
            route = []
            for low in range(0, nodes, 2 * span):
                hops = [(low + span - 1, low + span + offset)]
                if riders and 2 * offset < span:
                    middle = low + span + span // 2
                    hops.append((middle - 1, middle + offset))
                for source, target in hops:
                    route += [(2 * source + c, 2 * target + c) for c in range(2)]
            results.append(lax.ppermute(value, "seq", route))
        return results

    def held(count):
        return [
            struct((count, 2, 128, 128), BF16),
            struct((count, 2, 128, 128), BF16),
            struct((count, 2, 128, 256), BF16),
        ]

    square = (heads, 128, 128)
    code_shape = struct((heads * 128 + 16, 128), BF16)
    upper = pl.pallas_call(
        upper_kernel,
        out_shape=held(8) + [struct((8, 128, 128))] * 2,
        scratch_shapes=[pltpu.VMEM((8 + CHUNK, half), F32)] * 2,
        compiler_params=params(24),
        cost_estimate=cost(4_000_000_000),
        name="upper",
    )(
        key_half,
        key_other,
        value_half,
        value_other,
        key_taps_half,
        value_taps_half,
        small,
        small_other,
    )
    local = []
    arrived = []
    after = upper[4]
    for group in range(GROUPS):
        after, halo_first = lax.optimization_barrier((after, halo_one))
        made = pl.pallas_call(
            functools.partial(lower_kernel, group, heads),
            out_shape=held(heads)
            + [struct(square), struct(square), struct(square), struct(square), code_shape],
            scratch_shapes=[pltpu.VMEM((8 + CHUNK, lanes), F32)] * 2,
            compiler_params=params(24),
            cost_estimate=cost(2_500_000_000),
            name="lower",
        )(
            key_half,
            key_other,
            value_half,
            value_other,
            key_taps_half,
            value_taps_half,
            halo_first,
            halo_two,
            small,
            small_other,
            upper[3],
            upper[4],
        )
        local.append(made)
        after = made[7]
        arrived.append(fan(made[7], 0) if shard_bits else [])

    _, late_message = lax.optimization_barrier((local[0][7], message))
    query_other = gate_other = lax.ppermute(late_message, "seq", cores)
    state = [x[4] for x in local]
    transit = [x[6] for x in local]
    count = heads // PIECES
    outs = [[] for _ in range(GROUPS)]
    moved = [[] for _ in range(GROUPS)]
    pending = [(group, piece) for group in range(GROUPS) for piece in range(PIECES)]

    def ask(after):
        group, piece = pending.pop(0)
        made = local[group]
        shape = struct((count, 2 * CHUNK, 128))
        operands = [
            query_half,
            query_other,
            query_taps_half,
            halo_one,
            halo_two,
            small,
            small_other,
            *made[:3],
            *upper[:3],
            made[3],
            made[5],
        ]
        out, move = pl.pallas_call(
            functools.partial(asked_kernel, group, heads, piece * count, count, near),
            in_specs=[pl.BlockSpec(memory_space=pl.ANY)]
            + [pl.BlockSpec(memory_space=pltpu.VMEM)] * len(operands),
            out_shape=[shape, shape],
            scratch_shapes=[pltpu.VMEM((8 + CHUNK, count * 128), F32)] * 2,
            compiler_params=params(16),
            cost_estimate=cost(1_000_000),
            name="queries",
        )(after, *operands)
        outs[group].append(out)
        moved[group].append(move)
        return out

    moved_shape = struct((heads, 2 * CHUNK, 128))
    transit_codes = [None] * GROUPS

    def send_transit():
        return pl.pallas_call(
            code_kernel,
            out_shape=struct((8 * 128 + 16, 128), BF16),
            compiler_params=params(8),
            cost_estimate=cost(1_000_000),
            name="code",
        )(*transit)

    shifts = [heads * group for group in range(GROUPS)]
    passing = [[]] * GROUPS
    for level in range(shard_bits - 1):
        keeps = level < shard_bits - 2

        fanned = [[]] * GROUPS
        if keeps and level == 0:
            fanned = [fan(send_transit(), level)] * GROUPS
        elif keeps:
            fanned = [fan(x, level) for x in transit_codes]
        following = []
        for group in range(GROUPS):
            shapes = [code_shape]
            operands = list(arrived[group])
            if keeps:
                shapes += [struct(square), struct(square), code_shape]
                operands += fanned[group]
            waits = [after]
            if level == 0 and group == GROUPS - 1:
                waits += [query_other]
            joined = pl.pallas_call(
                functools.partial(
                    join_kernel, level, len(arrived[group]), keeps, shifts[group], len(waits)
                ),
                in_specs=[pl.BlockSpec(memory_space=pl.ANY)] * len(waits)
                + [pl.BlockSpec(memory_space=pltpu.VMEM)] * (len(operands) + 2),
                out_shape=shapes,
                compiler_params=params(12),
                cost_estimate=cost(4_000_000_000),
                name="join",
            )(*waits, *operands, state[group], transit[group])
            after = joined[0]
            following.append(fan(joined[0], level + 1, not keeps))
            if keeps:
                state[group], transit[group], transit_codes[group] = joined[1:]
        arrivals = len(arrived[0])
        if level == 0:
            after, small_here = lax.optimization_barrier((after, small))
            operands = [x for group in range(GROUPS) for x in arrived[group]]
            operands += [query_half, query_other, query_taps_half, halo_one, halo_two]
            operands += [small_here, small_other, *upper[:3]]
            for group in sorted({group for group, _ in pending}):
                made = local[group]
                operands += [*made[:3], made[3], made[5]]
            for group in range(GROUPS):
                for out, move in zip(outs[group], moved[group]):
                    operands += [out, move]
            results = pl.pallas_call(
                functools.partial(
                    tail_kernel,
                    level,
                    32 + 16 * (near + 1 + level),
                    GROUPS,
                    heads,
                    count,
                    tuple(pending),
                    near,
                    arrivals,
                ),
                out_shape=[moved_shape] * (2 * GROUPS),
                scratch_shapes=[pltpu.VMEM((8 + CHUNK, count * 128), F32)] * 2
                + [pltpu.VMEM((count, 2 * CHUNK, 128), F32)] * (2 * len(pending)),
                compiler_params=params(24),
                cost_estimate=cost(1_000_000),
                name="tail",
            )(*operands)
            pending.clear()
            for group in range(GROUPS):
                outs[group], moved[group] = [results[2 * group]], [results[2 * group + 1]]
        else:
            for group in range(GROUPS):
                out, move = pl.pallas_call(
                    functools.partial(
                        absorb_kernel,
                        level,
                        32 + 16 * (near + 1 + level),
                        group,
                        heads,
                        arrivals,
                        len(passing[group]),
                        len(outs[group]),
                    ),
                    out_shape=[moved_shape, moved_shape],
                    compiler_params=params(12),
                    cost_estimate=cost(800_000_000),
                    name="absorb",
                )(
                    *arrived[group],
                    *passing[group],
                    small,
                    small_other,
                    *outs[group],
                    *moved[group],
                )
                outs[group], moved[group] = [out], [move]
        arrived = following
        passing = fanned
        shifts = [0] * GROUPS
    while pending:
        after = ask(after)

    level = max(shard_bits - 1, 0)
    stays = []
    comes = []
    for group in range(GROUPS):
        operands = [
            *arrived[group],
            small,
            small_other,
            gate_half,
            gate_other,
            gain,
            *outs[group],
            *moved[group],
        ]
        specs = [pl.BlockSpec(memory_space=pltpu.VMEM)] * len(operands)
        if group:
            operands = [stays[-1]] + operands
            specs = [pl.BlockSpec(memory_space=pl.ANY)] + specs
        stay, leave = pl.pallas_call(
            functools.partial(
                finish_kernel,
                level,
                32 + 16 * (near + 1 + level),
                group,
                heads,
                len(arrived[group]),
                len(outs[group]),
            ),
            in_specs=specs,
            out_shape=[struct((rows, lanes), BF16)] * 2,
            scratch_shapes=[pltpu.VMEM((heads, 2 * CHUNK, 128), F32)],
            compiler_params=params(12),
            cost_estimate=cost(1_000_000),
            name="finish",
        )(*operands)
        stays.append(stay)
        comes.append(lax.ppermute(leave, "seq", cores))
    return pl.pallas_call(
        swap_kernel,
        in_specs=[pl.BlockSpec(memory_space=pltpu.VMEM)] * (2 * GROUPS),
        out_specs=pl.BlockSpec(memory_space=pltpu.HBM),
        out_shape=struct((rows, width), BF16),
        scratch_shapes=[pltpu.SemaphoreType.DMA((2 * GROUPS,))],
        compiler_params=params(4),
        name="swap",
    )(*stays, *comes)


def solution(mesh):
    placed = (
        P(("req", "seq"), None),
        P(("req", "seq"), None),
        P(("req", "seq"), None),
        P(),
        P(),
        P(),
        P(None, ("req", "seq")),
        P(None, ("req", "seq")),
        P(None, None, ("req", "seq")),
        P(("req", "seq"), None),
        P(),
    )
    return jax.shard_map(
        per_device, mesh=mesh, in_specs=placed, out_specs=P(("req", "seq"), None), check_vma=False
    )
```

```python
import functools

import jax
import jax.numpy as jnp
from jax import lax
from jax.experimental import pallas as pl
from jax.experimental.pallas import tpu as pltpu
from jax.sharding import PartitionSpec as P

HEAD_DIM = 128
CHUNK = 128
CODE = 125.0
F32 = jnp.float32
BF16 = jnp.bfloat16


def split(x):
    high = x.astype(BF16)
    return high, (x - high.astype(F32)).astype(BF16)


def dot(a, b):
    return jnp.dot(a, b, preferred_element_type=F32)


def wide(b):
    row = jnp.concatenate(b, axis=1)
    return jnp.concatenate([row, row], axis=0)


def mm(a, b):
    width = b[0].shape[1]
    if b[0].shape[0] <= 128 and (width > 128 or a[0].shape[0] <= 128):
        both = jnp.concatenate([b[0], b[0]], axis=0)
        return dot(jnp.concatenate(a, axis=1), both) + dot(a[0], b[1])
    out = dot(jnp.concatenate(a, axis=1), wide(b))
    return out[:, :width] + out[:, width:]


def mm_three(a, b):
    return (dot(a[1], b[0]) + dot(a[0], b[1])) + dot(a[0], b[0])


def silu(u):
    half = 0.5 * u
    return half + half * jnp.tanh(half)


def encode(state):
    top = jnp.max(jnp.abs(state), axis=0, keepdims=True)
    scale = (top * 1.02 + 1e-30).astype(BF16).astype(F32)
    grade = jnp.abs(state) / scale
    level = jnp.exp2(grade * (2.0 * CODE) - CODE)
    return jnp.where(state < 0, -level, level).astype(BF16), scale


def decode(code, scale):
    grade = jnp.log2(jnp.abs(code)) * (0.5 / CODE) + 0.5
    size = grade * scale
    return jnp.where(code < 0, -size, size)


def iotas(rows, columns):
    return (
        lax.broadcasted_iota(jnp.int32, (rows, columns), 0),
        lax.broadcasted_iota(jnp.int32, (rows, columns), 1),
    )


def place():
    index = lax.axis_index("seq")
    return index % 2, index // 2


def fill(scratch, own, other, before, core, chunk, first_lane, packed=False):
    lanes = scratch.shape[1]
    start = pl.multiple_of(core * 8 * HEAD_DIM + first_lane, 128)
    mine = own[:, first_lane : first_lane + lanes]
    theirs = other[:, first_lane : first_lane + lanes] if packed else other[:, pl.ds(start, lanes)]
    if before is None:
        last = jnp.where(core == 1, theirs[CHUNK - 16 :], mine[CHUNK - 16 :]).astype(F32)[13:16]
    else:
        one, two, first = before
        rows = one[:, pl.ds(start, lanes)].astype(F32) + two[:, pl.ds(start, lanes)].astype(F32)
        last = rows[first : first + 3]
    scratch[5:8, :] = last
    scratch[8 : 8 + CHUNK, :] = jnp.where(core == chunk, mine, theirs).astype(F32)


def conv(scratch, taps, columns, taps_columns):
    total = None
    for tap in range(4):
        part = taps[tap : tap + 1, taps_columns] * scratch[5 + tap : 5 + tap + CHUNK, columns]
        total = part if total is None else total + part
    return silu(total)


def unit(rows):
    return rows * lax.rsqrt(jnp.sum(rows * rows, axis=-1, keepdims=True) + 1e-6)


def token_row(own, other, row, core, chunk):
    return jnp.where(core == chunk, own[pl.ds(row, 1), :], other[pl.ds(row, 1), :])


def rows_table(rows):
    pad = -len(rows) % 8
    if pad:
        rows = rows + [jnp.zeros((pad, CHUNK), F32)]
    return jnp.concatenate(rows, axis=0)


def sums(own, other, base, parts, core):
    rows = [token_row(own, other, base + head, core, chunk) for head, chunk in parts]
    t, j = iotas(CHUNK, CHUNK)
    upper = (t <= j).astype(F32)
    run = jnp.dot(
        rows_table(rows), upper, preferred_element_type=F32, precision=lax.Precision.HIGHEST
    )
    return [run[i : i + 1] for i in range(len(parts))]


def invert(coupling, t, j):
    apart = t ^ j
    count = len(coupling)
    near = [split(jnp.where(apart < 8, -a, 0.0)) for a in coupling]
    eye = (t == j).astype(F32)
    squared = [mm(n, n) for n in near]
    grown = []
    fourth = []
    for i in range(count):
        base = eye + near[i][0].astype(F32) + near[i][1].astype(F32)
        left = split(jnp.concatenate([squared[i], base], axis=0))
        both = mm(left, split(squared[i]))
        fourth.append(both[:CHUNK])
        grown.append(base + both[CHUNK:])
    inverse = [
        grown[i] + mm(split(grown[i]), split(fourth[i])) for i in range(count)
    ]
    inverse = [split(x) for x in inverse]
    size = 8
    while size < CHUNK:
        starts = range(size, CHUNK, 2 * size)

        def pick(x):
            return jnp.concatenate([x[s : s + size] for s in starts], axis=0)

        zero = jnp.zeros((size, CHUNK), BF16)

        def spread(x):
            pieces = []
            for k in range(len(starts)):
                pieces += [zero, x[k * size : (k + 1) * size]]
            return jnp.concatenate(pieces, axis=0)

        def merge(x, rows):
            pieces = []
            for k, s in enumerate(starts):
                pieces += [x[s - size : s], rows[k * size : (k + 1) * size]]
            return jnp.concatenate(pieces, axis=0)

        mask = pick((apart >= size) & (apart < 2 * size))
        middle = []
        for i in range(count):
            lower = split(jnp.where(mask, pick(coupling[i]), 0.0))
            middle.append(split(mm(lower, inverse[i])))
        for i in range(count):
            high, low = inverse[i]
            rows = (pick(high), pick(low))
            change = mm(rows, tuple(spread(m) for m in middle[i]))
            fresh = split(rows[0].astype(F32) + rows[1].astype(F32) - change)
            inverse[i] = (merge(high, fresh[0]), merge(low, fresh[1]))
        size *= 2
    return inverse


def decay(column, row, t, j):
    return jnp.exp(jnp.where(t >= j, column - row, -1e30))


def prepare_kernel(query, key, value, gate, log_alpha, strength, mixture, query_taps, key_taps,
                   value_taps, gain, query_half, key_half, value_half, gate_half, query_taps_half,
                   key_taps_half, value_taps_half, halo, small, gain_out, message_out,
                   tails, sems):
    core, _ = place()
    rows, half = query_half.shape
    lanes = pl.ds(pl.multiple_of(core * half, half), half)
    copies = []

    def copy(source, target):
        made = pltpu.make_async_copy(source, target, sems.at[len(copies)])
        made.start()
        copies.append(made)

    for i, x in enumerate((query, key, value)):
        copy(x.at[rows - 16 : rows, :], tails.at[i])
    copy(log_alpha, small.at[0:16])
    copy(strength, small.at[16:32])
    copy(mixture, small.at[32 : small.shape[0]])
    for x, y in (
        (key, key_half),
        (value, value_half),
        (key_taps, key_taps_half),
        (value_taps, value_taps_half),
        (query_taps, query_taps_half),
        (query, query_half),
        (gate, gate_half),
    ):
        copy(x.at[:, lanes], y)
    copy(gain, gain_out)
    away = pl.ds(pl.multiple_of((1 - core) * half, half), half)
    copy(query.at[:, away], message_out.at[:, 0:half])
    copy(gate.at[:, away], message_out.at[:, half : 2 * half])
    for made in copies:
        made.wait()
    message = [tails[i][13:16, :].astype(F32) for i in range(3)]
    message.append(jnp.zeros((7, 2 * half), F32))
    halo[...] = jnp.concatenate(message, axis=0).astype(BF16)


def chunk_states(
    chunk,
    first,
    heads,
    key_taps,
    value_taps,
    small_own,
    small_other,
    key_cols_out,
    inverse_out,
    write_out,
    key_scratch,
    value_scratch,
):
    core, _ = place()
    t, j = iotas(CHUNK, CHUNK)
    base = 8 * core + first
    parts = [(head, chunk) for head in range(heads)]
    run = sums(small_own, small_other, base, parts, core)
    strengths = [
        token_row(small_own, small_other, 16 + base + head, core, chunk) for head in range(heads)
    ]
    columns = rows_table(run + strengths).T

    def lanes(head):
        return slice(head * 128, head * 128 + 128)

    def beta(head):
        return columns[:, heads + head : heads + head + 1]

    keys = [
        unit(conv(key_scratch, key_taps, lanes(head), lanes(first + head)))
        for head in range(heads)
    ]
    keys_t = [key.T for key in keys]
    coupling = []
    for head in range(heads):
        pair = split(keys_t[head])
        key_cols_out[head, 0] = pair[0]
        key_cols_out[head, 1] = pair[1]
        gram = mm(split(keys[head]), pair)
        ratio = decay(columns[:, head : head + 1], run[head], t, j)
        coupling.append(jnp.where(t > j, gram * ratio * beta(head), 0.0))
    inverse = invert(coupling, t, j)
    mixed = []
    for head in range(heads):
        inverse_out[head, 0] = inverse[head][0]
        inverse_out[head, 1] = inverse[head][1]
        last = run[head][:, CHUNK - 1 : CHUNK]
        tail = keys_t[head] * jnp.exp(last - run[head])
        mixed.append(mm(split(tail), inverse[head]))
    transits = []
    states = []
    for head in range(heads):
        value = conv(value_scratch, value_taps, lanes(head), lanes(first + head))
        grow = jnp.exp(columns[:, head : head + 1])
        write = jnp.concatenate([keys[head] * (beta(head) * grow), value * beta(head)], axis=1)
        write = split(write)
        write_out[head, 0] = write[0]
        write_out[head, 1] = write[1]
        last = run[head][:, CHUNK - 1 : CHUNK]
        both = mm(split(mixed[head]), write)
        transits.append(jnp.where(t == j, jnp.exp(last), 0.0) - both[:, :128])
        states.append(both[:, 128:])
    return transits, states


def upper_kernel(
    key_own,
    key_other,
    value_own,
    value_other,
    key_taps,
    value_taps,
    small_own,
    small_other,
    key_cols_out,
    inverse_out,
    write_out,
    transit_out,
    state_out,
    key_scratch,
    value_scratch,
):
    core, _ = place()
    fill(key_scratch, key_own, key_other, None, core, 1, 0)
    fill(value_scratch, value_own, value_other, None, core, 1, 0)
    transits, states = chunk_states(
        1,
        0,
        8,
        key_taps,
        value_taps,
        small_own,
        small_other,
        key_cols_out,
        inverse_out,
        write_out,
        key_scratch,
        value_scratch,
    )
    for head in range(8):
        transit_out[head] = transits[head]
        state_out[head] = states[head]


def lower_kernel(
    group,
    heads,
    key_own,
    key_other,
    value_own,
    value_other,
    key_taps,
    value_taps,
    halo_one,
    halo_two,
    small_own,
    small_other,
    upper_transit,
    upper_state,
    key_cols_out,
    inverse_out,
    write_out,
    first_state_out,
    state_out,
    transit_one_out,
    transit_out,
    code_out,
    key_scratch,
    value_scratch,
):
    core, _ = place()
    first = group * heads
    fill(key_scratch, key_own, key_other, (halo_one, halo_two, 3), core, 0, first * 128)
    fill(value_scratch, value_own, value_other, (halo_one, halo_two, 6), core, 0, first * 128)
    transits, states = chunk_states(
        0,
        first,
        heads,
        key_taps,
        value_taps,
        small_own,
        small_other,
        key_cols_out,
        inverse_out,
        write_out,
        key_scratch,
        value_scratch,
    )
    joined = []
    pairs = [split(upper_transit[first + head]) for head in range(heads)]
    for head in range(heads):
        joined.append(mm(pairs[head], split(states[head])) + upper_state[first + head])
    encode_all(joined, code_out)
    for head in range(heads):
        first_state_out[head] = states[head]
        transit_one_out[head] = transits[head]
        state_out[head] = joined[head]
        transit_out[head] = mm(pairs[head], split(transits[head]))


def queries_kernel(
    group,
    heads,
    first,
    count,
    near,
    query_own,
    query_other,
    query_taps,
    halo_one,
    halo_two,
    small_own,
    small_other,
    key_cols_one,
    inverse_one,
    write_one,
    key_cols_two,
    inverse_two,
    write_two,
    first_state,
    transit_one,
    out,
    moved,
    scratch_one,
    scratch_two,
):
    core, _ = place()
    start = group * heads + first
    fill(scratch_one, query_own, query_other, (halo_one, halo_two, 0), core, 0, start * 128, True)
    fill(scratch_two, query_own, query_other, None, core, 1, start * 128, True)
    t, j = iotas(CHUNK, CHUNK)
    apart = t ^ j
    parts = [(head, chunk) for head in range(count) for chunk in range(2)]
    base = 8 * core + start
    run = sums(small_own, small_other, base, parts, core)
    rows = list(run)
    for head, chunk in parts:
        for level in range(near + 1):
            row = 32 + 16 * level + base + head
            rows.append(token_row(small_own, small_other, row, core, chunk))
    columns = rows_table(rows).T

    def held(one, two, head, chunk):
        if chunk:
            return two[start + head, 0], two[start + head, 1]
        return one[first + head, 0], one[first + head, 1]

    mixings = []
    queries = []
    for i, (head, chunk) in enumerate(parts):
        lanes = slice(head * 128, head * 128 + 128)
        taps_lanes = slice((start + head) * 128, (start + head) * 128 + 128)
        scratch = scratch_two if chunk else scratch_one
        query = unit(conv(scratch, query_taps, lanes, taps_lanes))
        queries.append(query)
        ratio = decay(columns[:, i : i + 1], run[i], t, j)
        scores = mm(split(query), held(key_cols_one, key_cols_two, head, chunk)) * ratio
        mixings.append(mm(split(scores), held(inverse_one, inverse_two, head, chunk)))
    for i, (head, chunk) in enumerate(parts):
        at = len(parts) + i * (near + 1)
        level_mat = columns[:, at : at + 1]
        for level in range(1, near):
            weight = columns[:, at + level : at + level + 1]
            level_mat = jnp.where(apart >= 1 << (level - 1), weight, level_mat)
        high, low = held(write_one, write_two, head, chunk)
        within = mm(split(mixings[i] * level_mat), (high[:, 128:], low[:, 128:]))
        grow = jnp.exp(columns[:, i : i + 1])
        effective = grow * queries[i] - mm(split(mixings[i]), (high[:, :128], low[:, :128]))
        rows = slice(chunk * CHUNK, chunk * CHUNK + CHUNK)
        if chunk:
            pair = split(effective)
            weight = columns[:, at + near : at + near + 1]
            within = within + weight * mm(pair, split(first_state[first + head]))
            effective = mm(pair, split(transit_one[first + head]))
        out[head, rows, :] = within
        moved[head, rows, :] = effective


def asked_kernel(group, heads, first, count, near, after, *refs):
    queries_kernel(group, heads, first, count, near, *refs)


def received(refs, head):
    code = None
    scale = None
    for ref in refs:
        tail = ref.shape[0] - 16 + head
        part = ref[head * 128 : head * 128 + 128, :].astype(F32)
        row = ref[tail : tail + 1, :].astype(F32)
        code = part if code is None else code + part
        scale = row if scale is None else scale + row
    return decode(code, scale)


def pack_rows(scales):
    zeros = jnp.zeros((16 - len(scales), 128), F32)
    return jnp.concatenate(scales + [zeros], axis=0).astype(BF16)


def encode_all(values, code_out):
    scales = []
    for head, value in enumerate(values):
        code, scale = encode(value)
        code_out[head * 128 : head * 128 + 128, :] = code
        scales.append(scale)
    head = len(values)
    code_out[head * 128 : head * 128 + 16, :] = pack_rows(scales)


def join_kernel(level, arrivals, with_transit, shift, waits, *refs):
    refs = refs[waits:]
    state_in = refs[:arrivals]
    refs = refs[arrivals:]
    transit_in = ()
    if with_transit:
        transit_in = refs[:arrivals]
        refs = refs[arrivals:]
    state, transit, code_out = refs[:3]
    refs = refs[3:]
    heads = state.shape[0]
    _, node = place()
    upper = (node >> level) % 2 == 1
    if not with_transit:
        late = (node >> (level + 1)) % 2 == 1
        riding = late & jnp.logical_not(upper)
        upper = upper & jnp.logical_not(late)

        @pl.when(riding)
        def _():
            encode_all([transit[head] for head in range(heads)], code_out)

    @pl.when(upper)
    def _():
        fresh = []
        for head in range(heads):
            pair = split(transit[head])
            fresh.append(mm(pair, split(received(state_in, head))) + state[head])
            if with_transit:
                refs[0][head] = fresh[head]
                refs[1][head] = mm(pair, split(received(transit_in, shift + head)))
        encode_all(fresh, code_out)
        if with_transit:
            encode_all([refs[1][head] for head in range(heads)], refs[2])

    if with_transit:

        @pl.when(jnp.logical_not(upper))
        def _():
            encode_all([state[head] for head in range(heads)], code_out)
            for head in range(heads):
                refs[0][head] = state[head]
                refs[1][head] = transit[head]
            encode_all([transit[head] for head in range(heads)], refs[2])


def code_kernel(*refs):
    values = [ref[head] for ref in refs[:-1] for head in range(ref.shape[0])]
    encode_all(values, refs[-1])


def level_weight(own, other, row, core):
    rows = [token_row(own, other, row, core, chunk) for chunk in range(2)]
    columns = rows_table(rows).T
    return jnp.concatenate([columns[:, 0:1], columns[:, 1:2]], axis=0)


def absorb_kernel(level, weight_row, group, heads, arrivals, passed, pieces, *refs):
    state_in = refs[:arrivals]
    transit_in = refs[arrivals : arrivals + passed]
    refs = refs[arrivals + passed :]
    small_own, small_other = refs[:2]
    outs_in = refs[2 : 2 + pieces]
    moved_in = refs[2 + pieces : 2 + 2 * pieces]
    out, moved = refs[2 + 2 * pieces :]
    core, node = place()
    upper = (node >> level) % 2 == 1
    each = heads // pieces
    behind = jnp.bool_(False)
    if passed:
        behind = ((node >> (level - 1)) % 2 == 1) & ((node >> level) > 0)

        @pl.when(behind)
        def _():
            shift = group * heads if level == 1 else 0
            for head in range(heads):
                pair = split(moved_in[head // each][head % each])
                moved[head] = mm(pair, split(received(transit_in, shift + head)))

    @pl.when(jnp.logical_not(behind))
    def _():
        for head in range(heads):
            moved[head] = moved_in[head // each][head % each]

    @pl.when(upper)
    def _():
        for head in range(heads):
            pair = split(moved[head])
            row = weight_row + 8 * core + heads * group + head
            weight = level_weight(small_own, small_other, row, core)
            gain = mm(pair, split(received(state_in, head)))
            out[head] = outs_in[head // each][head % each] + weight * gain

    @pl.when(jnp.logical_not(upper))
    def _():
        for head in range(heads):
            out[head] = outs_in[head // each][head % each]


def tail_kernel(level, weight_row, groups, heads, count, pending, near, arrivals, *refs):
    state_in = [refs[g * arrivals : (g + 1) * arrivals] for g in range(groups)]
    refs = refs[groups * arrivals :]
    query_refs, refs = refs[:7], refs[7:]
    uppers, refs = refs[:3], refs[3:]
    lowers = {}
    for group in sorted({group for group, _ in pending}):
        lowers[group], refs = refs[:5], refs[5:]
    pieces = heads // count
    outs_in = {}
    for group in range(groups):
        for piece in range(pieces):
            if (group, piece) not in pending:
                outs_in[group, piece], refs = refs[:2], refs[2:]
    outs, refs = refs[: 2 * groups], refs[2 * groups :]
    scratch, refs = refs[:2], refs[2:]
    for group, piece in pending:
        temporary, refs = refs[:2], refs[2:]
        made = lowers[group]
        queries_kernel(
            group,
            heads,
            piece * count,
            count,
            near,
            *query_refs,
            *made[:3],
            *uppers,
            *made[3:],
            *temporary,
            *scratch,
        )
        outs_in[group, piece] = temporary
    for group in range(groups):
        absorb_kernel(
            level,
            weight_row,
            group,
            heads,
            arrivals,
            0,
            pieces,
            *state_in[group],
            *query_refs[5:7],
            *[outs_in[group, piece][0] for piece in range(pieces)],
            *[outs_in[group, piece][1] for piece in range(pieces)],
            outs[2 * group],
            outs[2 * group + 1],
        )


def finish_kernel(level, weight_row, group, heads, arrivals, pieces, *refs):
    refs = refs[min(group, 1) :]
    state_in = refs[:arrivals]
    refs = refs[arrivals:]
    small_own, small_other, gate_own, gate_other, gain = refs[:5]
    outs_in = refs[5 : 5 + pieces]
    moved_in = refs[5 + pieces : 5 + 2 * pieces]
    stay, leave, total = refs[5 + 2 * pieces :]
    core, node = place()
    upper = (node >> level) % 2 == 1
    each = heads // pieces

    def add(states, transits):
        for head in range(heads):
            found = split(received(states, head))
            if transits is not None:
                found = split(mm(split(received(transits, head)), found))
            row = weight_row + 8 * core + heads * group + head
            weight = level_weight(small_own, small_other, row, core)
            extra = mm_three(split(moved_in[head // each][head % each]), found)
            total[head] = outs_in[head // each][head % each] + weight * extra

    if level:
        through = (node >> (level - 1)) % 2 == 1
        far, close = state_in[: arrivals // 2], state_in[arrivals // 2 :]

        @pl.when(upper & through)
        def _():
            add(far, close)

        @pl.when(upper & jnp.logical_not(through))
        def _():
            add(close, None)

    else:

        @pl.when(upper)
        def _():
            add(state_in, None)

    @pl.when(jnp.logical_not(upper))
    def _():
        for head in range(heads):
            total[head] = outs_in[head // each][head % each]

    lanes_all = heads * 128
    at = gate_other.shape[1] // 2 + group * lanes_all
    gates = (
        gate_own[:, group * lanes_all : (group + 1) * lanes_all],
        gate_other[:, at : at + lanes_all],
    )
    for head in range(heads):
        lanes = slice(head * 128, head * 128 + 128)
        for gate, chunk, target in ((gates[0], core, stay), (gates[1], 1 - core, leave)):
            rows = pl.ds(pl.multiple_of(chunk * CHUNK, CHUNK), CHUNK)
            attended = total[head, rows, :]
            scale = lax.rsqrt(jnp.mean(attended * attended, axis=-1, keepdims=True) + 1e-5)
            gated = attended * scale * gain[...] * silu(gate[:, lanes].astype(F32))
            target[:, lanes] = gated.astype(BF16)


def swap_kernel(*refs):
    out, sems = refs[-2:]
    count = (len(refs) - 2) // 2
    core, _ = place()
    half = out.shape[1] // 2
    width = half // count
    copies = []
    for i in range(count):
        for j, side in ((i, core), (count + i, 1 - core)):
            start = pl.multiple_of(side * half + i * width, width)
            made = pltpu.make_async_copy(refs[j], out.at[:, pl.ds(start, width)], sems.at[j])
            made.start()
            copies.append(made)
    for made in copies:
        made.wait()


def struct(shape, dtype=F32):
    return jax.ShapeDtypeStruct(shape, dtype)


def params(mib):
    return pltpu.CompilerParams(vmem_limit_bytes=mib << 20)


def cost(flops):
    return pl.CostEstimate(flops=flops, bytes_accessed=1_000_000, transcendentals=0)


GROUPS = 2
PIECES = 2


def per_device(
    query_rows,
    key_rows,
    value_rows,
    query_taps,
    key_taps,
    value_taps,
    log_alpha,
    write_strength,
    tier_mixture,
    output_gate,
    norm_gain,
):
    rows, width = query_rows.shape
    half = width // 2
    size = lax.axis_size("seq")
    nodes = size // 2
    level_total = tier_mixture.shape[0]
    near = CHUNK.bit_length()
    heads = 8 // GROUPS
    lanes = heads * 128
    shard_bits = nodes.bit_length() - 1
    cores = [(i, i ^ 1) for i in range(size)]
    small_rows = 16 * (2 + level_total)
    key_other = lax.ppermute(key_rows, "seq", cores)
    value_other = lax.ppermute(value_rows, "seq", cores)
    half_shape = struct((rows, half), BF16)
    taps_shape = struct((4, half))
    (
        query_half,
        key_half,
        value_half,
        gate_half,
        query_taps_half,
        key_taps_half,
        value_taps_half,
        halo,
        small,
        gain,
        message,
    ) = pl.pallas_call(
        prepare_kernel,
        in_specs=[pl.BlockSpec(memory_space=pltpu.HBM)] * 11,
        out_shape=[half_shape] * 4
        + [taps_shape] * 3
        + [struct((16, width), BF16), struct((small_rows, 128)), struct((1, 128))]
        + [struct((rows, width), BF16)],
        scratch_shapes=[pltpu.VMEM((3, 16, width), BF16), pltpu.SemaphoreType.DMA((16,))],
        compiler_params=params(8),
        name="prepare",
    )(
        *[
            pltpu.with_memory_space_constraint(x, pltpu.HBM)
            for x in (
                query_rows,
                key_rows,
                value_rows,
                output_gate,
                log_alpha,
                write_strength,
                tier_mixture.reshape(level_total * 16, rows),
                query_taps,
                key_taps,
                value_taps,
                norm_gain.reshape(1, 128),
            )
        ]
    )
    small_other = lax.ppermute(small, "seq", cores)
    halo_one = lax.ppermute(halo, "seq", [(i, i + 1) for i in range(1, size - 1, 2)])
    halo_two = lax.ppermute(halo, "seq", [(i, i + 2) for i in range(1, size - 1, 2)])

    def fan(value, level, riders=False):
        span = 1 << level
        results = []
        for offset in reversed(range(span)):
            route = []
            for low in range(0, nodes, 2 * span):
                hops = [(low + span - 1, low + span + offset)]
                if riders and 2 * offset < span:
                    middle = low + span + span // 2
                    hops.append((middle - 1, middle + offset))
                for source, target in hops:
                    route += [(2 * source + c, 2 * target + c) for c in range(2)]
            results.append(lax.ppermute(value, "seq", route))
        return results

    def held(count):
        return [
            struct((count, 2, 128, 128), BF16),
            struct((count, 2, 128, 128), BF16),
            struct((count, 2, 128, 256), BF16),
        ]

    square = (heads, 128, 128)
    code_shape = struct((heads * 128 + 16, 128), BF16)
    upper = pl.pallas_call(
        upper_kernel,
        out_shape=held(8) + [struct((8, 128, 128))] * 2,
        scratch_shapes=[pltpu.VMEM((8 + CHUNK, half), F32)] * 2,
        compiler_params=params(24),
        cost_estimate=cost(4_000_000_000),
        name="upper",
    )(
        key_half,
        key_other,
        value_half,
        value_other,
        key_taps_half,
        value_taps_half,
        small,
        small_other,
    )
    local = []
    arrived = []
    after = upper[4]
    for group in range(GROUPS):
        after, halo_first = lax.optimization_barrier((after, halo_one))
        made = pl.pallas_call(
            functools.partial(lower_kernel, group, heads),
            out_shape=held(heads)
            + [struct(square), struct(square), struct(square), struct(square), code_shape],
            scratch_shapes=[pltpu.VMEM((8 + CHUNK, lanes), F32)] * 2,
            compiler_params=params(24),
            cost_estimate=cost(2_500_000_000),
            name="lower",
        )(
            key_half,
            key_other,
            value_half,
            value_other,
            key_taps_half,
            value_taps_half,
            halo_first,
            halo_two,
            small,
            small_other,
            upper[3],
            upper[4],
        )
        local.append(made)
        after = made[7]
        arrived.append(fan(made[7], 0) if shard_bits else [])

    _, late_message = lax.optimization_barrier((local[0][7], message))
    query_other = gate_other = lax.ppermute(late_message, "seq", cores)
    state = [x[4] for x in local]
    transit = [x[6] for x in local]
    count = heads // PIECES
    outs = [[] for _ in range(GROUPS)]
    moved = [[] for _ in range(GROUPS)]
    pending = [(group, piece) for group in range(GROUPS) for piece in range(PIECES)]

    def ask(after):
        group, piece = pending.pop(0)
        made = local[group]
        shape = struct((count, 2 * CHUNK, 128))
        operands = [
            query_half,
            query_other,
            query_taps_half,
            halo_one,
            halo_two,
            small,
            small_other,
            *made[:3],
            *upper[:3],
            made[3],
            made[5],
        ]
        out, move = pl.pallas_call(
            functools.partial(asked_kernel, group, heads, piece * count, count, near),
            in_specs=[pl.BlockSpec(memory_space=pl.ANY)]
            + [pl.BlockSpec(memory_space=pltpu.VMEM)] * len(operands),
            out_shape=[shape, shape],
            scratch_shapes=[pltpu.VMEM((8 + CHUNK, count * 128), F32)] * 2,
            compiler_params=params(16),
            cost_estimate=cost(1_000_000),
            name="queries",
        )(after, *operands)
        outs[group].append(out)
        moved[group].append(move)
        return out

    moved_shape = struct((heads, 2 * CHUNK, 128))
    transit_codes = [None] * GROUPS

    def send_transit():
        return pl.pallas_call(
            code_kernel,
            out_shape=struct((8 * 128 + 16, 128), BF16),
            compiler_params=params(8),
            cost_estimate=cost(1_000_000),
            name="code",
        )(*transit)

    shifts = [heads * group for group in range(GROUPS)]
    passing = [[]] * GROUPS
    for level in range(shard_bits - 1):
        keeps = level < shard_bits - 2

        fanned = [[]] * GROUPS
        if keeps and level == 0:
            fanned = [fan(send_transit(), level)] * GROUPS
        elif keeps:
            fanned = [fan(x, level) for x in transit_codes]
        following = []
        for group in range(GROUPS):
            shapes = [code_shape]
            operands = list(arrived[group])
            if keeps:
                shapes += [struct(square), struct(square), code_shape]
                operands += fanned[group]
            if level == 0 and group == 1:
                after = ask(after)
            waits = [after]
            if level == 0 and group == GROUPS - 1:
                waits += [query_other]
            joined = pl.pallas_call(
                functools.partial(
                    join_kernel, level, len(arrived[group]), keeps, shifts[group], len(waits)
                ),
                in_specs=[pl.BlockSpec(memory_space=pl.ANY)] * len(waits)
                + [pl.BlockSpec(memory_space=pltpu.VMEM)] * (len(operands) + 2),
                out_shape=shapes,
                compiler_params=params(12),
                cost_estimate=cost(4_000_000_000),
                name="join",
            )(*waits, *operands, state[group], transit[group])
            after = joined[0]
            following.append(fan(joined[0], level + 1, not keeps))
            if keeps:
                state[group], transit[group], transit_codes[group] = joined[1:]
        arrivals = len(arrived[0])
        if level == 0:
            after, small_here = lax.optimization_barrier((after, small))
            operands = [x for group in range(GROUPS) for x in arrived[group]]
            operands += [query_half, query_other, query_taps_half, halo_one, halo_two]
            operands += [small_here, small_other, *upper[:3]]
            for group in sorted({group for group, _ in pending}):
                made = local[group]
                operands += [*made[:3], made[3], made[5]]
            for group in range(GROUPS):
                for out, move in zip(outs[group], moved[group]):
                    operands += [out, move]
            results = pl.pallas_call(
                functools.partial(
                    tail_kernel,
                    level,
                    32 + 16 * (near + 1 + level),
                    GROUPS,
                    heads,
                    count,
                    tuple(pending),
                    near,
                    arrivals,
                ),
                out_shape=[moved_shape] * (2 * GROUPS),
                scratch_shapes=[pltpu.VMEM((8 + CHUNK, count * 128), F32)] * 2
                + [pltpu.VMEM((count, 2 * CHUNK, 128), F32)] * (2 * len(pending)),
                compiler_params=params(24),
                cost_estimate=cost(1_000_000),
                name="tail",
            )(*operands)
            pending.clear()
            for group in range(GROUPS):
                outs[group], moved[group] = [results[2 * group]], [results[2 * group + 1]]
        else:
            for group in range(GROUPS):
                out, move = pl.pallas_call(
                    functools.partial(
                        absorb_kernel,
                        level,
                        32 + 16 * (near + 1 + level),
                        group,
                        heads,
                        arrivals,
                        len(passing[group]),
                        len(outs[group]),
                    ),
                    out_shape=[moved_shape, moved_shape],
                    compiler_params=params(12),
                    cost_estimate=cost(800_000_000),
                    name="absorb",
                )(
                    *arrived[group],
                    *passing[group],
                    small,
                    small_other,
                    *outs[group],
                    *moved[group],
                )
                outs[group], moved[group] = [out], [move]
        arrived = following
        passing = fanned
        shifts = [0] * GROUPS
    while pending:
        after = ask(after)

    level = max(shard_bits - 1, 0)
    stays = []
    comes = []
    for group in range(GROUPS):
        operands = [
            *arrived[group],
            small,
            small_other,
            gate_half,
            gate_other,
            gain,
            *outs[group],
            *moved[group],
        ]
        specs = [pl.BlockSpec(memory_space=pltpu.VMEM)] * len(operands)
        if group:
            operands = [stays[-1]] + operands
            specs = [pl.BlockSpec(memory_space=pl.ANY)] + specs
        stay, leave = pl.pallas_call(
            functools.partial(
                finish_kernel,
                level,
                32 + 16 * (near + 1 + level),
                group,
                heads,
                len(arrived[group]),
                len(outs[group]),
            ),
            in_specs=specs,
            out_shape=[struct((rows, lanes), BF16)] * 2,
            scratch_shapes=[pltpu.VMEM((heads, 2 * CHUNK, 128), F32)],
            compiler_params=params(12),
            cost_estimate=cost(1_000_000),
            name="finish",
        )(*operands)
        stays.append(stay)
        comes.append(lax.ppermute(leave, "seq", cores))
    return pl.pallas_call(
        swap_kernel,
        in_specs=[pl.BlockSpec(memory_space=pltpu.VMEM)] * (2 * GROUPS),
        out_specs=pl.BlockSpec(memory_space=pltpu.HBM),
        out_shape=struct((rows, width), BF16),
        scratch_shapes=[pltpu.SemaphoreType.DMA((2 * GROUPS,))],
        compiler_params=params(4),
        name="swap",
    )(*stays, *comes)


def solution(mesh):
    placed = (
        P(("req", "seq"), None),
        P(("req", "seq"), None),
        P(("req", "seq"), None),
        P(),
        P(),
        P(),
        P(None, ("req", "seq")),
        P(None, ("req", "seq")),
        P(None, None, ("req", "seq")),
        P(("req", "seq"), None),
        P(),
    )
    return jax.shard_map(
        per_device, mesh=mesh, in_specs=placed, out_specs=P(("req", "seq"), None), check_vma=False
    )
```

```python
import functools

import jax
import jax.numpy as jnp
from jax import lax
from jax.experimental import pallas as pl
from jax.experimental.pallas import tpu as pltpu
from jax.sharding import PartitionSpec as P

HEAD_DIM = 128
CHUNK = 128
CODE = 125.0
F32 = jnp.float32
BF16 = jnp.bfloat16


def split(x):
    high = x.astype(BF16)
    return high, (x - high.astype(F32)).astype(BF16)


def dot(a, b):
    return jnp.dot(a, b, preferred_element_type=F32)


def wide(b):
    row = jnp.concatenate(b, axis=1)
    return jnp.concatenate([row, row], axis=0)


def mm(a, b):
    width = b[0].shape[1]
    if b[0].shape[0] <= 128 and (width > 128 or a[0].shape[0] <= 128):
        both = jnp.concatenate([b[0], b[0]], axis=0)
        return dot(jnp.concatenate(a, axis=1), both) + dot(a[0], b[1])
    out = dot(jnp.concatenate(a, axis=1), wide(b))
    return out[:, :width] + out[:, width:]


def mm_three(a, b):
    return (dot(a[1], b[0]) + dot(a[0], b[1])) + dot(a[0], b[0])


def silu(u):
    half = 0.5 * u
    return half + half * jnp.tanh(half)


def encode(state):
    top = jnp.max(jnp.abs(state), axis=0, keepdims=True)
    scale = (top * 1.02 + 1e-30).astype(BF16).astype(F32)
    grade = jnp.abs(state) / scale
    level = jnp.exp2(grade * (2.0 * CODE) - CODE)
    return jnp.where(state < 0, -level, level).astype(BF16), scale


def decode(code, scale):
    grade = jnp.log2(jnp.abs(code)) * (0.5 / CODE) + 0.5
    size = grade * scale
    return jnp.where(code < 0, -size, size)


def iotas(rows, columns):
    return (
        lax.broadcasted_iota(jnp.int32, (rows, columns), 0),
        lax.broadcasted_iota(jnp.int32, (rows, columns), 1),
    )


def place():
    index = lax.axis_index("seq")
    return index % 2, index // 2


def fill(scratch, own, other, before, core, chunk, first_lane, packed=False):
    lanes = scratch.shape[1]
    start = pl.multiple_of(core * 8 * HEAD_DIM + first_lane, 128)
    mine = own[:, first_lane : first_lane + lanes]
    theirs = other[:, first_lane : first_lane + lanes] if packed else other[:, pl.ds(start, lanes)]
    if before is None:
        last = jnp.where(core == 1, theirs[CHUNK - 16 :], mine[CHUNK - 16 :]).astype(F32)[13:16]
    else:
        one, two, first = before
        rows = one[:, pl.ds(start, lanes)].astype(F32) + two[:, pl.ds(start, lanes)].astype(F32)
        last = rows[first : first + 3]
    scratch[5:8, :] = last
    scratch[8 : 8 + CHUNK, :] = jnp.where(core == chunk, mine, theirs).astype(F32)


def conv(scratch, taps, columns, taps_columns):
    total = None
    for tap in range(4):
        part = taps[tap : tap + 1, taps_columns] * scratch[5 + tap : 5 + tap + CHUNK, columns]
        total = part if total is None else total + part
    return silu(total)


def unit(rows):
    return rows * lax.rsqrt(jnp.sum(rows * rows, axis=-1, keepdims=True) + 1e-6)


def token_row(own, other, row, core, chunk):
    return jnp.where(core == chunk, own[pl.ds(row, 1), :], other[pl.ds(row, 1), :])


def rows_table(rows):
    pad = -len(rows) % 8
    if pad:
        rows = rows + [jnp.zeros((pad, CHUNK), F32)]
    return jnp.concatenate(rows, axis=0)


def sums(own, other, base, parts, core):
    rows = [token_row(own, other, base + head, core, chunk) for head, chunk in parts]
    t, j = iotas(CHUNK, CHUNK)
    upper = (t <= j).astype(F32)
    run = jnp.dot(
        rows_table(rows), upper, preferred_element_type=F32, precision=lax.Precision.HIGHEST
    )
    return [run[i : i + 1] for i in range(len(parts))]


def invert(coupling, t, j):
    apart = t ^ j
    count = len(coupling)
    near = [split(jnp.where(apart < 16, -a, 0.0)) for a in coupling]
    eye = (t == j).astype(F32)
    powers = [split(mm(n, n)) for n in near]
    grown = [eye + n[0].astype(F32) + n[1].astype(F32) for n in near]
    for _ in range(2):
        for i in range(count):
            base = split(grown[i])
            left = tuple(jnp.concatenate([powers[i][k], base[k]], axis=0) for k in range(2))
            both = mm(left, powers[i])
            powers[i] = split(both[:CHUNK])
            grown[i] = grown[i] + both[CHUNK:]
    inverse = [split(grown[i] + mm(split(grown[i]), powers[i])) for i in range(count)]
    size = 16
    while size < CHUNK:
        starts = range(size, CHUNK, 2 * size)

        def pick(x):
            return jnp.concatenate([x[s : s + size] for s in starts], axis=0)

        zero = jnp.zeros((size, CHUNK), BF16)

        def spread(x):
            pieces = []
            for k in range(len(starts)):
                pieces += [zero, x[k * size : (k + 1) * size]]
            return jnp.concatenate(pieces, axis=0)

        def merge(x, rows):
            pieces = []
            for k, s in enumerate(starts):
                pieces += [x[s - size : s], rows[k * size : (k + 1) * size]]
            return jnp.concatenate(pieces, axis=0)

        mask = pick((apart >= size) & (apart < 2 * size))
        middle = []
        for i in range(count):
            lower = split(jnp.where(mask, pick(coupling[i]), 0.0))
            middle.append(split(mm(lower, inverse[i])))
        for i in range(count):
            high, low = inverse[i]
            rows = (pick(high), pick(low))
            change = mm(rows, tuple(spread(m) for m in middle[i]))
            fresh = split(rows[0].astype(F32) + rows[1].astype(F32) - change)
            inverse[i] = (merge(high, fresh[0]), merge(low, fresh[1]))
        size *= 2
    return inverse


def decay(column, row, t, j):
    return jnp.exp(jnp.where(t >= j, column - row, -1e30))


def prepare_kernel(query, key, value, gate, log_alpha, strength, mixture, query_taps, key_taps,
                   value_taps, gain, query_half, key_half, value_half, gate_half, query_taps_half,
                   key_taps_half, value_taps_half, halo, small, gain_out, message_out,
                   tails, sems):
    core, _ = place()
    rows, half = query_half.shape
    lanes = pl.ds(pl.multiple_of(core * half, half), half)
    copies = []

    def copy(source, target):
        made = pltpu.make_async_copy(source, target, sems.at[len(copies)])
        made.start()
        copies.append(made)

    for i, x in enumerate((query, key, value)):
        copy(x.at[rows - 16 : rows, :], tails.at[i])
    copy(log_alpha, small.at[0:16])
    copy(strength, small.at[16:32])
    copy(mixture, small.at[32 : small.shape[0]])
    for x, y in (
        (key, key_half),
        (value, value_half),
        (key_taps, key_taps_half),
        (value_taps, value_taps_half),
        (query_taps, query_taps_half),
        (query, query_half),
        (gate, gate_half),
    ):
        copy(x.at[:, lanes], y)
    copy(gain, gain_out)
    away = pl.ds(pl.multiple_of((1 - core) * half, half), half)
    copy(query.at[:, away], message_out.at[:, 0:half])
    copy(gate.at[:, away], message_out.at[:, half : 2 * half])
    for made in copies:
        made.wait()
    message = [tails[i][13:16, :].astype(F32) for i in range(3)]
    message.append(jnp.zeros((7, 2 * half), F32))
    halo[...] = jnp.concatenate(message, axis=0).astype(BF16)


def chunk_states(
    chunk,
    first,
    heads,
    key_taps,
    value_taps,
    small_own,
    small_other,
    key_cols_out,
    inverse_out,
    write_out,
    key_scratch,
    value_scratch,
):
    core, _ = place()
    t, j = iotas(CHUNK, CHUNK)
    base = 8 * core + first
    parts = [(head, chunk) for head in range(heads)]
    run = sums(small_own, small_other, base, parts, core)
    strengths = [
        token_row(small_own, small_other, 16 + base + head, core, chunk) for head in range(heads)
    ]
    columns = rows_table(run + strengths).T

    def lanes(head):
        return slice(head * 128, head * 128 + 128)

    def beta(head):
        return columns[:, heads + head : heads + head + 1]

    keys = [
        unit(conv(key_scratch, key_taps, lanes(head), lanes(first + head)))
        for head in range(heads)
    ]
    keys_t = [key.T for key in keys]
    coupling = []
    for head in range(heads):
        pair = split(keys_t[head])
        key_cols_out[head, 0] = pair[0]
        key_cols_out[head, 1] = pair[1]
        gram = mm(split(keys[head]), pair)
        ratio = decay(columns[:, head : head + 1], run[head], t, j)
        coupling.append(jnp.where(t > j, gram * ratio * beta(head), 0.0))
    inverse = invert(coupling, t, j)
    mixed = []
    for head in range(heads):
        inverse_out[head, 0] = inverse[head][0]
        inverse_out[head, 1] = inverse[head][1]
        last = run[head][:, CHUNK - 1 : CHUNK]
        tail = keys_t[head] * jnp.exp(last - run[head])
        mixed.append(mm(split(tail), inverse[head]))
    transits = []
    states = []
    for head in range(heads):
        value = conv(value_scratch, value_taps, lanes(head), lanes(first + head))
        grow = jnp.exp(columns[:, head : head + 1])
        write = jnp.concatenate([keys[head] * (beta(head) * grow), value * beta(head)], axis=1)
        write = split(write)
        write_out[head, 0] = write[0]
        write_out[head, 1] = write[1]
        last = run[head][:, CHUNK - 1 : CHUNK]
        both = mm(split(mixed[head]), write)
        transits.append(jnp.where(t == j, jnp.exp(last), 0.0) - both[:, :128])
        states.append(both[:, 128:])
    return transits, states


def upper_kernel(
    key_own,
    key_other,
    value_own,
    value_other,
    key_taps,
    value_taps,
    small_own,
    small_other,
    key_cols_out,
    inverse_out,
    write_out,
    transit_out,
    state_out,
    key_scratch,
    value_scratch,
):
    core, _ = place()
    fill(key_scratch, key_own, key_other, None, core, 1, 0)
    fill(value_scratch, value_own, value_other, None, core, 1, 0)
    transits, states = chunk_states(
        1,
        0,
        8,
        key_taps,
        value_taps,
        small_own,
        small_other,
        key_cols_out,
        inverse_out,
        write_out,
        key_scratch,
        value_scratch,
    )
    for head in range(8):
        transit_out[head] = transits[head]
        state_out[head] = states[head]


def lower_kernel(
    group,
    heads,
    key_own,
    key_other,
    value_own,
    value_other,
    key_taps,
    value_taps,
    halo_one,
    halo_two,
    small_own,
    small_other,
    upper_transit,
    upper_state,
    key_cols_out,
    inverse_out,
    write_out,
    first_state_out,
    state_out,
    transit_one_out,
    transit_out,
    code_out,
    key_scratch,
    value_scratch,
):
    core, _ = place()
    first = group * heads
    fill(key_scratch, key_own, key_other, (halo_one, halo_two, 3), core, 0, first * 128)
    fill(value_scratch, value_own, value_other, (halo_one, halo_two, 6), core, 0, first * 128)
    transits, states = chunk_states(
        0,
        first,
        heads,
        key_taps,
        value_taps,
        small_own,
        small_other,
        key_cols_out,
        inverse_out,
        write_out,
        key_scratch,
        value_scratch,
    )
    joined = []
    pairs = [split(upper_transit[first + head]) for head in range(heads)]
    for head in range(heads):
        joined.append(mm(pairs[head], split(states[head])) + upper_state[first + head])
    encode_all(joined, code_out)
    for head in range(heads):
        first_state_out[head] = states[head]
        transit_one_out[head] = transits[head]
        state_out[head] = joined[head]
        transit_out[head] = mm(pairs[head], split(transits[head]))


def queries_kernel(
    group,
    heads,
    first,
    count,
    near,
    query_own,
    query_other,
    query_taps,
    halo_one,
    halo_two,
    small_own,
    small_other,
    key_cols_one,
    inverse_one,
    write_one,
    key_cols_two,
    inverse_two,
    write_two,
    first_state,
    transit_one,
    out,
    moved,
    scratch_one,
    scratch_two,
):
    core, _ = place()
    start = group * heads + first
    fill(scratch_one, query_own, query_other, (halo_one, halo_two, 0), core, 0, start * 128, True)
    fill(scratch_two, query_own, query_other, None, core, 1, start * 128, True)
    t, j = iotas(CHUNK, CHUNK)
    apart = t ^ j
    parts = [(head, chunk) for head in range(count) for chunk in range(2)]
    base = 8 * core + start
    run = sums(small_own, small_other, base, parts, core)
    rows = list(run)
    for head, chunk in parts:
        for level in range(near + 1):
            row = 32 + 16 * level + base + head
            rows.append(token_row(small_own, small_other, row, core, chunk))
    columns = rows_table(rows).T

    def held(one, two, head, chunk):
        if chunk:
            return two[start + head, 0], two[start + head, 1]
        return one[first + head, 0], one[first + head, 1]

    mixings = []
    queries = []
    for i, (head, chunk) in enumerate(parts):
        lanes = slice(head * 128, head * 128 + 128)
        taps_lanes = slice((start + head) * 128, (start + head) * 128 + 128)
        scratch = scratch_two if chunk else scratch_one
        query = unit(conv(scratch, query_taps, lanes, taps_lanes))
        queries.append(query)
        ratio = decay(columns[:, i : i + 1], run[i], t, j)
        scores = mm(split(query), held(key_cols_one, key_cols_two, head, chunk)) * ratio
        mixings.append(mm(split(scores), held(inverse_one, inverse_two, head, chunk)))
    for i, (head, chunk) in enumerate(parts):
        at = len(parts) + i * (near + 1)
        level_mat = columns[:, at : at + 1]
        for level in range(1, near):
            weight = columns[:, at + level : at + level + 1]
            level_mat = jnp.where(apart >= 1 << (level - 1), weight, level_mat)
        high, low = held(write_one, write_two, head, chunk)
        within = mm(split(mixings[i] * level_mat), (high[:, 128:], low[:, 128:]))
        grow = jnp.exp(columns[:, i : i + 1])
        effective = grow * queries[i] - mm(split(mixings[i]), (high[:, :128], low[:, :128]))
        rows = slice(chunk * CHUNK, chunk * CHUNK + CHUNK)
        if chunk:
            pair = split(effective)
            weight = columns[:, at + near : at + near + 1]
            within = within + weight * mm(pair, split(first_state[first + head]))
            effective = mm(pair, split(transit_one[first + head]))
        out[head, rows, :] = within
        moved[head, rows, :] = effective


def asked_kernel(group, heads, first, count, near, after, *refs):
    queries_kernel(group, heads, first, count, near, *refs)


def received(refs, head):
    code = None
    scale = None
    for ref in refs:
        tail = ref.shape[0] - 16 + head
        part = ref[head * 128 : head * 128 + 128, :].astype(F32)
        row = ref[tail : tail + 1, :].astype(F32)
        code = part if code is None else code + part
        scale = row if scale is None else scale + row
    return decode(code, scale)


def pack_rows(scales):
    zeros = jnp.zeros((16 - len(scales), 128), F32)
    return jnp.concatenate(scales + [zeros], axis=0).astype(BF16)


def encode_all(values, code_out):
    scales = []
    for head, value in enumerate(values):
        code, scale = encode(value)
        code_out[head * 128 : head * 128 + 128, :] = code
        scales.append(scale)
    head = len(values)
    code_out[head * 128 : head * 128 + 16, :] = pack_rows(scales)


def join_kernel(level, arrivals, with_transit, shift, waits, *refs):
    refs = refs[waits:]
    state_in = refs[:arrivals]
    refs = refs[arrivals:]
    transit_in = ()
    if with_transit:
        transit_in = refs[:arrivals]
        refs = refs[arrivals:]
    state, transit, code_out = refs[:3]
    refs = refs[3:]
    heads = state.shape[0]
    _, node = place()
    upper = (node >> level) % 2 == 1
    if not with_transit:
        late = (node >> (level + 1)) % 2 == 1
        riding = late & jnp.logical_not(upper)
        upper = upper & jnp.logical_not(late)

        @pl.when(riding)
        def _():
            encode_all([transit[head] for head in range(heads)], code_out)

    @pl.when(upper)
    def _():
        fresh = []
        for head in range(heads):
            pair = split(transit[head])
            fresh.append(mm(pair, split(received(state_in, head))) + state[head])
            if with_transit:
                refs[0][head] = fresh[head]
                refs[1][head] = mm(pair, split(received(transit_in, shift + head)))
        encode_all(fresh, code_out)
        if with_transit:
            encode_all([refs[1][head] for head in range(heads)], refs[2])

    if with_transit:

        @pl.when(jnp.logical_not(upper))
        def _():
            encode_all([state[head] for head in range(heads)], code_out)
            for head in range(heads):
                refs[0][head] = state[head]
                refs[1][head] = transit[head]
            encode_all([transit[head] for head in range(heads)], refs[2])


def code_kernel(*refs):
    values = [ref[head] for ref in refs[:-1] for head in range(ref.shape[0])]
    encode_all(values, refs[-1])


def level_weight(own, other, row, core):
    rows = [token_row(own, other, row, core, chunk) for chunk in range(2)]
    columns = rows_table(rows).T
    return jnp.concatenate([columns[:, 0:1], columns[:, 1:2]], axis=0)


def absorb_kernel(level, weight_row, group, heads, arrivals, passed, pieces, *refs):
    state_in = refs[:arrivals]
    transit_in = refs[arrivals : arrivals + passed]
    refs = refs[arrivals + passed :]
    small_own, small_other = refs[:2]
    outs_in = refs[2 : 2 + pieces]
    moved_in = refs[2 + pieces : 2 + 2 * pieces]
    out, moved = refs[2 + 2 * pieces :]
    core, node = place()
    upper = (node >> level) % 2 == 1
    each = heads // pieces
    behind = jnp.bool_(False)
    if passed:
        behind = ((node >> (level - 1)) % 2 == 1) & ((node >> level) > 0)

        @pl.when(behind)
        def _():
            shift = group * heads if level == 1 else 0
            for head in range(heads):
                pair = split(moved_in[head // each][head % each])
                moved[head] = mm(pair, split(received(transit_in, shift + head)))

    @pl.when(jnp.logical_not(behind))
    def _():
        for head in range(heads):
            moved[head] = moved_in[head // each][head % each]

    @pl.when(upper)
    def _():
        for head in range(heads):
            pair = split(moved[head])
            row = weight_row + 8 * core + heads * group + head
            weight = level_weight(small_own, small_other, row, core)
            gain = mm(pair, split(received(state_in, head)))
            out[head] = outs_in[head // each][head % each] + weight * gain

    @pl.when(jnp.logical_not(upper))
    def _():
        for head in range(heads):
            out[head] = outs_in[head // each][head % each]


def tail_kernel(level, weight_row, groups, heads, count, pending, near, arrivals, *refs):
    state_in = [refs[g * arrivals : (g + 1) * arrivals] for g in range(groups)]
    refs = refs[groups * arrivals :]
    query_refs, refs = refs[:7], refs[7:]
    uppers, refs = refs[:3], refs[3:]
    lowers = {}
    for group in sorted({group for group, _ in pending}):
        lowers[group], refs = refs[:5], refs[5:]
    pieces = heads // count
    outs_in = {}
    for group in range(groups):
        for piece in range(pieces):
            if (group, piece) not in pending:
                outs_in[group, piece], refs = refs[:2], refs[2:]
    outs, refs = refs[: 2 * groups], refs[2 * groups :]
    scratch, refs = refs[:2], refs[2:]
    for group, piece in pending:
        temporary, refs = refs[:2], refs[2:]
        made = lowers[group]
        queries_kernel(
            group,
            heads,
            piece * count,
            count,
            near,
            *query_refs,
            *made[:3],
            *uppers,
            *made[3:],
            *temporary,
            *scratch,
        )
        outs_in[group, piece] = temporary
    for group in range(groups):
        absorb_kernel(
            level,
            weight_row,
            group,
            heads,
            arrivals,
            0,
            pieces,
            *state_in[group],
            *query_refs[5:7],
            *[outs_in[group, piece][0] for piece in range(pieces)],
            *[outs_in[group, piece][1] for piece in range(pieces)],
            outs[2 * group],
            outs[2 * group + 1],
        )


def finish_kernel(level, weight_row, group, heads, arrivals, pieces, *refs):
    refs = refs[min(group, 1) :]
    state_in = refs[:arrivals]
    refs = refs[arrivals:]
    small_own, small_other, gate_own, gate_other, gain = refs[:5]
    outs_in = refs[5 : 5 + pieces]
    moved_in = refs[5 + pieces : 5 + 2 * pieces]
    stay, leave, total = refs[5 + 2 * pieces :]
    core, node = place()
    upper = (node >> level) % 2 == 1
    each = heads // pieces

    def add(states, transits):
        for head in range(heads):
            found = split(received(states, head))
            if transits is not None:
                found = split(mm(split(received(transits, head)), found))
            row = weight_row + 8 * core + heads * group + head
            weight = level_weight(small_own, small_other, row, core)
            extra = mm_three(split(moved_in[head // each][head % each]), found)
            total[head] = outs_in[head // each][head % each] + weight * extra

    if level:
        through = (node >> (level - 1)) % 2 == 1
        far, close = state_in[: arrivals // 2], state_in[arrivals // 2 :]

        @pl.when(upper & through)
        def _():
            add(far, close)

        @pl.when(upper & jnp.logical_not(through))
        def _():
            add(close, None)

    else:

        @pl.when(upper)
        def _():
            add(state_in, None)

    @pl.when(jnp.logical_not(upper))
    def _():
        for head in range(heads):
            total[head] = outs_in[head // each][head % each]

    lanes_all = heads * 128
    at = gate_other.shape[1] // 2 + group * lanes_all
    gates = (
        gate_own[:, group * lanes_all : (group + 1) * lanes_all],
        gate_other[:, at : at + lanes_all],
    )
    for head in range(heads):
        lanes = slice(head * 128, head * 128 + 128)
        for gate, chunk, target in ((gates[0], core, stay), (gates[1], 1 - core, leave)):
            rows = pl.ds(pl.multiple_of(chunk * CHUNK, CHUNK), CHUNK)
            attended = total[head, rows, :]
            scale = lax.rsqrt(jnp.mean(attended * attended, axis=-1, keepdims=True) + 1e-5)
            gated = attended * scale * gain[...] * silu(gate[:, lanes].astype(F32))
            target[:, lanes] = gated.astype(BF16)


def swap_kernel(*refs):
    out, sems = refs[-2:]
    count = (len(refs) - 2) // 2
    core, _ = place()
    half = out.shape[1] // 2
    width = half // count
    copies = []
    for i in range(count):
        for j, side in ((i, core), (count + i, 1 - core)):
            start = pl.multiple_of(side * half + i * width, width)
            made = pltpu.make_async_copy(refs[j], out.at[:, pl.ds(start, width)], sems.at[j])
            made.start()
            copies.append(made)
    for made in copies:
        made.wait()


def struct(shape, dtype=F32):
    return jax.ShapeDtypeStruct(shape, dtype)


def params(mib):
    return pltpu.CompilerParams(vmem_limit_bytes=mib << 20)


def cost(flops):
    return pl.CostEstimate(flops=flops, bytes_accessed=1_000_000, transcendentals=0)


GROUPS = 2
PIECES = 2


def per_device(
    query_rows,
    key_rows,
    value_rows,
    query_taps,
    key_taps,
    value_taps,
    log_alpha,
    write_strength,
    tier_mixture,
    output_gate,
    norm_gain,
):
    rows, width = query_rows.shape
    half = width // 2
    size = lax.axis_size("seq")
    nodes = size // 2
    level_total = tier_mixture.shape[0]
    near = CHUNK.bit_length()
    heads = 8 // GROUPS
    lanes = heads * 128
    shard_bits = nodes.bit_length() - 1
    cores = [(i, i ^ 1) for i in range(size)]
    small_rows = 16 * (2 + level_total)
    key_other = lax.ppermute(key_rows, "seq", cores)
    value_other = lax.ppermute(value_rows, "seq", cores)
    half_shape = struct((rows, half), BF16)
    taps_shape = struct((4, half))
    (
        query_half,
        key_half,
        value_half,
        gate_half,
        query_taps_half,
        key_taps_half,
        value_taps_half,
        halo,
        small,
        gain,
        message,
    ) = pl.pallas_call(
        prepare_kernel,
        in_specs=[pl.BlockSpec(memory_space=pltpu.HBM)] * 11,
        out_shape=[half_shape] * 4
        + [taps_shape] * 3
        + [struct((16, width), BF16), struct((small_rows, 128)), struct((1, 128))]
        + [struct((rows, width), BF16)],
        scratch_shapes=[pltpu.VMEM((3, 16, width), BF16), pltpu.SemaphoreType.DMA((16,))],
        compiler_params=params(8),
        name="prepare",
    )(
        *[
            pltpu.with_memory_space_constraint(x, pltpu.HBM)
            for x in (
                query_rows,
                key_rows,
                value_rows,
                output_gate,
                log_alpha,
                write_strength,
                tier_mixture.reshape(level_total * 16, rows),
                query_taps,
                key_taps,
                value_taps,
                norm_gain.reshape(1, 128),
            )
        ]
    )
    small_other = lax.ppermute(small, "seq", cores)
    halo_one = lax.ppermute(halo, "seq", [(i, i + 1) for i in range(1, size - 1, 2)])
    halo_two = lax.ppermute(halo, "seq", [(i, i + 2) for i in range(1, size - 1, 2)])

    def fan(value, level, riders=False):
        span = 1 << level
        results = []
        for offset in reversed(range(span)):
            route = []
            for low in range(0, nodes, 2 * span):
                hops = [(low + span - 1, low + span + offset)]
                if riders and 2 * offset < span:
                    middle = low + span + span // 2
                    hops.append((middle - 1, middle + offset))
                for source, target in hops:
                    route += [(2 * source + c, 2 * target + c) for c in range(2)]
            results.append(lax.ppermute(value, "seq", route))
        return results

    def held(count):
        return [
            struct((count, 2, 128, 128), BF16),
            struct((count, 2, 128, 128), BF16),
            struct((count, 2, 128, 256), BF16),
        ]

    square = (heads, 128, 128)
    code_shape = struct((heads * 128 + 16, 128), BF16)
    upper = pl.pallas_call(
        upper_kernel,
        out_shape=held(8) + [struct((8, 128, 128))] * 2,
        scratch_shapes=[pltpu.VMEM((8 + CHUNK, half), F32)] * 2,
        compiler_params=params(24),
        cost_estimate=cost(4_000_000_000),
        name="upper",
    )(
        key_half,
        key_other,
        value_half,
        value_other,
        key_taps_half,
        value_taps_half,
        small,
        small_other,
    )
    local = []
    arrived = []
    after = upper[4]
    for group in range(GROUPS):
        after, halo_first = lax.optimization_barrier((after, halo_one))
        made = pl.pallas_call(
            functools.partial(lower_kernel, group, heads),
            out_shape=held(heads)
            + [struct(square), struct(square), struct(square), struct(square), code_shape],
            scratch_shapes=[pltpu.VMEM((8 + CHUNK, lanes), F32)] * 2,
            compiler_params=params(24),
            cost_estimate=cost(2_500_000_000),
            name="lower",
        )(
            key_half,
            key_other,
            value_half,
            value_other,
            key_taps_half,
            value_taps_half,
            halo_first,
            halo_two,
            small,
            small_other,
            upper[3],
            upper[4],
        )
        local.append(made)
        after = made[7]
        arrived.append(fan(made[7], 0) if shard_bits else [])

    _, late_message = lax.optimization_barrier((local[0][7], message))
    query_other = gate_other = lax.ppermute(late_message, "seq", cores)
    state = [x[4] for x in local]
    transit = [x[6] for x in local]
    count = heads // PIECES
    outs = [[] for _ in range(GROUPS)]
    moved = [[] for _ in range(GROUPS)]
    pending = [(group, piece) for group in range(GROUPS) for piece in range(PIECES)]

    def ask(after):
        group, piece = pending.pop(0)
        made = local[group]
        shape = struct((count, 2 * CHUNK, 128))
        operands = [
            query_half,
            query_other,
            query_taps_half,
            halo_one,
            halo_two,
            small,
            small_other,
            *made[:3],
            *upper[:3],
            made[3],
            made[5],
        ]
        out, move = pl.pallas_call(
            functools.partial(asked_kernel, group, heads, piece * count, count, near),
            in_specs=[pl.BlockSpec(memory_space=pl.ANY)]
            + [pl.BlockSpec(memory_space=pltpu.VMEM)] * len(operands),
            out_shape=[shape, shape],
            scratch_shapes=[pltpu.VMEM((8 + CHUNK, count * 128), F32)] * 2,
            compiler_params=params(16),
            cost_estimate=cost(1_000_000),
            name="queries",
        )(after, *operands)
        outs[group].append(out)
        moved[group].append(move)
        return out

    moved_shape = struct((heads, 2 * CHUNK, 128))
    transit_codes = [None] * GROUPS

    def send_transit():
        return pl.pallas_call(
            code_kernel,
            out_shape=struct((8 * 128 + 16, 128), BF16),
            compiler_params=params(8),
            cost_estimate=cost(1_000_000),
            name="code",
        )(*transit)

    shifts = [heads * group for group in range(GROUPS)]
    passing = [[]] * GROUPS
    for level in range(shard_bits - 1):
        keeps = level < shard_bits - 2

        fanned = [[]] * GROUPS
        if keeps and level == 0:
            fanned = [fan(send_transit(), level)] * GROUPS
        elif keeps:
            fanned = [fan(x, level) for x in transit_codes]
        following = []
        for group in range(GROUPS):
            shapes = [code_shape]
            operands = list(arrived[group])
            if keeps:
                shapes += [struct(square), struct(square), code_shape]
                operands += fanned[group]
            if level == 0 and group == 1:
                after = ask(after)
            waits = [after]
            if level == 0 and group == GROUPS - 1:
                waits += [query_other]
            joined = pl.pallas_call(
                functools.partial(
                    join_kernel, level, len(arrived[group]), keeps, shifts[group], len(waits)
                ),
                in_specs=[pl.BlockSpec(memory_space=pl.ANY)] * len(waits)
                + [pl.BlockSpec(memory_space=pltpu.VMEM)] * (len(operands) + 2),
                out_shape=shapes,
                compiler_params=params(12),
                cost_estimate=cost(4_000_000_000),
                name="join",
            )(*waits, *operands, state[group], transit[group])
            after = joined[0]
            following.append(fan(joined[0], level + 1, not keeps))
            if keeps:
                state[group], transit[group], transit_codes[group] = joined[1:]
        arrivals = len(arrived[0])
        if level == 0:
            after, small_here = lax.optimization_barrier((after, small))
            operands = [x for group in range(GROUPS) for x in arrived[group]]
            operands += [query_half, query_other, query_taps_half, halo_one, halo_two]
            operands += [small_here, small_other, *upper[:3]]
            for group in sorted({group for group, _ in pending}):
                made = local[group]
                operands += [*made[:3], made[3], made[5]]
            for group in range(GROUPS):
                for out, move in zip(outs[group], moved[group]):
                    operands += [out, move]
            results = pl.pallas_call(
                functools.partial(
                    tail_kernel,
                    level,
                    32 + 16 * (near + 1 + level),
                    GROUPS,
                    heads,
                    count,
                    tuple(pending),
                    near,
                    arrivals,
                ),
                out_shape=[moved_shape] * (2 * GROUPS),
                scratch_shapes=[pltpu.VMEM((8 + CHUNK, count * 128), F32)] * 2
                + [pltpu.VMEM((count, 2 * CHUNK, 128), F32)] * (2 * len(pending)),
                compiler_params=params(24),
                cost_estimate=cost(1_000_000),
                name="tail",
            )(*operands)
            pending.clear()
            for group in range(GROUPS):
                outs[group], moved[group] = [results[2 * group]], [results[2 * group + 1]]
        else:
            for group in range(GROUPS):
                out, move = pl.pallas_call(
                    functools.partial(
                        absorb_kernel,
                        level,
                        32 + 16 * (near + 1 + level),
                        group,
                        heads,
                        arrivals,
                        len(passing[group]),
                        len(outs[group]),
                    ),
                    out_shape=[moved_shape, moved_shape],
                    compiler_params=params(12),
                    cost_estimate=cost(800_000_000),
                    name="absorb",
                )(
                    *arrived[group],
                    *passing[group],
                    small,
                    small_other,
                    *outs[group],
                    *moved[group],
                )
                outs[group], moved[group] = [out], [move]
        arrived = following
        passing = fanned
        shifts = [0] * GROUPS
    while pending:
        after = ask(after)

    level = max(shard_bits - 1, 0)
    stays = []
    comes = []
    for group in range(GROUPS):
        operands = [
            *arrived[group],
            small,
            small_other,
            gate_half,
            gate_other,
            gain,
            *outs[group],
            *moved[group],
        ]
        specs = [pl.BlockSpec(memory_space=pltpu.VMEM)] * len(operands)
        if group:
            operands = [stays[-1]] + operands
            specs = [pl.BlockSpec(memory_space=pl.ANY)] + specs
        stay, leave = pl.pallas_call(
            functools.partial(
                finish_kernel,
                level,
                32 + 16 * (near + 1 + level),
                group,
                heads,
                len(arrived[group]),
                len(outs[group]),
            ),
            in_specs=specs,
            out_shape=[struct((rows, lanes), BF16)] * 2,
            scratch_shapes=[pltpu.VMEM((heads, 2 * CHUNK, 128), F32)],
            compiler_params=params(12),
            cost_estimate=cost(1_000_000),
            name="finish",
        )(*operands)
        stays.append(stay)
        comes.append(lax.ppermute(leave, "seq", cores))
    return pl.pallas_call(
        swap_kernel,
        in_specs=[pl.BlockSpec(memory_space=pltpu.VMEM)] * (2 * GROUPS),
        out_specs=pl.BlockSpec(memory_space=pltpu.HBM),
        out_shape=struct((rows, width), BF16),
        scratch_shapes=[pltpu.SemaphoreType.DMA((2 * GROUPS,))],
        compiler_params=params(4),
        name="swap",
    )(*stays, *comes)


def solution(mesh):
    placed = (
        P(("req", "seq"), None),
        P(("req", "seq"), None),
        P(("req", "seq"), None),
        P(),
        P(),
        P(),
        P(None, ("req", "seq")),
        P(None, ("req", "seq")),
        P(None, None, ("req", "seq")),
        P(("req", "seq"), None),
        P(),
    )
    return jax.shard_map(
        per_device, mesh=mesh, in_specs=placed, out_specs=P(("req", "seq"), None), check_vma=False
    )
```

```python
import functools

import jax
import jax.numpy as jnp
from jax import lax
from jax.experimental import pallas as pl
from jax.experimental.pallas import tpu as pltpu
from jax.sharding import PartitionSpec as P

HEAD_DIM = 128
CHUNK = 128
CODE = 125.0
F32 = jnp.float32
BF16 = jnp.bfloat16


def split(x):
    high = x.astype(BF16)
    return high, (x - high.astype(F32)).astype(BF16)


def dot(a, b):
    return jnp.dot(a, b, preferred_element_type=F32)


def wide(b):
    row = jnp.concatenate(b, axis=1)
    return jnp.concatenate([row, row], axis=0)


def mm(a, b):
    width = b[0].shape[1]
    if b[0].shape[0] <= 128 and (width > 128 or a[0].shape[0] <= 128):
        both = jnp.concatenate([b[0], b[0]], axis=0)
        return dot(jnp.concatenate(a, axis=1), both) + dot(a[0], b[1])
    out = dot(jnp.concatenate(a, axis=1), wide(b))
    return out[:, :width] + out[:, width:]


def mm_three(a, b):
    return (dot(a[1], b[0]) + dot(a[0], b[1])) + dot(a[0], b[0])


def silu(u):
    half = 0.5 * u
    return half + half * jnp.tanh(half)


def encode(state):
    top = jnp.max(jnp.abs(state), axis=0, keepdims=True)
    scale = (top * 1.02 + 1e-30).astype(BF16).astype(F32)
    grade = jnp.abs(state) * (1.0 / scale)
    level = jnp.exp2(grade * (2.0 * CODE) - CODE)
    return jnp.where(state < 0, -level, level).astype(BF16), scale


def decode(code, scale):
    grade = jnp.log2(jnp.abs(code)) * (0.5 / CODE) + 0.5
    size = grade * scale
    return jnp.where(code < 0, -size, size)


def iotas(rows, columns):
    return (
        lax.broadcasted_iota(jnp.int32, (rows, columns), 0),
        lax.broadcasted_iota(jnp.int32, (rows, columns), 1),
    )


def place():
    index = lax.axis_index("seq")
    return index % 2, index // 2


def fill(scratch, own, other, before, core, chunk, first_lane, packed=False):
    lanes = scratch.shape[1]
    start = pl.multiple_of(core * 8 * HEAD_DIM + first_lane, 128)
    mine = own[:, first_lane : first_lane + lanes]
    theirs = other[:, first_lane : first_lane + lanes] if packed else other[:, pl.ds(start, lanes)]
    if before is None:
        last = jnp.where(core == 1, theirs[CHUNK - 16 :], mine[CHUNK - 16 :]).astype(F32)[13:16]
    else:
        one, two, first = before
        rows = one[:, pl.ds(start, lanes)].astype(F32) + two[:, pl.ds(start, lanes)].astype(F32)
        last = rows[first : first + 3]
    scratch[5:8, :] = last
    scratch[8 : 8 + CHUNK, :] = jnp.where(core == chunk, mine, theirs).astype(F32)


def conv(scratch, taps, columns, taps_columns):
    total = None
    for tap in range(4):
        part = taps[tap : tap + 1, taps_columns] * scratch[5 + tap : 5 + tap + CHUNK, columns]
        total = part if total is None else total + part
    return silu(total)


def unit(rows):
    return rows * lax.rsqrt(jnp.sum(rows * rows, axis=-1, keepdims=True) + 1e-6)


def token_row(own, other, row, core, chunk):
    return jnp.where(core == chunk, own[pl.ds(row, 1), :], other[pl.ds(row, 1), :])


def rows_table(rows):
    pad = -len(rows) % 8
    if pad:
        rows = rows + [jnp.zeros((pad, CHUNK), F32)]
    return jnp.concatenate(rows, axis=0)


def sums(own, other, base, parts, core):
    rows = [token_row(own, other, base + head, core, chunk) for head, chunk in parts]
    t, j = iotas(CHUNK, CHUNK)
    upper = (t <= j).astype(F32)
    run = jnp.dot(
        rows_table(rows), upper, preferred_element_type=F32, precision=lax.Precision.HIGHEST
    )
    return [run[i : i + 1] for i in range(len(parts))]


def invert(coupling, t, j):
    apart = t ^ j
    count = len(coupling)
    near = [split(jnp.where(apart < 16, -a, 0.0)) for a in coupling]
    eye = (t == j).astype(F32)
    powers = [split(mm(n, n)) for n in near]
    grown = [eye + n[0].astype(F32) + n[1].astype(F32) for n in near]
    for _ in range(2):
        for i in range(count):
            base = split(grown[i])
            left = tuple(jnp.concatenate([powers[i][k], base[k]], axis=0) for k in range(2))
            both = mm(left, powers[i])
            powers[i] = split(both[:CHUNK])
            grown[i] = grown[i] + both[CHUNK:]
    inverse = [split(grown[i] + mm(split(grown[i]), powers[i])) for i in range(count)]
    size = 16
    while size < CHUNK:
        starts = range(size, CHUNK, 2 * size)

        def pick(x):
            return jnp.concatenate([x[s : s + size] for s in starts], axis=0)

        zero = jnp.zeros((size, CHUNK), BF16)

        def spread(x):
            pieces = []
            for k in range(len(starts)):
                pieces += [zero, x[k * size : (k + 1) * size]]
            return jnp.concatenate(pieces, axis=0)

        def merge(x, rows):
            pieces = []
            for k, s in enumerate(starts):
                pieces += [x[s - size : s], rows[k * size : (k + 1) * size]]
            return jnp.concatenate(pieces, axis=0)

        mask = pick((apart >= size) & (apart < 2 * size))
        middle = []
        for i in range(count):
            lower = split(jnp.where(mask, pick(coupling[i]), 0.0))
            middle.append(split(mm(lower, inverse[i])))
        for i in range(count):
            high, low = inverse[i]
            rows = (pick(high), pick(low))
            change = mm(rows, tuple(spread(m) for m in middle[i]))
            fresh = split(rows[0].astype(F32) + rows[1].astype(F32) - change)
            inverse[i] = (merge(high, fresh[0]), merge(low, fresh[1]))
        size *= 2
    return inverse


def decay(column, row, t, j):
    return jnp.exp(jnp.where(t >= j, column - row, -1e30))


def prepare_kernel(query, key, value, gate, log_alpha, strength, mixture, query_taps, key_taps,
                   value_taps, gain, query_half, key_half, value_half, gate_half, query_taps_half,
                   key_taps_half, value_taps_half, halo, small, gain_out, message_out,
                   tails, sems):
    core, _ = place()
    rows, half = query_half.shape
    lanes = pl.ds(pl.multiple_of(core * half, half), half)
    copies = []

    def copy(source, target):
        made = pltpu.make_async_copy(source, target, sems.at[len(copies)])
        made.start()
        copies.append(made)

    for i, x in enumerate((query, key, value)):
        copy(x.at[rows - 16 : rows, :], tails.at[i])
    copy(log_alpha, small.at[0:16])
    copy(strength, small.at[16:32])
    copy(mixture, small.at[32 : small.shape[0]])
    for x, y in (
        (key, key_half),
        (value, value_half),
        (key_taps, key_taps_half),
        (value_taps, value_taps_half),
        (query_taps, query_taps_half),
        (query, query_half),
        (gate, gate_half),
    ):
        copy(x.at[:, lanes], y)
    copy(gain, gain_out)
    away = pl.ds(pl.multiple_of((1 - core) * half, half), half)
    copy(query.at[:, away], message_out.at[:, 0:half])
    copy(gate.at[:, away], message_out.at[:, half : 2 * half])
    for made in copies:
        made.wait()
    message = [tails[i][13:16, :].astype(F32) for i in range(3)]
    message.append(jnp.zeros((7, 2 * half), F32))
    halo[...] = jnp.concatenate(message, axis=0).astype(BF16)


def chunk_states(
    chunk,
    first,
    heads,
    key_taps,
    value_taps,
    small_own,
    small_other,
    key_cols_out,
    inverse_out,
    write_out,
    key_scratch,
    value_scratch,
):
    core, _ = place()
    t, j = iotas(CHUNK, CHUNK)
    base = 8 * core + first
    parts = [(head, chunk) for head in range(heads)]
    run = sums(small_own, small_other, base, parts, core)
    strengths = [
        token_row(small_own, small_other, 16 + base + head, core, chunk) for head in range(heads)
    ]
    columns = rows_table(run + strengths).T

    def lanes(head):
        return slice(head * 128, head * 128 + 128)

    def beta(head):
        return columns[:, heads + head : heads + head + 1]

    keys = [
        unit(conv(key_scratch, key_taps, lanes(head), lanes(first + head)))
        for head in range(heads)
    ]
    keys_t = [key.T for key in keys]
    coupling = []
    for head in range(heads):
        pair = split(keys_t[head])
        key_cols_out[head, 0] = pair[0]
        key_cols_out[head, 1] = pair[1]
        gram = mm(split(keys[head]), pair)
        ratio = decay(columns[:, head : head + 1], run[head], t, j)
        coupling.append(jnp.where(t > j, gram * ratio * beta(head), 0.0))
    writes = []
    for head in range(heads):
        value = conv(value_scratch, value_taps, lanes(head), lanes(first + head))
        grow = jnp.exp(columns[:, head : head + 1])
        write = jnp.concatenate([keys[head] * (beta(head) * grow), value * beta(head)], axis=1)
        write = split(write)
        write_out[head, 0] = write[0]
        write_out[head, 1] = write[1]
        writes.append(write)
    inverse = invert(coupling, t, j)
    mixed = []
    for head in range(heads):
        inverse_out[head, 0] = inverse[head][0]
        inverse_out[head, 1] = inverse[head][1]
        last = run[head][:, CHUNK - 1 : CHUNK]
        tail = keys_t[head] * jnp.exp(last - run[head])
        mixed.append(mm(split(tail), inverse[head]))
    transits = []
    states = []
    for head in range(heads):
        last = run[head][:, CHUNK - 1 : CHUNK]
        both = mm(split(mixed[head]), writes[head])
        transits.append(jnp.where(t == j, jnp.exp(last), 0.0) - both[:, :128])
        states.append(both[:, 128:])
    return transits, states


def upper_kernel(
    key_own,
    key_other,
    value_own,
    value_other,
    key_taps,
    value_taps,
    small_own,
    small_other,
    key_cols_out,
    inverse_out,
    write_out,
    transit_out,
    state_out,
    key_scratch,
    value_scratch,
):
    core, _ = place()
    fill(key_scratch, key_own, key_other, None, core, 1, 0)
    fill(value_scratch, value_own, value_other, None, core, 1, 0)
    transits, states = chunk_states(
        1,
        0,
        8,
        key_taps,
        value_taps,
        small_own,
        small_other,
        key_cols_out,
        inverse_out,
        write_out,
        key_scratch,
        value_scratch,
    )
    for head in range(8):
        transit_out[head] = transits[head]
        state_out[head] = states[head]


def lower_kernel(
    group,
    heads,
    key_own,
    key_other,
    value_own,
    value_other,
    key_taps,
    value_taps,
    halo_one,
    halo_two,
    small_own,
    small_other,
    upper_transit,
    upper_state,
    key_cols_out,
    inverse_out,
    write_out,
    first_state_out,
    state_out,
    transit_one_out,
    transit_out,
    code_out,
    key_scratch,
    value_scratch,
):
    core, _ = place()
    first = group * heads
    fill(key_scratch, key_own, key_other, (halo_one, halo_two, 3), core, 0, first * 128)
    fill(value_scratch, value_own, value_other, (halo_one, halo_two, 6), core, 0, first * 128)
    transits, states = chunk_states(
        0,
        first,
        heads,
        key_taps,
        value_taps,
        small_own,
        small_other,
        key_cols_out,
        inverse_out,
        write_out,
        key_scratch,
        value_scratch,
    )
    joined = []
    pairs = [split(upper_transit[first + head]) for head in range(heads)]
    for head in range(heads):
        joined.append(mm(pairs[head], split(states[head])) + upper_state[first + head])
    encode_all(joined, code_out)
    for head in range(heads):
        first_state_out[head] = states[head]
        transit_one_out[head] = transits[head]
        state_out[head] = joined[head]
        transit_out[head] = mm(pairs[head], split(transits[head]))


def queries_kernel(
    group,
    heads,
    first,
    count,
    near,
    query_own,
    query_other,
    query_taps,
    halo_one,
    halo_two,
    small_own,
    small_other,
    key_cols_one,
    inverse_one,
    write_one,
    key_cols_two,
    inverse_two,
    write_two,
    first_state,
    transit_one,
    out,
    moved,
    scratch_one,
    scratch_two,
):
    core, _ = place()
    start = group * heads + first
    fill(scratch_one, query_own, query_other, (halo_one, halo_two, 0), core, 0, start * 128, True)
    fill(scratch_two, query_own, query_other, None, core, 1, start * 128, True)
    t, j = iotas(CHUNK, CHUNK)
    apart = t ^ j
    parts = [(head, chunk) for head in range(count) for chunk in range(2)]
    base = 8 * core + start
    run = sums(small_own, small_other, base, parts, core)
    rows = list(run)
    for head, chunk in parts:
        for level in range(near + 1):
            row = 32 + 16 * level + base + head
            rows.append(token_row(small_own, small_other, row, core, chunk))
    columns = rows_table(rows).T

    def held(one, two, head, chunk):
        if chunk:
            return two[start + head, 0], two[start + head, 1]
        return one[first + head, 0], one[first + head, 1]

    mixings = []
    queries = []
    for i, (head, chunk) in enumerate(parts):
        lanes = slice(head * 128, head * 128 + 128)
        taps_lanes = slice((start + head) * 128, (start + head) * 128 + 128)
        scratch = scratch_two if chunk else scratch_one
        query = unit(conv(scratch, query_taps, lanes, taps_lanes))
        queries.append(query)
        ratio = decay(columns[:, i : i + 1], run[i], t, j)
        scores = mm(split(query), held(key_cols_one, key_cols_two, head, chunk)) * ratio
        mixings.append(mm(split(scores), held(inverse_one, inverse_two, head, chunk)))
    for i, (head, chunk) in enumerate(parts):
        at = len(parts) + i * (near + 1)
        level_mat = columns[:, at : at + 1]
        for level in range(1, near):
            weight = columns[:, at + level : at + level + 1]
            level_mat = jnp.where(apart >= 1 << (level - 1), weight, level_mat)
        high, low = held(write_one, write_two, head, chunk)
        within = mm(split(mixings[i] * level_mat), (high[:, 128:], low[:, 128:]))
        grow = jnp.exp(columns[:, i : i + 1])
        effective = grow * queries[i] - mm(split(mixings[i]), (high[:, :128], low[:, :128]))
        rows = slice(chunk * CHUNK, chunk * CHUNK + CHUNK)
        if chunk:
            pair = split(effective)
            weight = columns[:, at + near : at + near + 1]
            within = within + weight * mm(pair, split(first_state[first + head]))
            effective = mm(pair, split(transit_one[first + head]))
        out[head, rows, :] = within
        moved[head, rows, :] = effective


def asked_kernel(group, heads, first, count, near, after, *refs):
    queries_kernel(group, heads, first, count, near, *refs)


def received(refs, head):
    code = None
    scale = None
    for ref in refs:
        tail = ref.shape[0] - 16 + head
        part = ref[head * 128 : head * 128 + 128, :].astype(F32)
        row = ref[tail : tail + 1, :].astype(F32)
        code = part if code is None else code + part
        scale = row if scale is None else scale + row
    return decode(code, scale)


def pack_rows(scales):
    zeros = jnp.zeros((16 - len(scales), 128), F32)
    return jnp.concatenate(scales + [zeros], axis=0).astype(BF16)


def encode_all(values, code_out):
    scales = []
    for head, value in enumerate(values):
        code, scale = encode(value)
        code_out[head * 128 : head * 128 + 128, :] = code
        scales.append(scale)
    head = len(values)
    code_out[head * 128 : head * 128 + 16, :] = pack_rows(scales)


def join_kernel(level, arrivals, with_transit, shift, waits, *refs):
    refs = refs[waits:]
    state_in = refs[:arrivals]
    refs = refs[arrivals:]
    transit_in = ()
    if with_transit:
        transit_in = refs[:arrivals]
        refs = refs[arrivals:]
    state, transit, code_out = refs[:3]
    refs = refs[3:]
    heads = state.shape[0]
    _, node = place()
    upper = (node >> level) % 2 == 1
    if not with_transit:
        late = (node >> (level + 1)) % 2 == 1
        riding = late & jnp.logical_not(upper)
        upper = upper & jnp.logical_not(late)

        @pl.when(riding)
        def _():
            encode_all([transit[head] for head in range(heads)], code_out)

    @pl.when(upper)
    def _():
        fresh = []
        for head in range(heads):
            pair = split(transit[head])
            fresh.append(mm(pair, split(received(state_in, head))) + state[head])
            if with_transit:
                refs[0][head] = fresh[head]
                refs[1][head] = mm(pair, split(received(transit_in, shift + head)))
        encode_all(fresh, code_out)
        if with_transit:
            encode_all([refs[1][head] for head in range(heads)], refs[2])

    if with_transit:

        @pl.when(jnp.logical_not(upper))
        def _():
            encode_all([state[head] for head in range(heads)], code_out)
            for head in range(heads):
                refs[0][head] = state[head]
                refs[1][head] = transit[head]
            encode_all([transit[head] for head in range(heads)], refs[2])


def code_kernel(*refs):
    values = [ref[head] for ref in refs[:-1] for head in range(ref.shape[0])]
    encode_all(values, refs[-1])


def level_weight(own, other, row, core):
    rows = [token_row(own, other, row, core, chunk) for chunk in range(2)]
    columns = rows_table(rows).T
    return jnp.concatenate([columns[:, 0:1], columns[:, 1:2]], axis=0)


def absorb_kernel(level, weight_row, group, heads, arrivals, passed, pieces, *refs):
    state_in = refs[:arrivals]
    transit_in = refs[arrivals : arrivals + passed]
    refs = refs[arrivals + passed :]
    small_own, small_other = refs[:2]
    outs_in = refs[2 : 2 + pieces]
    moved_in = refs[2 + pieces : 2 + 2 * pieces]
    out, moved = refs[2 + 2 * pieces :]
    core, node = place()
    upper = (node >> level) % 2 == 1
    each = heads // pieces
    behind = jnp.bool_(False)
    if passed:
        behind = ((node >> (level - 1)) % 2 == 1) & ((node >> level) > 0)

        @pl.when(behind)
        def _():
            shift = group * heads if level == 1 else 0
            for head in range(heads):
                pair = split(moved_in[head // each][head % each])
                moved[head] = mm(pair, split(received(transit_in, shift + head)))

    @pl.when(jnp.logical_not(behind))
    def _():
        for head in range(heads):
            moved[head] = moved_in[head // each][head % each]

    @pl.when(upper)
    def _():
        for head in range(heads):
            pair = split(moved[head])
            row = weight_row + 8 * core + heads * group + head
            weight = level_weight(small_own, small_other, row, core)
            gain = mm(pair, split(received(state_in, head)))
            out[head] = outs_in[head // each][head % each] + weight * gain

    @pl.when(jnp.logical_not(upper))
    def _():
        for head in range(heads):
            out[head] = outs_in[head // each][head % each]


def tail_kernel(level, weight_row, groups, heads, count, pending, near, arrivals, *refs):
    state_in = [refs[g * arrivals : (g + 1) * arrivals] for g in range(groups)]
    refs = refs[groups * arrivals :]
    query_refs, refs = refs[:7], refs[7:]
    uppers, refs = refs[:3], refs[3:]
    lowers = {}
    for group in sorted({group for group, _ in pending}):
        lowers[group], refs = refs[:5], refs[5:]
    pieces = heads // count
    outs_in = {}
    for group in range(groups):
        for piece in range(pieces):
            if (group, piece) not in pending:
                outs_in[group, piece], refs = refs[:2], refs[2:]
    outs, refs = refs[: 2 * groups], refs[2 * groups :]
    scratch, refs = refs[:2], refs[2:]
    for group, piece in pending:
        temporary, refs = refs[:2], refs[2:]
        made = lowers[group]
        queries_kernel(
            group,
            heads,
            piece * count,
            count,
            near,
            *query_refs,
            *made[:3],
            *uppers,
            *made[3:],
            *temporary,
            *scratch,
        )
        outs_in[group, piece] = temporary
    for group in range(groups):
        absorb_kernel(
            level,
            weight_row,
            group,
            heads,
            arrivals,
            0,
            pieces,
            *state_in[group],
            *query_refs[5:7],
            *[outs_in[group, piece][0] for piece in range(pieces)],
            *[outs_in[group, piece][1] for piece in range(pieces)],
            outs[2 * group],
            outs[2 * group + 1],
        )


def finish_kernel(level, weight_row, group, heads, arrivals, pieces, *refs):
    refs = refs[min(group, 1) :]
    state_in = refs[:arrivals]
    refs = refs[arrivals:]
    small_own, small_other, gate_own, gate_other, gain = refs[:5]
    outs_in = refs[5 : 5 + pieces]
    moved_in = refs[5 + pieces : 5 + 2 * pieces]
    stay, leave, total = refs[5 + 2 * pieces :]
    core, node = place()
    upper = (node >> level) % 2 == 1
    each = heads // pieces

    def add(states, transits):
        for head in range(heads):
            found = split(received(states, head))
            if transits is not None:
                found = split(mm(split(received(transits, head)), found))
            row = weight_row + 8 * core + heads * group + head
            weight = level_weight(small_own, small_other, row, core)
            extra = mm_three(split(moved_in[head // each][head % each]), found)
            total[head] = outs_in[head // each][head % each] + weight * extra

    if level:
        through = (node >> (level - 1)) % 2 == 1
        far, close = state_in[: arrivals // 2], state_in[arrivals // 2 :]

        @pl.when(upper & through)
        def _():
            add(far, close)

        @pl.when(upper & jnp.logical_not(through))
        def _():
            add(close, None)

    else:

        @pl.when(upper)
        def _():
            add(state_in, None)

    @pl.when(jnp.logical_not(upper))
    def _():
        for head in range(heads):
            total[head] = outs_in[head // each][head % each]

    lanes_all = heads * 128
    at = gate_other.shape[1] // 2 + group * lanes_all
    gates = (
        gate_own[:, group * lanes_all : (group + 1) * lanes_all],
        gate_other[:, at : at + lanes_all],
    )
    for head in range(heads):
        lanes = slice(head * 128, head * 128 + 128)
        for gate, chunk, target in ((gates[0], core, stay), (gates[1], 1 - core, leave)):
            rows = pl.ds(pl.multiple_of(chunk * CHUNK, CHUNK), CHUNK)
            attended = total[head, rows, :]
            scale = lax.rsqrt(jnp.mean(attended * attended, axis=-1, keepdims=True) + 1e-5)
            gated = attended * scale * gain[...] * silu(gate[:, lanes].astype(F32))
            target[:, lanes] = gated.astype(BF16)


def swap_kernel(*refs):
    out, sems = refs[-2:]
    count = (len(refs) - 2) // 2
    core, _ = place()
    half = out.shape[1] // 2
    width = half // count
    copies = []
    for i in range(count):
        for j, side in ((i, core), (count + i, 1 - core)):
            start = pl.multiple_of(side * half + i * width, width)
            made = pltpu.make_async_copy(refs[j], out.at[:, pl.ds(start, width)], sems.at[j])
            made.start()
            copies.append(made)
    for made in copies:
        made.wait()


def struct(shape, dtype=F32):
    return jax.ShapeDtypeStruct(shape, dtype)


def params(mib):
    return pltpu.CompilerParams(vmem_limit_bytes=mib << 20)


def cost(flops):
    return pl.CostEstimate(flops=flops, bytes_accessed=1_000_000, transcendentals=0)


GROUPS = 2
PIECES = 2


def per_device(
    query_rows,
    key_rows,
    value_rows,
    query_taps,
    key_taps,
    value_taps,
    log_alpha,
    write_strength,
    tier_mixture,
    output_gate,
    norm_gain,
):
    rows, width = query_rows.shape
    half = width // 2
    size = lax.axis_size("seq")
    nodes = size // 2
    level_total = tier_mixture.shape[0]
    near = CHUNK.bit_length()
    heads = 8 // GROUPS
    lanes = heads * 128
    shard_bits = nodes.bit_length() - 1
    cores = [(i, i ^ 1) for i in range(size)]
    small_rows = 16 * (2 + level_total)
    key_other = lax.ppermute(key_rows, "seq", cores)
    value_other = lax.ppermute(value_rows, "seq", cores)
    half_shape = struct((rows, half), BF16)
    taps_shape = struct((4, half))
    (
        query_half,
        key_half,
        value_half,
        gate_half,
        query_taps_half,
        key_taps_half,
        value_taps_half,
        halo,
        small,
        gain,
        message,
    ) = pl.pallas_call(
        prepare_kernel,
        in_specs=[pl.BlockSpec(memory_space=pltpu.HBM)] * 11,
        out_shape=[half_shape] * 4
        + [taps_shape] * 3
        + [struct((16, width), BF16), struct((small_rows, 128)), struct((1, 128))]
        + [struct((rows, width), BF16)],
        scratch_shapes=[pltpu.VMEM((3, 16, width), BF16), pltpu.SemaphoreType.DMA((16,))],
        compiler_params=params(8),
        name="prepare",
    )(
        *[
            pltpu.with_memory_space_constraint(x, pltpu.HBM)
            for x in (
                query_rows,
                key_rows,
                value_rows,
                output_gate,
                log_alpha,
                write_strength,
                tier_mixture.reshape(level_total * 16, rows),
                query_taps,
                key_taps,
                value_taps,
                norm_gain.reshape(1, 128),
            )
        ]
    )
    small_other = lax.ppermute(small, "seq", cores)
    halo_one = lax.ppermute(halo, "seq", [(i, i + 1) for i in range(1, size - 1, 2)])
    halo_two = lax.ppermute(halo, "seq", [(i, i + 2) for i in range(1, size - 1, 2)])

    def fan(value, level, riders=False):
        span = 1 << level
        results = []
        for offset in reversed(range(span)):
            route = []
            for low in range(0, nodes, 2 * span):
                hops = [(low + span - 1, low + span + offset)]
                if riders and 2 * offset < span:
                    middle = low + span + span // 2
                    hops.append((middle - 1, middle + offset))
                for source, target in hops:
                    route += [(2 * source + c, 2 * target + c) for c in range(2)]
            results.append(lax.ppermute(value, "seq", route))
        return results

    def held(count):
        return [
            struct((count, 2, 128, 128), BF16),
            struct((count, 2, 128, 128), BF16),
            struct((count, 2, 128, 256), BF16),
        ]

    square = (heads, 128, 128)
    code_shape = struct((heads * 128 + 16, 128), BF16)
    upper = pl.pallas_call(
        upper_kernel,
        out_shape=held(8) + [struct((8, 128, 128))] * 2,
        scratch_shapes=[pltpu.VMEM((8 + CHUNK, half), F32)] * 2,
        compiler_params=params(24),
        cost_estimate=cost(4_000_000_000),
        name="upper",
    )(
        key_half,
        key_other,
        value_half,
        value_other,
        key_taps_half,
        value_taps_half,
        small,
        small_other,
    )
    local = []
    arrived = []
    after = upper[4]
    for group in range(GROUPS):
        after, halo_first = lax.optimization_barrier((after, halo_one))
        made = pl.pallas_call(
            functools.partial(lower_kernel, group, heads),
            out_shape=held(heads)
            + [struct(square), struct(square), struct(square), struct(square), code_shape],
            scratch_shapes=[pltpu.VMEM((8 + CHUNK, lanes), F32)] * 2,
            compiler_params=params(24),
            cost_estimate=cost(2_500_000_000),
            name="lower",
        )(
            key_half,
            key_other,
            value_half,
            value_other,
            key_taps_half,
            value_taps_half,
            halo_first,
            halo_two,
            small,
            small_other,
            upper[3],
            upper[4],
        )
        local.append(made)
        after = made[7]
        arrived.append(fan(made[7], 0) if shard_bits else [])

    _, late_message = lax.optimization_barrier((local[0][7], message))
    query_other = gate_other = lax.ppermute(late_message, "seq", cores)
    state = [x[4] for x in local]
    transit = [x[6] for x in local]
    count = heads // PIECES
    outs = [[] for _ in range(GROUPS)]
    moved = [[] for _ in range(GROUPS)]
    pending = [(group, piece) for group in range(GROUPS) for piece in range(PIECES)]

    def ask(after):
        group, piece = pending.pop(0)
        made = local[group]
        shape = struct((count, 2 * CHUNK, 128))
        operands = [
            query_half,
            query_other,
            query_taps_half,
            halo_one,
            halo_two,
            small,
            small_other,
            *made[:3],
            *upper[:3],
            made[3],
            made[5],
        ]
        out, move = pl.pallas_call(
            functools.partial(asked_kernel, group, heads, piece * count, count, near),
            in_specs=[pl.BlockSpec(memory_space=pl.ANY)]
            + [pl.BlockSpec(memory_space=pltpu.VMEM)] * len(operands),
            out_shape=[shape, shape],
            scratch_shapes=[pltpu.VMEM((8 + CHUNK, count * 128), F32)] * 2,
            compiler_params=params(16),
            cost_estimate=cost(1_000_000),
            name="queries",
        )(after, *operands)
        outs[group].append(out)
        moved[group].append(move)
        return out

    moved_shape = struct((heads, 2 * CHUNK, 128))
    transit_codes = [None] * GROUPS

    def send_transit():
        return pl.pallas_call(
            code_kernel,
            out_shape=struct((8 * 128 + 16, 128), BF16),
            compiler_params=params(8),
            cost_estimate=cost(1_000_000),
            name="code",
        )(*transit)

    shifts = [heads * group for group in range(GROUPS)]
    passing = [[]] * GROUPS
    for level in range(shard_bits - 1):
        keeps = level < shard_bits - 2

        fanned = [[]] * GROUPS
        if keeps and level == 0:
            fanned = [fan(send_transit(), level)] * GROUPS
        elif keeps:
            fanned = [fan(x, level) for x in transit_codes]
        following = []
        for group in range(GROUPS):
            shapes = [code_shape]
            operands = list(arrived[group])
            if keeps:
                shapes += [struct(square), struct(square), code_shape]
                operands += fanned[group]
            if level == 0 and group == 1:
                after = ask(after)
            waits = [after]
            if level == 0 and group == GROUPS - 1:
                waits += [query_other]
            joined = pl.pallas_call(
                functools.partial(
                    join_kernel, level, len(arrived[group]), keeps, shifts[group], len(waits)
                ),
                in_specs=[pl.BlockSpec(memory_space=pl.ANY)] * len(waits)
                + [pl.BlockSpec(memory_space=pltpu.VMEM)] * (len(operands) + 2),
                out_shape=shapes,
                compiler_params=params(12),
                cost_estimate=cost(4_000_000_000),
                name="join",
            )(*waits, *operands, state[group], transit[group])
            after = joined[0]
            following.append(fan(joined[0], level + 1, not keeps))
            if keeps:
                state[group], transit[group], transit_codes[group] = joined[1:]
        arrivals = len(arrived[0])
        if level == 0:
            after, small_here = lax.optimization_barrier((after, small))
            operands = [x for group in range(GROUPS) for x in arrived[group]]
            operands += [query_half, query_other, query_taps_half, halo_one, halo_two]
            operands += [small_here, small_other, *upper[:3]]
            for group in sorted({group for group, _ in pending}):
                made = local[group]
                operands += [*made[:3], made[3], made[5]]
            for group in range(GROUPS):
                for out, move in zip(outs[group], moved[group]):
                    operands += [out, move]
            results = pl.pallas_call(
                functools.partial(
                    tail_kernel,
                    level,
                    32 + 16 * (near + 1 + level),
                    GROUPS,
                    heads,
                    count,
                    tuple(pending),
                    near,
                    arrivals,
                ),
                out_shape=[moved_shape] * (2 * GROUPS),
                scratch_shapes=[pltpu.VMEM((8 + CHUNK, count * 128), F32)] * 2
                + [pltpu.VMEM((count, 2 * CHUNK, 128), F32)] * (2 * len(pending)),
                compiler_params=params(24),
                cost_estimate=cost(1_000_000),
                name="tail",
            )(*operands)
            pending.clear()
            for group in range(GROUPS):
                outs[group], moved[group] = [results[2 * group]], [results[2 * group + 1]]
        else:
            for group in range(GROUPS):
                out, move = pl.pallas_call(
                    functools.partial(
                        absorb_kernel,
                        level,
                        32 + 16 * (near + 1 + level),
                        group,
                        heads,
                        arrivals,
                        len(passing[group]),
                        len(outs[group]),
                    ),
                    out_shape=[moved_shape, moved_shape],
                    compiler_params=params(12),
                    cost_estimate=cost(800_000_000),
                    name="absorb",
                )(
                    *arrived[group],
                    *passing[group],
                    small,
                    small_other,
                    *outs[group],
                    *moved[group],
                )
                outs[group], moved[group] = [out], [move]
        arrived = following
        passing = fanned
        shifts = [0] * GROUPS
    while pending:
        after = ask(after)

    level = max(shard_bits - 1, 0)
    stays = []
    comes = []
    for group in range(GROUPS):
        operands = [
            *arrived[group],
            small,
            small_other,
            gate_half,
            gate_other,
            gain,
            *outs[group],
            *moved[group],
        ]
        specs = [pl.BlockSpec(memory_space=pltpu.VMEM)] * len(operands)
        if group:
            operands = [stays[-1]] + operands
            specs = [pl.BlockSpec(memory_space=pl.ANY)] + specs
        stay, leave = pl.pallas_call(
            functools.partial(
                finish_kernel,
                level,
                32 + 16 * (near + 1 + level),
                group,
                heads,
                len(arrived[group]),
                len(outs[group]),
            ),
            in_specs=specs,
            out_shape=[struct((rows, lanes), BF16)] * 2,
            scratch_shapes=[pltpu.VMEM((heads, 2 * CHUNK, 128), F32)],
            compiler_params=params(12),
            cost_estimate=cost(1_000_000),
            name="finish",
        )(*operands)
        stays.append(stay)
        comes.append(lax.ppermute(leave, "seq", cores))
    return pl.pallas_call(
        swap_kernel,
        in_specs=[pl.BlockSpec(memory_space=pltpu.VMEM)] * (2 * GROUPS),
        out_specs=pl.BlockSpec(memory_space=pltpu.HBM),
        out_shape=struct((rows, width), BF16),
        scratch_shapes=[pltpu.SemaphoreType.DMA((2 * GROUPS,))],
        compiler_params=params(4),
        name="swap",
    )(*stays, *comes)


def solution(mesh):
    placed = (
        P(("req", "seq"), None),
        P(("req", "seq"), None),
        P(("req", "seq"), None),
        P(),
        P(),
        P(),
        P(None, ("req", "seq")),
        P(None, ("req", "seq")),
        P(None, None, ("req", "seq")),
        P(("req", "seq"), None),
        P(),
    )
    return jax.shard_map(
        per_device, mesh=mesh, in_specs=placed, out_specs=P(("req", "seq"), None), check_vma=False
    )
```

```python
import functools

import jax
import jax.numpy as jnp
from jax import lax
from jax.experimental import pallas as pl
from jax.experimental.pallas import tpu as pltpu
from jax.sharding import PartitionSpec as P

HEAD_DIM = 128
CHUNK = 128
CODE = 125.0
F32 = jnp.float32
BF16 = jnp.bfloat16


def split(x):
    high = x.astype(BF16)
    return high, (x - high.astype(F32)).astype(BF16)


def dot(a, b):
    return jnp.dot(a, b, preferred_element_type=F32)


def wide(b):
    row = jnp.concatenate(b, axis=1)
    return jnp.concatenate([row, row], axis=0)


def mm(a, b):
    width = b[0].shape[1]
    if b[0].shape[0] <= 128 and (width > 128 or a[0].shape[0] <= 128):
        both = jnp.concatenate([b[0], b[0]], axis=0)
        return dot(jnp.concatenate(a, axis=1), both) + dot(a[0], b[1])
    out = dot(jnp.concatenate(a, axis=1), wide(b))
    return out[:, :width] + out[:, width:]


def mm_three(a, b):
    return (dot(a[1], b[0]) + dot(a[0], b[1])) + dot(a[0], b[0])


def silu(u):
    half = 0.5 * u
    return half + half * jnp.tanh(half)


def encode(state):
    top = jnp.max(jnp.abs(state), axis=0, keepdims=True)
    scale = (top * 1.02 + 1e-30).astype(BF16).astype(F32)
    grade = jnp.abs(state) * (1.0 / scale)
    level = jnp.exp2(grade * (2.0 * CODE) - CODE)
    return jnp.where(state < 0, -level, level).astype(BF16), scale


def decode(code, scale):
    grade = jnp.log2(jnp.abs(code)) * (0.5 / CODE) + 0.5
    size = grade * scale
    return jnp.where(code < 0, -size, size)


def iotas(rows, columns):
    return (
        lax.broadcasted_iota(jnp.int32, (rows, columns), 0),
        lax.broadcasted_iota(jnp.int32, (rows, columns), 1),
    )


def place():
    index = lax.axis_index("seq")
    return index % 2, index // 2


def fill(scratch, own, other, before, core, chunk, first_lane, packed=False):
    lanes = scratch.shape[1]
    start = pl.multiple_of(core * 8 * HEAD_DIM + first_lane, 128)
    mine = own[:, first_lane : first_lane + lanes]
    theirs = other[:, first_lane : first_lane + lanes] if packed else other[:, pl.ds(start, lanes)]
    if before is None:
        last = jnp.where(core == 1, theirs[CHUNK - 16 :], mine[CHUNK - 16 :]).astype(F32)[13:16]
    else:
        one, two, first = before
        rows = one[:, pl.ds(start, lanes)].astype(F32) + two[:, pl.ds(start, lanes)].astype(F32)
        last = rows[first : first + 3]
    scratch[5:8, :] = last
    scratch[8 : 8 + CHUNK, :] = jnp.where(core == chunk, mine, theirs).astype(F32)


def conv(scratch, taps, columns, taps_columns):
    total = None
    for tap in range(4):
        part = taps[tap : tap + 1, taps_columns] * scratch[5 + tap : 5 + tap + CHUNK, columns]
        total = part if total is None else total + part
    return silu(total)


def unit(rows):
    return rows * lax.rsqrt(jnp.sum(rows * rows, axis=-1, keepdims=True) + 1e-6)


def token_row(own, other, row, core, chunk):
    return jnp.where(core == chunk, own[pl.ds(row, 1), :], other[pl.ds(row, 1), :])


def rows_table(rows):
    pad = -len(rows) % 8
    if pad:
        rows = rows + [jnp.zeros((pad, CHUNK), F32)]
    return jnp.concatenate(rows, axis=0)


def sums(own, other, base, parts, core):
    rows = [token_row(own, other, base + head, core, chunk) for head, chunk in parts]
    t, j = iotas(CHUNK, CHUNK)
    upper = (t <= j).astype(F32)
    run = jnp.dot(
        rows_table(rows), upper, preferred_element_type=F32, precision=lax.Precision.HIGHEST
    )
    return [run[i : i + 1] for i in range(len(parts))]


def invert(coupling, t, j):
    apart = t ^ j
    count = len(coupling)
    near = [split(jnp.where(apart < 16, -a, 0.0)) for a in coupling]
    eye = (t == j).astype(F32)
    powers = [split(mm(n, n)) for n in near]
    grown = [eye + n[0].astype(F32) + n[1].astype(F32) for n in near]
    for _ in range(2):
        for i in range(count):
            base = split(grown[i])
            left = tuple(jnp.concatenate([powers[i][k], base[k]], axis=0) for k in range(2))
            both = mm(left, powers[i])
            powers[i] = split(both[:CHUNK])
            grown[i] = grown[i] + both[CHUNK:]
    inverse = [split(grown[i] + mm(split(grown[i]), powers[i])) for i in range(count)]
    size = 16
    while size < CHUNK:
        starts = range(size, CHUNK, 2 * size)

        def pick(x):
            return jnp.concatenate([x[s : s + size] for s in starts], axis=0)

        zero = jnp.zeros((size, CHUNK), BF16)

        def spread(x):
            pieces = []
            for k in range(len(starts)):
                pieces += [zero, x[k * size : (k + 1) * size]]
            return jnp.concatenate(pieces, axis=0)

        def merge(x, rows):
            pieces = []
            for k, s in enumerate(starts):
                pieces += [x[s - size : s], rows[k * size : (k + 1) * size]]
            return jnp.concatenate(pieces, axis=0)

        mask = pick((apart >= size) & (apart < 2 * size))
        middle = []
        for i in range(count):
            lower = split(jnp.where(mask, pick(coupling[i]), 0.0))
            middle.append(split(mm(lower, inverse[i])))
        for i in range(count):
            high, low = inverse[i]
            rows = (pick(high), pick(low))
            change = mm(rows, tuple(spread(m) for m in middle[i]))
            fresh = split(rows[0].astype(F32) + rows[1].astype(F32) - change)
            inverse[i] = (merge(high, fresh[0]), merge(low, fresh[1]))
        size *= 2
    return inverse


def decay(column, row, t, j):
    return jnp.exp(jnp.where(t >= j, column - row, -1e30))


def prepare_kernel(query, key, value, gate, log_alpha, strength, mixture, query_taps, key_taps,
                   value_taps, gain, query_half, key_half, value_half, gate_half, query_taps_half,
                   key_taps_half, value_taps_half, halo, small, gain_out, message_out,
                   tails, sems):
    core, _ = place()
    rows, half = query_half.shape
    lanes = pl.ds(pl.multiple_of(core * half, half), half)
    copies = []

    def copy(source, target):
        made = pltpu.make_async_copy(source, target, sems.at[len(copies)])
        made.start()
        copies.append(made)

    for i, x in enumerate((query, key, value)):
        copy(x.at[rows - 16 : rows, :], tails.at[i])
    copy(log_alpha, small.at[0:16])
    copy(strength, small.at[16:32])
    copy(mixture, small.at[32 : small.shape[0]])
    for x, y in (
        (key, key_half),
        (value, value_half),
        (key_taps, key_taps_half),
        (value_taps, value_taps_half),
        (query_taps, query_taps_half),
        (query, query_half),
        (gate, gate_half),
    ):
        copy(x.at[:, lanes], y)
    copy(gain, gain_out)
    away = pl.ds(pl.multiple_of((1 - core) * half, half), half)
    copy(query.at[:, away], message_out.at[:, 0:half])
    copy(gate.at[:, away], message_out.at[:, half : 2 * half])
    for made in copies:
        made.wait()
    message = [tails[i][13:16, :].astype(F32) for i in range(3)]
    message.append(jnp.zeros((7, 2 * half), F32))
    halo[...] = jnp.concatenate(message, axis=0).astype(BF16)


def chunk_states(
    chunk,
    first,
    heads,
    key_taps,
    value_taps,
    small_own,
    small_other,
    key_cols_out,
    inverse_out,
    write_out,
    key_scratch,
    value_scratch,
):
    core, _ = place()
    t, j = iotas(CHUNK, CHUNK)
    base = 8 * core + first
    parts = [(head, chunk) for head in range(heads)]
    run = sums(small_own, small_other, base, parts, core)
    strengths = [
        token_row(small_own, small_other, 16 + base + head, core, chunk) for head in range(heads)
    ]
    columns = rows_table(run + strengths).T

    def lanes(head):
        return slice(head * 128, head * 128 + 128)

    def beta(head):
        return columns[:, heads + head : heads + head + 1]

    keys = [
        unit(conv(key_scratch, key_taps, lanes(head), lanes(first + head)))
        for head in range(heads)
    ]
    keys_t = [key.T for key in keys]
    coupling = []
    for head in range(heads):
        pair = split(keys_t[head])
        key_cols_out[head, 0] = pair[0]
        key_cols_out[head, 1] = pair[1]
        gram = mm(split(keys[head]), pair)
        ratio = decay(columns[:, head : head + 1], run[head], t, j)
        coupling.append(jnp.where(t > j, gram * ratio * beta(head), 0.0))
    inverse = invert(coupling, t, j)
    mixed = []
    for head in range(heads):
        inverse_out[head, 0] = inverse[head][0]
        inverse_out[head, 1] = inverse[head][1]
        last = run[head][:, CHUNK - 1 : CHUNK]
        tail = keys_t[head] * jnp.exp(last - run[head])
        mixed.append(mm(split(tail), inverse[head]))
    transits = []
    states = []
    for head in range(heads):
        value = conv(value_scratch, value_taps, lanes(head), lanes(first + head))
        grow = jnp.exp(columns[:, head : head + 1])
        write = jnp.concatenate([keys[head] * (beta(head) * grow), value * beta(head)], axis=1)
        write = split(write)
        write_out[head, 0] = write[0]
        write_out[head, 1] = write[1]
        last = run[head][:, CHUNK - 1 : CHUNK]
        both = mm(split(mixed[head]), write)
        transits.append(jnp.where(t == j, jnp.exp(last), 0.0) - both[:, :128])
        states.append(both[:, 128:])
    return transits, states


def upper_kernel(
    key_own,
    key_other,
    value_own,
    value_other,
    key_taps,
    value_taps,
    small_own,
    small_other,
    key_cols_out,
    inverse_out,
    write_out,
    transit_out,
    state_out,
    key_scratch,
    value_scratch,
):
    core, _ = place()
    fill(key_scratch, key_own, key_other, None, core, 1, 0)
    fill(value_scratch, value_own, value_other, None, core, 1, 0)
    transits, states = chunk_states(
        1,
        0,
        8,
        key_taps,
        value_taps,
        small_own,
        small_other,
        key_cols_out,
        inverse_out,
        write_out,
        key_scratch,
        value_scratch,
    )
    for head in range(8):
        transit_out[head] = transits[head]
        state_out[head] = states[head]


def lower_kernel(
    group,
    heads,
    key_own,
    key_other,
    value_own,
    value_other,
    key_taps,
    value_taps,
    halo_one,
    halo_two,
    small_own,
    small_other,
    upper_transit,
    upper_state,
    key_cols_out,
    inverse_out,
    write_out,
    first_state_out,
    state_out,
    transit_one_out,
    transit_out,
    code_out,
    key_scratch,
    value_scratch,
):
    core, _ = place()
    first = group * heads
    fill(key_scratch, key_own, key_other, (halo_one, halo_two, 3), core, 0, first * 128)
    fill(value_scratch, value_own, value_other, (halo_one, halo_two, 6), core, 0, first * 128)
    transits, states = chunk_states(
        0,
        first,
        heads,
        key_taps,
        value_taps,
        small_own,
        small_other,
        key_cols_out,
        inverse_out,
        write_out,
        key_scratch,
        value_scratch,
    )
    joined = []
    pairs = [split(upper_transit[first + head]) for head in range(heads)]
    for head in range(heads):
        joined.append(mm(pairs[head], split(states[head])) + upper_state[first + head])
    encode_all(joined, code_out)
    for head in range(heads):
        first_state_out[head] = states[head]
        transit_one_out[head] = transits[head]
        state_out[head] = joined[head]
        transit_out[head] = mm(pairs[head], split(transits[head]))


def queries_kernel(
    group,
    heads,
    first,
    count,
    near,
    query_own,
    query_other,
    query_taps,
    halo_one,
    halo_two,
    small_own,
    small_other,
    key_cols_one,
    inverse_one,
    write_one,
    key_cols_two,
    inverse_two,
    write_two,
    first_state,
    transit_one,
    out,
    moved,
    scratch_one,
    scratch_two,
):
    core, _ = place()
    start = group * heads + first
    fill(scratch_one, query_own, query_other, (halo_one, halo_two, 0), core, 0, start * 128, True)
    fill(scratch_two, query_own, query_other, None, core, 1, start * 128, True)
    t, j = iotas(CHUNK, CHUNK)
    apart = t ^ j
    parts = [(head, chunk) for head in range(count) for chunk in range(2)]
    base = 8 * core + start
    run = sums(small_own, small_other, base, parts, core)
    rows = list(run)
    for head, chunk in parts:
        for level in range(near + 1):
            row = 32 + 16 * level + base + head
            rows.append(token_row(small_own, small_other, row, core, chunk))
    columns = rows_table(rows).T

    def held(one, two, head, chunk):
        if chunk:
            return two[start + head, 0], two[start + head, 1]
        return one[first + head, 0], one[first + head, 1]

    mixings = []
    queries = []
    for i, (head, chunk) in enumerate(parts):
        lanes = slice(head * 128, head * 128 + 128)
        taps_lanes = slice((start + head) * 128, (start + head) * 128 + 128)
        scratch = scratch_two if chunk else scratch_one
        query = unit(conv(scratch, query_taps, lanes, taps_lanes))
        queries.append(query)
        ratio = decay(columns[:, i : i + 1], run[i], t, j)
        scores = mm(split(query), held(key_cols_one, key_cols_two, head, chunk)) * ratio
        mixings.append(mm(split(scores), held(inverse_one, inverse_two, head, chunk)))
    for i, (head, chunk) in enumerate(parts):
        at = len(parts) + i * (near + 1)
        level_mat = columns[:, at : at + 1]
        for level in range(1, near):
            weight = columns[:, at + level : at + level + 1]
            level_mat = jnp.where(apart >= 1 << (level - 1), weight, level_mat)
        high, low = held(write_one, write_two, head, chunk)
        within = mm(split(mixings[i] * level_mat), (high[:, 128:], low[:, 128:]))
        grow = jnp.exp(columns[:, i : i + 1])
        effective = grow * queries[i] - mm(split(mixings[i]), (high[:, :128], low[:, :128]))
        rows = slice(chunk * CHUNK, chunk * CHUNK + CHUNK)
        if chunk:
            pair = split(effective)
            weight = columns[:, at + near : at + near + 1]
            within = within + weight * mm(pair, split(first_state[first + head]))
            effective = mm(pair, split(transit_one[first + head]))
        out[head, rows, :] = within
        moved[head, rows, :] = effective


def asked_kernel(group, heads, first, count, near, after, *refs):
    queries_kernel(group, heads, first, count, near, *refs)


def received(refs, head):
    code = None
    scale = None
    for ref in refs:
        tail = ref.shape[0] - 16 + head
        part = ref[head * 128 : head * 128 + 128, :].astype(F32)
        row = ref[tail : tail + 1, :].astype(F32)
        code = part if code is None else code + part
        scale = row if scale is None else scale + row
    return decode(code, scale)


def pack_rows(scales):
    zeros = jnp.zeros((16 - len(scales), 128), F32)
    return jnp.concatenate(scales + [zeros], axis=0).astype(BF16)


def encode_all(values, code_out):
    scales = []
    for head, value in enumerate(values):
        code, scale = encode(value)
        code_out[head * 128 : head * 128 + 128, :] = code
        scales.append(scale)
    head = len(values)
    code_out[head * 128 : head * 128 + 16, :] = pack_rows(scales)


def join_kernel(level, arrivals, with_transit, shift, waits, *refs):
    refs = refs[waits:]
    state_in = refs[:arrivals]
    refs = refs[arrivals:]
    transit_in = ()
    if with_transit:
        transit_in = refs[:arrivals]
        refs = refs[arrivals:]
    state, transit, code_out = refs[:3]
    refs = refs[3:]
    heads = state.shape[0]
    _, node = place()
    upper = (node >> level) % 2 == 1
    if not with_transit:
        late = (node >> (level + 1)) % 2 == 1
        riding = late & jnp.logical_not(upper)
        upper = upper & jnp.logical_not(late)

        @pl.when(riding)
        def _():
            encode_all([transit[head] for head in range(heads)], code_out)

    @pl.when(upper)
    def _():
        fresh = []
        for head in range(heads):
            pair = split(transit[head])
            fresh.append(mm(pair, split(received(state_in, head))) + state[head])
            if with_transit:
                refs[0][head] = fresh[head]
                refs[1][head] = mm(pair, split(received(transit_in, shift + head)))
        encode_all(fresh, code_out)
        if with_transit:
            encode_all([refs[1][head] for head in range(heads)], refs[2])

    if with_transit:

        @pl.when(jnp.logical_not(upper))
        def _():
            encode_all([state[head] for head in range(heads)], code_out)
            for head in range(heads):
                refs[0][head] = state[head]
                refs[1][head] = transit[head]
            encode_all([transit[head] for head in range(heads)], refs[2])


def code_kernel(*refs):
    values = [ref[head] for ref in refs[:-1] for head in range(ref.shape[0])]
    encode_all(values, refs[-1])


def level_weight(own, other, row, core):
    rows = [token_row(own, other, row, core, chunk) for chunk in range(2)]
    columns = rows_table(rows).T
    return jnp.concatenate([columns[:, 0:1], columns[:, 1:2]], axis=0)


def absorb_kernel(level, weight_row, group, heads, arrivals, passed, pieces, *refs):
    state_in = refs[:arrivals]
    transit_in = refs[arrivals : arrivals + passed]
    refs = refs[arrivals + passed :]
    small_own, small_other = refs[:2]
    outs_in = refs[2 : 2 + pieces]
    moved_in = refs[2 + pieces : 2 + 2 * pieces]
    out, moved = refs[2 + 2 * pieces :]
    core, node = place()
    upper = (node >> level) % 2 == 1
    each = heads // pieces
    behind = jnp.bool_(False)
    if passed:
        behind = ((node >> (level - 1)) % 2 == 1) & ((node >> level) > 0)

        @pl.when(behind)
        def _():
            shift = group * heads if level == 1 else 0
            for head in range(heads):
                pair = split(moved_in[head // each][head % each])
                moved[head] = mm(pair, split(received(transit_in, shift + head)))

    @pl.when(jnp.logical_not(behind))
    def _():
        for head in range(heads):
            moved[head] = moved_in[head // each][head % each]

    @pl.when(upper)
    def _():
        for head in range(heads):
            pair = split(moved[head])
            row = weight_row + 8 * core + heads * group + head
            weight = level_weight(small_own, small_other, row, core)
            gain = mm(pair, split(received(state_in, head)))
            out[head] = outs_in[head // each][head % each] + weight * gain

    @pl.when(jnp.logical_not(upper))
    def _():
        for head in range(heads):
            out[head] = outs_in[head // each][head % each]


def tail_kernel(level, weight_row, groups, heads, count, pending, near, arrivals, *refs):
    state_in = [refs[g * arrivals : (g + 1) * arrivals] for g in range(groups)]
    refs = refs[groups * arrivals :]
    query_refs, refs = refs[:7], refs[7:]
    uppers, refs = refs[:3], refs[3:]
    lowers = {}
    for group in sorted({group for group, _ in pending}):
        lowers[group], refs = refs[:5], refs[5:]
    pieces = heads // count
    outs_in = {}
    for group in range(groups):
        for piece in range(pieces):
            if (group, piece) not in pending:
                outs_in[group, piece], refs = refs[:2], refs[2:]
    outs, refs = refs[: 2 * groups], refs[2 * groups :]
    scratch, refs = refs[:2], refs[2:]
    for group, piece in pending:
        temporary, refs = refs[:2], refs[2:]
        made = lowers[group]
        queries_kernel(
            group,
            heads,
            piece * count,
            count,
            near,
            *query_refs,
            *made[:3],
            *uppers,
            *made[3:],
            *temporary,
            *scratch,
        )
        outs_in[group, piece] = temporary
    for group in range(groups):
        absorb_kernel(
            level,
            weight_row,
            group,
            heads,
            arrivals,
            0,
            pieces,
            *state_in[group],
            *query_refs[5:7],
            *[outs_in[group, piece][0] for piece in range(pieces)],
            *[outs_in[group, piece][1] for piece in range(pieces)],
            outs[2 * group],
            outs[2 * group + 1],
        )


def finish_kernel(level, weight_row, group, heads, arrivals, pieces, *refs):
    refs = refs[min(group, 1) :]
    state_in = refs[:arrivals]
    refs = refs[arrivals:]
    small_own, small_other, gate_own, gate_other, gain = refs[:5]
    outs_in = refs[5 : 5 + pieces]
    moved_in = refs[5 + pieces : 5 + 2 * pieces]
    stay, leave, total = refs[5 + 2 * pieces :]
    core, node = place()
    upper = (node >> level) % 2 == 1
    each = heads // pieces

    def add(states, transits):
        for head in range(heads):
            found = split(received(states, head))
            if transits is not None:
                found = split(mm(split(received(transits, head)), found))
            row = weight_row + 8 * core + heads * group + head
            weight = level_weight(small_own, small_other, row, core)
            extra = mm_three(split(moved_in[head // each][head % each]), found)
            total[head] = outs_in[head // each][head % each] + weight * extra

    if level:
        through = (node >> (level - 1)) % 2 == 1
        far, close = state_in[: arrivals // 2], state_in[arrivals // 2 :]

        @pl.when(upper & through)
        def _():
            add(far, close)

        @pl.when(upper & jnp.logical_not(through))
        def _():
            add(close, None)

    else:

        @pl.when(upper)
        def _():
            add(state_in, None)

    @pl.when(jnp.logical_not(upper))
    def _():
        for head in range(heads):
            total[head] = outs_in[head // each][head % each]

    lanes_all = heads * 128
    at = gate_other.shape[1] // 2 + group * lanes_all
    gates = (
        gate_own[:, group * lanes_all : (group + 1) * lanes_all],
        gate_other[:, at : at + lanes_all],
    )
    for head in range(heads):
        lanes = slice(head * 128, head * 128 + 128)
        for gate, chunk, target in ((gates[0], core, stay), (gates[1], 1 - core, leave)):
            rows = pl.ds(pl.multiple_of(chunk * CHUNK, CHUNK), CHUNK)
            attended = total[head, rows, :]
            scale = lax.rsqrt(jnp.mean(attended * attended, axis=-1, keepdims=True) + 1e-5)
            gated = attended * scale * gain[...] * silu(gate[:, lanes].astype(F32))
            target[:, lanes] = gated.astype(BF16)


def swap_kernel(*refs):
    out, sems = refs[-2:]
    count = (len(refs) - 2) // 2
    core, _ = place()
    half = out.shape[1] // 2
    width = half // count
    copies = []
    for i in range(count):
        for j, side in ((i, core), (count + i, 1 - core)):
            start = pl.multiple_of(side * half + i * width, width)
            made = pltpu.make_async_copy(refs[j], out.at[:, pl.ds(start, width)], sems.at[j])
            made.start()
            copies.append(made)
    for made in copies:
        made.wait()


def struct(shape, dtype=F32):
    return jax.ShapeDtypeStruct(shape, dtype)


def params(mib):
    return pltpu.CompilerParams(vmem_limit_bytes=mib << 20)


def cost(flops):
    return pl.CostEstimate(flops=flops, bytes_accessed=1_000_000, transcendentals=0)


GROUPS = 2
PIECES = 2


def per_device(
    query_rows,
    key_rows,
    value_rows,
    query_taps,
    key_taps,
    value_taps,
    log_alpha,
    write_strength,
    tier_mixture,
    output_gate,
    norm_gain,
):
    rows, width = query_rows.shape
    half = width // 2
    size = lax.axis_size("seq")
    nodes = size // 2
    level_total = tier_mixture.shape[0]
    near = CHUNK.bit_length()
    heads = 8 // GROUPS
    lanes = heads * 128
    shard_bits = nodes.bit_length() - 1
    cores = [(i, i ^ 1) for i in range(size)]
    small_rows = 16 * (2 + level_total)
    key_other = lax.ppermute(key_rows, "seq", cores)
    value_other = lax.ppermute(value_rows, "seq", cores)
    half_shape = struct((rows, half), BF16)
    taps_shape = struct((4, half))
    (
        query_half,
        key_half,
        value_half,
        gate_half,
        query_taps_half,
        key_taps_half,
        value_taps_half,
        halo,
        small,
        gain,
        message,
    ) = pl.pallas_call(
        prepare_kernel,
        in_specs=[pl.BlockSpec(memory_space=pltpu.HBM)] * 11,
        out_shape=[half_shape] * 4
        + [taps_shape] * 3
        + [struct((16, width), BF16), struct((small_rows, 128)), struct((1, 128))]
        + [struct((rows, width), BF16)],
        scratch_shapes=[pltpu.VMEM((3, 16, width), BF16), pltpu.SemaphoreType.DMA((16,))],
        compiler_params=params(8),
        name="prepare",
    )(
        *[
            pltpu.with_memory_space_constraint(x, pltpu.HBM)
            for x in (
                query_rows,
                key_rows,
                value_rows,
                output_gate,
                log_alpha,
                write_strength,
                tier_mixture.reshape(level_total * 16, rows),
                query_taps,
                key_taps,
                value_taps,
                norm_gain.reshape(1, 128),
            )
        ]
    )
    small_other = lax.ppermute(small, "seq", cores)
    halo_one = lax.ppermute(halo, "seq", [(i, i + 1) for i in range(1, size - 1, 2)])
    halo_two = lax.ppermute(halo, "seq", [(i, i + 2) for i in range(1, size - 1, 2)])

    def fan(value, level, riders=False):
        span = 1 << level
        results = []
        for offset in reversed(range(span)):
            route = []
            for low in range(0, nodes, 2 * span):
                hops = [(low + span - 1, low + span + offset)]
                if riders and 2 * offset < span:
                    middle = low + span + span // 2
                    hops.append((middle - 1, middle + offset))
                for source, target in hops:
                    route += [(2 * source + c, 2 * target + c) for c in range(2)]
            results.append(lax.ppermute(value, "seq", route))
        return results

    def held(count):
        return [
            struct((count, 2, 128, 128), BF16),
            struct((count, 2, 128, 128), BF16),
            struct((count, 2, 128, 256), BF16),
        ]

    square = (heads, 128, 128)
    code_shape = struct((heads * 128 + 16, 128), BF16)
    upper = pl.pallas_call(
        upper_kernel,
        out_shape=held(8) + [struct((8, 128, 128))] * 2,
        scratch_shapes=[pltpu.VMEM((8 + CHUNK, half), F32)] * 2,
        compiler_params=params(24),
        cost_estimate=cost(4_000_000_000),
        name="upper",
    )(
        key_half,
        key_other,
        value_half,
        value_other,
        key_taps_half,
        value_taps_half,
        small,
        small_other,
    )
    local = []
    arrived = []
    after = upper[4]
    for group in range(GROUPS):
        after, halo_first = lax.optimization_barrier((after, halo_one))
        made = pl.pallas_call(
            functools.partial(lower_kernel, group, heads),
            out_shape=held(heads)
            + [struct(square), struct(square), struct(square), struct(square), code_shape],
            scratch_shapes=[pltpu.VMEM((8 + CHUNK, lanes), F32)] * 2,
            compiler_params=params(24),
            cost_estimate=cost(2_500_000_000),
            name="lower",
        )(
            key_half,
            key_other,
            value_half,
            value_other,
            key_taps_half,
            value_taps_half,
            halo_first,
            halo_two,
            small,
            small_other,
            upper[3],
            upper[4],
        )
        local.append(made)
        after = made[7]
        arrived.append(fan(made[7], 0) if shard_bits else [])

    _, late_message = lax.optimization_barrier((local[0][7], message))
    query_other = gate_other = lax.ppermute(late_message, "seq", cores)
    state = [x[4] for x in local]
    transit = [x[6] for x in local]
    count = heads // PIECES
    outs = [[] for _ in range(GROUPS)]
    moved = [[] for _ in range(GROUPS)]
    pending = [(group, piece) for group in range(GROUPS) for piece in range(PIECES)]

    def ask(after):
        group, piece = pending.pop(0)
        made = local[group]
        shape = struct((count, 2 * CHUNK, 128))
        operands = [
            query_half,
            query_other,
            query_taps_half,
            halo_one,
            halo_two,
            small,
            small_other,
            *made[:3],
            *upper[:3],
            made[3],
            made[5],
        ]
        out, move = pl.pallas_call(
            functools.partial(asked_kernel, group, heads, piece * count, count, near),
            in_specs=[pl.BlockSpec(memory_space=pl.ANY)]
            + [pl.BlockSpec(memory_space=pltpu.VMEM)] * len(operands),
            out_shape=[shape, shape],
            scratch_shapes=[pltpu.VMEM((8 + CHUNK, count * 128), F32)] * 2,
            compiler_params=params(16),
            cost_estimate=cost(1_000_000),
            name="queries",
        )(after, *operands)
        outs[group].append(out)
        moved[group].append(move)
        return out

    moved_shape = struct((heads, 2 * CHUNK, 128))
    transit_codes = [None] * GROUPS

    def send_transit():
        return pl.pallas_call(
            code_kernel,
            out_shape=struct((8 * 128 + 16, 128), BF16),
            compiler_params=params(8),
            cost_estimate=cost(1_000_000),
            name="code",
        )(*transit)

    shifts = [heads * group for group in range(GROUPS)]
    passing = [[]] * GROUPS
    for level in range(shard_bits - 1):
        keeps = level < shard_bits - 2

        fanned = [[]] * GROUPS
        if keeps and level == 0:
            fanned = [fan(send_transit(), level)] * GROUPS
        elif keeps:
            fanned = [fan(x, level) for x in transit_codes]
        following = []
        for group in range(GROUPS):
            shapes = [code_shape]
            operands = list(arrived[group])
            if keeps:
                shapes += [struct(square), struct(square), code_shape]
                operands += fanned[group]
            if level == 0 and group == 1:
                after = ask(after)
            waits = [after]
            if level == 0 and group == GROUPS - 1:
                waits += [query_other]
            joined = pl.pallas_call(
                functools.partial(
                    join_kernel, level, len(arrived[group]), keeps, shifts[group], len(waits)
                ),
                in_specs=[pl.BlockSpec(memory_space=pl.ANY)] * len(waits)
                + [pl.BlockSpec(memory_space=pltpu.VMEM)] * (len(operands) + 2),
                out_shape=shapes,
                compiler_params=params(12),
                cost_estimate=cost(4_000_000_000),
                name="join",
            )(*waits, *operands, state[group], transit[group])
            after = joined[0]
            following.append(fan(joined[0], level + 1, not keeps))
            if keeps:
                state[group], transit[group], transit_codes[group] = joined[1:]
        arrivals = len(arrived[0])
        if level == 0:
            after, small_here = lax.optimization_barrier((after, small))
            operands = [x for group in range(GROUPS) for x in arrived[group]]
            operands += [query_half, query_other, query_taps_half, halo_one, halo_two]
            operands += [small_here, small_other, *upper[:3]]
            for group in sorted({group for group, _ in pending}):
                made = local[group]
                operands += [*made[:3], made[3], made[5]]
            for group in range(GROUPS):
                for out, move in zip(outs[group], moved[group]):
                    operands += [out, move]
            results = pl.pallas_call(
                functools.partial(
                    tail_kernel,
                    level,
                    32 + 16 * (near + 1 + level),
                    GROUPS,
                    heads,
                    count,
                    tuple(pending),
                    near,
                    arrivals,
                ),
                out_shape=[moved_shape] * (2 * GROUPS),
                scratch_shapes=[pltpu.VMEM((8 + CHUNK, count * 128), F32)] * 2
                + [pltpu.VMEM((count, 2 * CHUNK, 128), F32)] * (2 * len(pending)),
                compiler_params=params(24),
                cost_estimate=cost(1_000_000),
                name="tail",
            )(*operands)
            pending.clear()
            for group in range(GROUPS):
                outs[group], moved[group] = [results[2 * group]], [results[2 * group + 1]]
        else:
            for group in range(GROUPS):
                out, move = pl.pallas_call(
                    functools.partial(
                        absorb_kernel,
                        level,
                        32 + 16 * (near + 1 + level),
                        group,
                        heads,
                        arrivals,
                        len(passing[group]),
                        len(outs[group]),
                    ),
                    out_shape=[moved_shape, moved_shape],
                    compiler_params=params(12),
                    cost_estimate=cost(800_000_000),
                    name="absorb",
                )(
                    *arrived[group],
                    *passing[group],
                    small,
                    small_other,
                    *outs[group],
                    *moved[group],
                )
                outs[group], moved[group] = [out], [move]
        arrived = following
        passing = fanned
        shifts = [0] * GROUPS
    while pending:
        after = ask(after)

    level = max(shard_bits - 1, 0)
    stays = []
    comes = []
    for group in range(GROUPS):
        operands = [
            *arrived[group],
            small,
            small_other,
            gate_half,
            gate_other,
            gain,
            *outs[group],
            *moved[group],
        ]
        specs = [pl.BlockSpec(memory_space=pltpu.VMEM)] * len(operands)
        if group:
            operands = [stays[-1]] + operands
            specs = [pl.BlockSpec(memory_space=pl.ANY)] + specs
        stay, leave = pl.pallas_call(
            functools.partial(
                finish_kernel,
                level,
                32 + 16 * (near + 1 + level),
                group,
                heads,
                len(arrived[group]),
                len(outs[group]),
            ),
            in_specs=specs,
            out_shape=[struct((rows, lanes), BF16)] * 2,
            scratch_shapes=[pltpu.VMEM((heads, 2 * CHUNK, 128), F32)],
            compiler_params=params(12),
            cost_estimate=cost(1_000_000),
            name="finish",
        )(*operands)
        stays.append(stay)
        comes.append(lax.ppermute(leave, "seq", cores))
    return pl.pallas_call(
        swap_kernel,
        in_specs=[pl.BlockSpec(memory_space=pltpu.VMEM)] * (2 * GROUPS),
        out_specs=pl.BlockSpec(memory_space=pltpu.HBM),
        out_shape=struct((rows, width), BF16),
        scratch_shapes=[pltpu.SemaphoreType.DMA((2 * GROUPS,))],
        compiler_params=params(4),
        name="swap",
    )(*stays, *comes)


def solution(mesh):
    placed = (
        P(("req", "seq"), None),
        P(("req", "seq"), None),
        P(("req", "seq"), None),
        P(),
        P(),
        P(),
        P(None, ("req", "seq")),
        P(None, ("req", "seq")),
        P(None, None, ("req", "seq")),
        P(("req", "seq"), None),
        P(),
    )
    return jax.shard_map(
        per_device, mesh=mesh, in_specs=placed, out_specs=P(("req", "seq"), None), check_vma=False
    )
```
